256 devices in a mesh: rows: 16 (over z_hi, x), cent: 16 (over z_lo, y, core).
Axes of the slice: x: 4, y: 4, z: 8 (z_hi: 4, z_lo: 2; z = z_hi * 2 + z_lo), core: 2. Of those that a mesh axis runs over, the one named last changes fastest.
Arguments:
- emb_values: bfloat16 [32768, 1024], P(('cent', 'rows')), may hold values from -6 to 6
- emb_scales: bfloat16 [32768, 8], P(('cent', 'rows')), may hold values from 0.125 to 8, as said below
- coarse_ids: int32 [16, 2048], P(None, 'rows'), may hold values from 0 to 32767, as said below
- centroids: bfloat16 [32768, 1024], P('cent'), may hold values from -6 to 6
- codes_one: int32 [16, 32768], P('rows', 'cent'), may hold values from 0 to 255
- codes_two: int32 [16, 32768], P('rows', 'cent'), may hold values from 0 to 255
- codebook_init: float32 [16, 256, 64], P('rows'), may hold values from -6 to 6
Outputs:
- coarse_gap: float32 [32768], P(('cent', 'rows'))
- codebook_one: float32 [16, 256, 64], P('rows')
- codebook_two: float32 [16, 256, 64], P('rows')
- distortion: float32 [16, 32768], P('rows', 'cent')
The draws below stay inside these ranges and needn't reach their ends.
Inputs may be any that keep to these rules, and one draw needn't show every extreme that they name: `coarse_ids`: in each aligned block of 128 rows of the flattened ids (the rows of one device), at most 16 ids fall in any one aligned range of 2048 centroids, and exactly 16 fall in some range. `emb_scales`: every scale is a power of two.
All inputs are finite; a program needn't handle non-finite values.
Results may differ from the reference program's by a relative error of at most 0.0003.
Values may be sent and summed in bfloat16 or wider, within the bound.
No kernel may reach another device: no remote copies, remote signals or barrier semaphores. Data moves between devices by JAX's collectives and lax.ppermute only.
A program may use at most 64 MiB of HBM per device.

```python
import math
import jax
import jax.numpy as jnp
import numpy as np
from jax import lax

D = 1024
BLOCK = 128
M = 16
K = 256
CENT_DEV = 2048
ROWS_DEV = 128
ROWS = 32768
CENTROIDS = 32768
BLOCKS = 8
SUB = 64


def draw_emb_scales(key, part):
    low_power, high_power = (-2, 3)
    powers = jax.random.randint(jax.random.fold_in(key, 11), (ROWS, BLOCKS), low_power, high_power)
    return jnp.exp2(powers.astype(jnp.float32)).astype(jnp.bfloat16)


def draw_coarse_ids(key, part):
    groups = ROWS // ROWS_DEV
    owners = CENTROIDS // CENT_DEV
    limit = max(2, 2 * ROWS_DEV // owners)

    def one_group(group_key):
        key_heavy, key_slots, key_order, key_local = jax.random.split(group_key, 4)
        heavy = jax.random.randint(key_heavy, (), 0, owners).astype(jnp.int32)
        slots = jax.random.permutation(key_slots, (owners - 1) * limit)[:ROWS_DEV - limit].astype(jnp.int32)
        others = (heavy + 1 + slots // limit) % owners
        owner = jnp.concatenate([jnp.zeros((limit,), jnp.int32) + heavy, others])
        owner = jax.random.permutation(key_order, owner)
        local = jax.random.randint(key_local, (ROWS_DEV,), 0, CENT_DEV).astype(jnp.int32)
        return owner * CENT_DEV + local
    group_keys = jax.random.split(jax.random.fold_in(key, 7), groups)
    drawn = jax.vmap(one_group)(group_keys)
    return drawn.reshape(owners, groups // owners * ROWS_DEV).astype(jnp.int32)


def place_ends(values, rng, least, largest):
    longest = values.shape.index(max(values.shape))
    spots = []
    for shift in (0, 1):
        where = [jax.random.randint(jax.random.fold_in(rng, axis), (), 0, length) for axis, length in enumerate(values.shape)]
        where[longest] = (where[longest] + shift) % values.shape[longest]
        spots.append(tuple(where))
    return values.at[spots[0]].set(least).at[spots[1]].set(largest)


def block_levels(rng, extent, cuts, least, largest):
    def one(axis_at, shards_of):
        draws = jax.random.uniform(jax.random.fold_in(jax.random.fold_in(rng, 6), axis_at), (shards_of,), jnp.float32, least / len(cuts), largest / len(cuts))
        return jnp.repeat(jnp.exp(draws), extent[axis_at] // shards_of).reshape((-1,) + (1,) * (len(extent) - axis_at - 1))

    factor_of = one(*cuts[0])
    for cut in cuts[1:]:
        factor_of = factor_of * one(*cut)
    return factor_of


def rank_table(count, lean):
    loads = [(1 << 20) // math.isqrt(rank ** lean) + 1 for rank in range(1, count + 1)]
    deviation = 1 + sum(loads) // (1 << 30)
    return np.cumsum(np.array([max(1, weight // deviation) for weight in loads]))


def ranked_ids(key, extent, number_of, skew):
    listing = rank_table(number_of, skew)
    lot = jax.random.randint(jax.random.fold_in(key, 1), extent, 0, int(listing[number_of - 1]))
    rank = jnp.searchsorted(jnp.asarray(listing, jnp.int32), lot, side="right")
    return jax.random.permutation(jax.random.fold_in(key, 2), number_of)[rank].astype(jnp.int32)


def noise(stream_key, shape, scale, most, shards=(), held_as=jnp.bfloat16):
    entries = scale * jax.random.normal(stream_key, shape, jnp.float32)
    if shards:
        entries = entries * block_levels(stream_key, shape, shards, -0.22, 0.18)
    return jnp.clip(entries, -most, most).astype(held_as)


def setup_inputs(seed: int = 0) -> dict:
    streams_of = jax.random.split(jax.random.key(seed), 8)
    return {
        "emb_values": noise(streams_of[0], (ROWS, D), 1.0, 6.0, ((0, 256),)),
        "emb_scales": draw_emb_scales(jax.random.fold_in(streams_of[7], 71), 0),
        "coarse_ids": draw_coarse_ids(jax.random.fold_in(streams_of[7], 71), 0),
        "centroids": noise(streams_of[3], (CENTROIDS, D), 1.0, 6.0, ((0, 16),)),
        "codes_one": place_ends(ranked_ids(streams_of[4], (M, ROWS), K, 2), jax.random.fold_in(streams_of[4], 3), 0, K - 1).astype(jnp.int32),
        "codes_two": place_ends(ranked_ids(streams_of[5], (M, ROWS), K, 2), jax.random.fold_in(streams_of[5], 3), 0, K - 1).astype(jnp.int32),
        "codebook_init": noise(streams_of[6], (M, K, SUB), 1.0, 6.0, ((0, 16),), jnp.float32),
    }


prior_weight = 8.0


def reference(emb_values, emb_scales, coarse_ids, centroids, codes_one, codes_two, codebook_init):
    dequantized = emb_values.astype(jnp.float32) * jnp.repeat(emb_scales.astype(jnp.float32), BLOCK, axis=1)
    quantized = dequantized.astype(jnp.bfloat16)
    cent_squares = jnp.sum(jnp.square(centroids.astype(jnp.float32)), axis=1)
    block_rows = min(512, ROWS)

    def nearest_block(row_batch):
        row_squares = jnp.sum(jnp.square(row_batch.astype(jnp.float32)), axis=1)
        cross_terms = lax.dot_general(row_batch, centroids, (((1,), (1,)), ((), ())), preferred_element_type=jnp.float32)
        distances = row_squares[:, None] - 2.0 * cross_terms + cent_squares[None, :]
        return jnp.min(distances, axis=1)

    group_best = lax.map(nearest_block, quantized.reshape(ROWS // block_rows, block_rows, D)).reshape(ROWS)
    coarse_gap = group_best / D
    flat_ids = coarse_ids.reshape(ROWS).astype(jnp.int32)
    fetched = jnp.take(centroids, flat_ids, axis=0).astype(jnp.float32)
    residual = dequantized - fetched
    stacked = residual.T.reshape(M, SUB, ROWS)

    def per_space(space_items):
        space_rows, first_codes, second_codes, init_book = space_items
        codeword_ids = jnp.arange(K, dtype=jnp.int32)
        one_first = (first_codes[None, :] == codeword_ids[:, None]).astype(jnp.float32)
        totals_one = jnp.dot(one_first, space_rows.T, precision=lax.Precision.HIGHEST)
        counts_one = jnp.sum(one_first, axis=1)
        book_one = (totals_one + prior_weight * init_book) / (counts_one + prior_weight)[:, None]
        one_second = (second_codes[None, :] == codeword_ids[:, None]).astype(jnp.float32)
        totals_two = jnp.dot(one_second, space_rows.T, precision=lax.Precision.HIGHEST)
        counts_two = jnp.sum(one_second, axis=1)
        book_two = (totals_two + prior_weight * book_one) / (counts_two + prior_weight)[:, None]
        rebuilt = jnp.dot(book_two.T, one_second, precision=lax.Precision.HIGHEST)
        difference = space_rows - rebuilt
        return book_one, book_two, jnp.sum(difference * difference, axis=0) / SUB

    book_one, book_two, distortion = lax.map(per_space, (stacked, codes_one, codes_two, codebook_init))
    return coarse_gap, book_one, book_two, distortion
```

```python
import functools

import jax
import jax.numpy as jnp
from jax import lax
from jax.experimental import pallas as pl
from jax.experimental.pallas import tpu as pltpu
from jax.sharding import PartitionSpec as P


bf16 = jnp.bfloat16
f32 = jnp.float32
prior_weight = 8.0
VM = pl.BlockSpec(memory_space=pltpu.VMEM)
LIMIT = pltpu.CompilerParams(vmem_limit_bytes=16 << 20)


def on_chip(x):
    return pltpu.with_memory_space_constraint(x, pltpu.VMEM)


STATS = 136
PAY = 144


def quantize_kernel(values_ref, scales_t_ref, q_ref, squares_ref):
    scales = scales_t_ref[...].astype(f32).T
    squares = None
    for b in range(scales.shape[1]):
        lanes = slice(128 * b, 128 * b + 128)
        q = (values_ref[:, lanes].astype(f32) * scales[:, b : b + 1]).astype(bf16)
        q_ref[:, lanes] = q
        wide = q.astype(f32)
        squares = wide * wide if squares is None else squares + wide * wide
    squares_ref[...] = jnp.sum(squares.T, axis=0, keepdims=True)


def quantize(values, scales):
    rows, width = values.shape
    return pl.pallas_call(
        quantize_kernel,
        out_shape=(
            pltpu.VMEM((rows, width), bf16),
            pltpu.VMEM((1, rows), f32),
        ),
        in_specs=[VM, VM],
        out_specs=(VM, VM),
        cost_estimate=pl.CostEstimate(flops=rows * width * 3, bytes_accessed=rows * width * 4, transcendentals=0),
        compiler_params=LIMIT,
        name="quantize",
    )(values, scales.T)


def gather_kernel(slots, ids_ref, cents_ref, out_ref, onehot_ref):
    count = cents_ref.shape[0]
    groups, rows = ids_ref.shape

    local = ids_ref[...] - lax.axis_index("cent") * count
    mine = (local >= 0) & (local < count)
    before = lax.broadcasted_iota(jnp.int32, (rows, rows), 0) <= lax.broadcasted_iota(
        jnp.int32, (rows, rows), 1
    )
    rank = jnp.dot(
        mine.astype(f32).astype(bf16), before.astype(f32).astype(bf16), preferred_element_type=f32
    )
    slot = jnp.where(mine, rank - 1.0, -1.0)
    local = local.astype(f32)
    spread_slot = jnp.concatenate(
        [jnp.broadcast_to(slot[g : g + 1], (slots, rows)) for g in range(groups)], axis=0
    )
    spread_local = jnp.concatenate(
        [jnp.broadcast_to(local[g : g + 1], (slots, rows)) for g in range(groups)], axis=0
    )
    number = lax.rem(lax.broadcasted_iota(jnp.int32, (groups * slots, rows), 0), slots).astype(f32)
    chosen = jnp.sum(jnp.where(spread_slot == number, spread_local + 1.0, 0.0), axis=1, keepdims=True)
    chosen = chosen.astype(jnp.int32) - 1
    for j in range(count // 256):
        at = lax.broadcasted_iota(jnp.int32, (groups * slots, 256), 1) + 256 * j
        onehot_ref[:, 256 * j : 256 * j + 256] = (at == chosen).astype(f32).astype(bf16)
    for j in range(cents_ref.shape[1] // 256):
        lanes = slice(256 * j, 256 * j + 256)
        out_ref[:, lanes] = jnp.dot(
            onehot_ref[...], cents_ref[:, lanes], preferred_element_type=f32
        ).astype(bf16)


def gather(ids, cents, slots):
    groups, rows = ids.shape
    count, width = cents.shape
    return pl.pallas_call(
        functools.partial(gather_kernel, slots),
        out_shape=pltpu.VMEM((groups * slots, width), bf16),
        in_specs=[VM, VM],
        out_specs=VM,
        scratch_shapes=[pltpu.VMEM((groups * slots, count), bf16)],
        cost_estimate=pl.CostEstimate(
            flops=2 * groups * slots * count * width, bytes_accessed=count * width * 2, transcendentals=0
        ),
        compiler_params=LIMIT,
        name="gather",
    )(ids, on_chip(cents))


def residual_kernel(count, slots, ids_ref, fetched_ref, q_ref, out_ref):
    rows, width = q_ref.shape
    ids = ids_ref[pl.ds(lax.axis_index("cent"), 1), :]
    owner = lax.div(ids, count)
    across = jnp.broadcast_to(owner, (rows, rows))
    down = across.astype(f32).T.astype(jnp.int32)
    earlier = lax.broadcasted_iota(jnp.int32, (rows, rows), 0) < lax.broadcasted_iota(
        jnp.int32, (rows, rows), 1
    )
    rank = jnp.sum(jnp.where((across == down) & earlier, 1.0, 0.0), axis=0, keepdims=True)
    slot = owner * slots + rank.astype(jnp.int32)
    number = lax.broadcasted_iota(jnp.int32, (fetched_ref.shape[0], rows), 0)
    place = (number == slot).astype(f32).astype(bf16)
    for j in range(width // 128):
        lanes = slice(128 * j, 128 * j + 128)
        fetched = lax.dot_general(
            place, fetched_ref[:, lanes], (((0,), (0,)), ((), ())), preferred_element_type=f32
        )
        out_ref[lanes, :] = (q_ref[:, lanes].astype(f32) - fetched).T


def residuals(ids, fetched, q, count, slots):
    rows, width = q.shape
    return pl.pallas_call(
        functools.partial(residual_kernel, count, slots),
        out_shape=pltpu.VMEM((width, rows), f32),
        in_specs=[VM] * 3,
        out_specs=VM,
        cost_estimate=pl.CostEstimate(
            flops=2 * fetched.size * rows, bytes_accessed=fetched.size * 2 + q.size * 6, transcendentals=0
        ),
        compiler_params=LIMIT,
        name="residuals",
    )(ids, on_chip(fetched), on_chip(q))


def nearest_kernel(blocks, first, *refs):
    x_refs, refs = refs[:blocks], refs[blocks:]
    cents_ref, squares_ref, out_ref = refs if not first else (refs[0], refs[2], refs[1])
    step = 256
    groups = [[]]
    for ref in x_refs:
        if sum(r.shape[0] for r in groups[-1]) == 256:
            groups.append([])
        groups[-1].append(ref)
    out_ref[...] = jnp.full(out_ref.shape, jnp.inf, f32)

    @pl.loop(0, cents_ref.shape[0] // step)
    def _(i):
        at = pl.ds(pl.multiple_of(i * step, step), step)
        block = cents_ref[at, :]
        if first:
            total = None
            for b in range(block.shape[1] // 128):
                wide = block[:, 128 * b : 128 * b + 128].astype(f32)
                total = wide * wide if total is None else total + wide * wide
            squares = jnp.broadcast_to(jnp.sum(total, axis=1, keepdims=True), (step, 128))
            squares_ref[at, :] = squares
        else:
            squares = squares_ref[at, :]
        squares = jnp.concatenate([squares, squares], axis=1)
        for j, group in enumerate(groups):
            x = jnp.concatenate([r[...] for r in group], axis=0)
            cross = lax.dot_general(block, x, (((1,), (1,)), ((), ())), preferred_element_type=f32)
            low = jnp.min(squares - 2.0 * cross, axis=0, keepdims=True)
            for k in range(2):
                row = slice(2 * j + k, 2 * j + k + 1)
                out_ref[row, :] = jnp.minimum(out_ref[row, :], low[:, 128 * k : 128 * k + 128])


def nearest(xs, cents, squares=None):
    count, width = cents.shape
    first = squares is None
    rows = sum(x.shape[0] for x in xs)
    out_shape = pltpu.VMEM((rows // 128, 128), f32)
    return pl.pallas_call(
        functools.partial(nearest_kernel, len(xs), first),
        out_shape=(out_shape, pltpu.VMEM((count, 128), f32)) if first else out_shape,
        in_specs=[VM] * (len(xs) + (1 if first else 2)),
        out_specs=(VM, VM) if first else VM,
        cost_estimate=pl.CostEstimate(
            flops=2 * rows * count * width, bytes_accessed=count * width * 2 + rows * width * 2, transcendentals=0
        ),
        compiler_params=LIMIT,
        name="nearest",
    )(*[on_chip(x) for x in xs], on_chip(cents), *([] if first else [on_chip(squares)]))


def halves_of(x):
    high = x.astype(bf16)
    return high, (x - high.astype(f32)).astype(bf16)


def statistics_kernel(where, sub_ref, one_ref, two_ref, *refs):
    gap_refs, (mine_ref, theirs_ref) = refs[:-2], refs[-2:]
    groups, width, rows = sub_ref.shape
    words = 256
    high, low = [], []
    for g in range(groups):
        h, l = halves_of(sub_ref[g])
        high.append(h)
        low.append(l)
    ones = jnp.ones((16, groups * rows), bf16)
    left = jnp.concatenate([jnp.concatenate(high, axis=1), jnp.concatenate(low, axis=1), ones], axis=0)
    word = lax.broadcasted_iota(jnp.int32, (words, groups * rows), 0)
    core = lax.rem(lax.axis_index("cent"), 2)
    odd = core == 1

    def totals(codes_ref):
        hit = (word == codes_ref[...]).astype(f32).astype(bf16)
        out = lax.dot_general(left, hit, (((1,), (1,)), ((), ())), preferred_element_type=f32)
        return out[:width] + out[width : 2 * width], out[2 * width : 2 * width + 8]

    for at, codes_ref in enumerate((one_ref, two_ref)):
        total, count = totals(codes_ref)
        rows_at = slice(width * at, width * at + width)
        a, b = total[:, :128], total[:, 128:]
        mine_ref[rows_at, :] = jnp.where(odd, b, a)
        theirs_ref[rows_at, :] = jnp.where(odd, a, b)
        a, b = count[:4, :128], count[:4, 128:]
        count_at = slice(2 * width + 4 * at, 2 * width + 4 * at + 4)
        mine_ref[count_at, :] = jnp.where(odd, b, a)
        theirs_ref[count_at, :] = jnp.where(odd, a, b)
    for j in range(8):
        for out_ref, d in ((mine_ref, 2 * j), (theirs_ref, 2 * j + 1)):
            k, row = where[d]
            out_ref[STATS + j : STATS + j + 1, :] = gap_refs[k][row : row + 1, :]


def statistics(sub, codes_one, codes_two, lows, where):
    shape = pltpu.VMEM((PAY, 128), f32)
    return pl.pallas_call(
        functools.partial(statistics_kernel, where),
        out_shape=(shape, shape),
        in_specs=[VM] * (3 + len(lows)),
        out_specs=(VM, VM),
        cost_estimate=pl.CostEstimate(
            flops=2 * 2 * sub.size * 512, bytes_accessed=sub.size * 4, transcendentals=0
        ),
        compiler_params=LIMIT,
        name="statistics",
    )(on_chip(sub), codes_one, codes_two, *[on_chip(x) for x in lows])


def join_kernel(shift, a_ref, b_ref, out_ref):
    out_ref[:STATS, :] = a_ref[:STATS, :] + b_ref[:STATS, :]
    keep = PAY - STATS - shift
    out_ref[STATS:PAY, :] = a_ref[STATS:PAY, :]
    out_ref[STATS : STATS + keep, :] = jnp.minimum(
        a_ref[STATS : STATS + keep, :], b_ref[STATS + shift : PAY, :]
    )


def join(a, b, shift):
    return pl.pallas_call(
        functools.partial(join_kernel, shift),
        out_shape=pltpu.VMEM(a.shape, f32),
        in_specs=[VM, VM],
        out_specs=VM,
        cost_estimate=pl.CostEstimate(flops=a.size, bytes_accessed=a.size * 12, transcendentals=0),
        compiler_params=LIMIT,
        name="join",
    )(on_chip(a), on_chip(b))


def update_kernel(width, a_ref, b_ref, c_ref, d_ref, init_ref, squares_ref, books_ref, gap_ref):
    core = lax.rem(lax.axis_index("cent"), 2)
    total = (a_ref[:STATS, :] + b_ref[:STATS, :]) + (c_ref[:STATS, :] + d_ref[:STATS, :])
    init = jnp.where(core == 1, init_ref[:, 128:], init_ref[:, :128])
    count_one = total[2 * width : 2 * width + 1]
    count_two = total[2 * width + 4 : 2 * width + 5]
    one = (total[:width] + prior_weight * init) / (count_one + prior_weight)
    two = (total[width : 2 * width] + prior_weight * one) / (count_two + prior_weight)
    books_ref[:width, :] = one
    books_ref[width:, :] = two
    low = jnp.minimum(
        jnp.minimum(a_ref[STATS : STATS + 1, :], b_ref[STATS + 1 : STATS + 2, :]),
        jnp.minimum(c_ref[STATS + 2 : STATS + 3, :], d_ref[STATS + 3 : STATS + 4, :]),
    )
    gap_ref[...] = (low + squares_ref[...]) * (1.0 / 1024.0)


def update(parts, init, squares):
    width = init.shape[0]
    return pl.pallas_call(
        functools.partial(update_kernel, width),
        out_shape=(
            pltpu.VMEM((2 * width, 128), f32),
            jax.ShapeDtypeStruct((1, 128), f32),
        ),
        in_specs=[VM] * 6,
        out_specs=(VM, VM),
        cost_estimate=pl.CostEstimate(flops=8 * STATS * 128, bytes_accessed=5 * PAY * 512, transcendentals=0),
        compiler_params=LIMIT,
        name="update",
    )(*[on_chip(x) for x in parts], init, on_chip(squares))


def distortion_kernel(sub_ref, two_ref, mine_ref, theirs_ref, one_out_ref, two_out_ref, out_ref):
    groups, width, rows = sub_ref.shape
    odd = lax.rem(lax.axis_index("cent"), 2) == 1
    mine, theirs = mine_ref[...], theirs_ref[...]
    books = jnp.concatenate([jnp.where(odd, theirs, mine), jnp.where(odd, mine, theirs)], axis=1)
    one_out_ref[...] = books[:width]
    book = books[width:]
    two_out_ref[...] = book
    high, low = halves_of(book)
    left = jnp.concatenate([high, low], axis=0)
    words = book.shape[1]
    for g in range(0, groups, 2):
        lanes = slice(rows * g, rows * g + 2 * rows)
        word = lax.broadcasted_iota(jnp.int32, (words, 2 * rows), 0)
        hit = (word == two_ref[:, lanes]).astype(f32).astype(bf16)
        rebuilt = jnp.dot(left, hit, preferred_element_type=f32)
        rebuilt = rebuilt[:width] + rebuilt[width:]
        sub = jnp.concatenate([sub_ref[g], sub_ref[g + 1]], axis=1)
        miss = sub - rebuilt
        out_ref[:, lanes] = jnp.sum(miss * miss, axis=0, keepdims=True) * (1.0 / width)


def distortions(sub, codes_two, mine, theirs):
    groups, width, rows = sub.shape
    return pl.pallas_call(
        distortion_kernel,
        out_shape=(
            jax.ShapeDtypeStruct((width, 256), f32),
            jax.ShapeDtypeStruct((width, 256), f32),
            jax.ShapeDtypeStruct((1, groups * rows), f32),
        ),
        in_specs=[VM] * 4,
        out_specs=(VM, VM, VM),
        cost_estimate=pl.CostEstimate(
            flops=4 * sub.size * 256, bytes_accessed=sub.size * 4, transcendentals=0
        ),
        compiler_params=LIMIT,
        name="distortion",
    )(on_chip(sub), codes_two, on_chip(mine), on_chip(theirs))


def swap(x, offset):
    return lax.ppermute(x, "cent", [(i, i ^ offset) for i in range(16)])


def on_device(emb_values, emb_scales, coarse_ids, centroids, codes_one, codes_two, codebook_init):
    own_rows, width = emb_values.shape
    count = centroids.shape[0]
    sub_width = codebook_init.shape[2]
    peers = coarse_ids.shape[0]
    slots = 16
    half = own_rows // 2

    q, row_squares = quantize(emb_values, emb_scales)
    sent = gather(coarse_ids, centroids, slots).reshape(peers, slots, width)
    fetched = lax.all_to_all(sent, "cent", 0, 0).reshape(peers * slots, width)

    core = 1
    blocks = {0: [q], core: [swap(q, core)]}
    a, b, z = swap(q, 2), swap(q, 6), swap(q, 8)
    blocks[2], blocks[6], blocks[8] = [a], [b], [z]
    blocks[4] = [swap(b[:half], 2), swap(a[half:], 6)]
    blocks[10], blocks[14] = [swap(z, 2)], [swap(z, 6)]
    blocks[12] = [swap(x, 8) for x in blocks[4]]
    for d in (2, 6, 8, 4, 10, 14, 12):
        blocks[d ^ core] = [swap(x, core) for x in blocks[d]]

    def near(order, squares=None):
        xs = [x for d in order for x in blocks[d]]
        return nearest(xs, centroids, squares)

    orders = ((0, 1, 2, 3), (6, 7, 8, 9), (4, 5, 10, 11, 14, 15, 12, 13))
    first, cent_squares = near(orders[0])
    lows = [first] + [near(order, cent_squares) for order in orders[1:]]
    where = {d: (k, j) for k, order in enumerate(orders) for j, d in enumerate(order)}
    residual = residuals(coarse_ids, fetched, q, count, slots)
    stacked = residual.reshape(width // sub_width, sub_width, own_rows)
    sub = lax.all_to_all(stacked, "rows", 0, 0)

    mine, theirs = statistics(sub, codes_one, codes_two, lows, where)
    mine = join(mine, swap(theirs, 1), 0)
    mine = join(mine, swap(mine, 8), 4)
    parts = [mine] + [swap(mine, d) for d in (2, 4, 6)]
    init = codebook_init[0].T
    books, coarse_gap = update(parts, init, row_squares)
    book_one, book_two, distortion = distortions(sub, codes_two, books, swap(books, 1))
    return coarse_gap[0], book_one.T[None], book_two.T[None], distortion


def solution(mesh):
    placed = (
        P(("cent", "rows"), None),
        P(("cent", "rows"), None),
        P(None, "rows"),
        P("cent", None),
        P("rows", "cent"),
        P("rows", "cent"),
        P("rows", None, None),
    )
    return jax.shard_map(
        on_device,
        mesh=mesh,
        in_specs=placed,
        out_specs=(
            P(("cent", "rows")),
            P("rows", None, None),
            P("rows", None, None),
            P("rows", "cent"),
        ),
        check_vma=False,
    )
```

```python
import functools

import jax
import jax.numpy as jnp
from jax import lax
from jax.experimental import pallas as pl
from jax.experimental.pallas import tpu as pltpu
from jax.sharding import PartitionSpec as P


bf16 = jnp.bfloat16
f32 = jnp.float32
prior_weight = 8.0
VM = pl.BlockSpec(memory_space=pltpu.VMEM)
LIMIT = pltpu.CompilerParams(vmem_limit_bytes=16 << 20)


def on_chip(x):
    return pltpu.with_memory_space_constraint(x, pltpu.VMEM)


STATS = 136
PAY = 144


def quantize_kernel(values_ref, scales_t_ref, q_ref, squares_ref):
    scales = scales_t_ref[...].astype(f32).T
    squares = None
    for b in range(scales.shape[1]):
        lanes = slice(128 * b, 128 * b + 128)
        q = (values_ref[:, lanes].astype(f32) * scales[:, b : b + 1]).astype(bf16)
        q_ref[:, lanes] = q
        wide = q.astype(f32)
        squares = wide * wide if squares is None else squares + wide * wide
    squares_ref[...] = jnp.sum(squares.T, axis=0, keepdims=True)


def quantize(values, scales):
    rows, width = values.shape
    return pl.pallas_call(
        quantize_kernel,
        out_shape=(
            pltpu.VMEM((rows, width), bf16),
            pltpu.VMEM((1, rows), f32),
        ),
        in_specs=[VM, VM],
        out_specs=(VM, VM),
        cost_estimate=pl.CostEstimate(flops=rows * width * 3, bytes_accessed=rows * width * 4, transcendentals=0),
        compiler_params=LIMIT,
        name="quantize",
    )(values, scales.T)


def gather_kernel(slots, ids_ref, cents_ref, out_ref, onehot_ref):
    count = cents_ref.shape[0]
    groups, rows = ids_ref.shape

    local = ids_ref[...] - lax.axis_index("cent") * count
    mine = (local >= 0) & (local < count)
    before = lax.broadcasted_iota(jnp.int32, (rows, rows), 0) <= lax.broadcasted_iota(
        jnp.int32, (rows, rows), 1
    )
    rank = jnp.dot(
        mine.astype(f32).astype(bf16), before.astype(f32).astype(bf16), preferred_element_type=f32
    )
    slot = jnp.where(mine, rank - 1.0, -1.0)
    local = local.astype(f32)
    spread_slot = jnp.concatenate(
        [jnp.broadcast_to(slot[g : g + 1], (slots, rows)) for g in range(groups)], axis=0
    )
    spread_local = jnp.concatenate(
        [jnp.broadcast_to(local[g : g + 1], (slots, rows)) for g in range(groups)], axis=0
    )
    number = lax.rem(lax.broadcasted_iota(jnp.int32, (groups * slots, rows), 0), slots).astype(f32)
    chosen = jnp.sum(jnp.where(spread_slot == number, spread_local + 1.0, 0.0), axis=1, keepdims=True)
    chosen = chosen.astype(jnp.int32) - 1
    for j in range(count // 256):
        at = lax.broadcasted_iota(jnp.int32, (groups * slots, 256), 1) + 256 * j
        onehot_ref[:, 256 * j : 256 * j + 256] = (at == chosen).astype(f32).astype(bf16)
    for j in range(cents_ref.shape[1] // 256):
        lanes = slice(256 * j, 256 * j + 256)
        out_ref[:, lanes] = jnp.dot(
            onehot_ref[...], cents_ref[:, lanes], preferred_element_type=f32
        ).astype(bf16)


def gather(ids, cents, slots):
    groups, _ = ids.shape
    count, width = cents.shape
    return pl.pallas_call(
        functools.partial(gather_kernel, slots),
        out_shape=pltpu.VMEM((groups * slots, width), bf16),
        in_specs=[VM, VM],
        out_specs=VM,
        scratch_shapes=[pltpu.VMEM((groups * slots, count), bf16)],
        cost_estimate=pl.CostEstimate(
            flops=2 * groups * slots * count * width, bytes_accessed=count * width * 2, transcendentals=0
        ),
        compiler_params=LIMIT,
        name="gather",
    )(ids, on_chip(cents))


def residual_kernel(count, slots, ids_ref, fetched_ref, q_ref, out_ref):
    rows, width = q_ref.shape
    ids = ids_ref[pl.ds(lax.axis_index("cent"), 1), :]
    owner = lax.div(ids, count)
    across = jnp.broadcast_to(owner, (rows, rows))
    down = across.astype(f32).T.astype(jnp.int32)
    earlier = lax.broadcasted_iota(jnp.int32, (rows, rows), 0) < lax.broadcasted_iota(
        jnp.int32, (rows, rows), 1
    )
    rank = jnp.sum(jnp.where((across == down) & earlier, 1.0, 0.0), axis=0, keepdims=True)
    slot = owner * slots + rank.astype(jnp.int32)
    number = lax.broadcasted_iota(jnp.int32, (fetched_ref.shape[0], rows), 0)
    place = (number == slot).astype(f32).astype(bf16)
    for j in range(width // 128):
        lanes = slice(128 * j, 128 * j + 128)
        fetched = lax.dot_general(
            place, fetched_ref[:, lanes], (((0,), (0,)), ((), ())), preferred_element_type=f32
        )
        out_ref[lanes, :] = (q_ref[:, lanes].astype(f32) - fetched).T


def residuals(ids, fetched, q, count, slots):
    rows, width = q.shape
    return pl.pallas_call(
        functools.partial(residual_kernel, count, slots),
        out_shape=pltpu.VMEM((width, rows), f32),
        in_specs=[VM] * 3,
        out_specs=VM,
        cost_estimate=pl.CostEstimate(
            flops=2 * fetched.size * rows, bytes_accessed=fetched.size * 2 + q.size * 6, transcendentals=0
        ),
        compiler_params=LIMIT,
        name="residuals",
    )(ids, on_chip(fetched), on_chip(q))


def nearest_kernel(blocks, first, *refs):
    x_refs, refs = refs[:blocks], refs[blocks:]
    cents_ref, squares_ref, out_ref = refs if not first else (refs[0], refs[2], refs[1])
    step = 256
    groups = [[]]
    for ref in x_refs:
        if sum(r.shape[0] for r in groups[-1]) == 256:
            groups.append([])
        groups[-1].append(ref)
    out_ref[...] = jnp.full(out_ref.shape, jnp.inf, f32)

    @pl.loop(0, cents_ref.shape[0] // step)
    def _(i):
        at = pl.ds(pl.multiple_of(i * step, step), step)
        block = cents_ref[at, :]
        if first:
            total = None
            for b in range(block.shape[1] // 128):
                wide = block[:, 128 * b : 128 * b + 128].astype(f32)
                total = wide * wide if total is None else total + wide * wide
            squares = jnp.broadcast_to(jnp.sum(total, axis=1, keepdims=True), (step, 128))
            squares_ref[at, :] = squares
        else:
            squares = squares_ref[at, :]
        squares = jnp.concatenate([squares, squares], axis=1)
        for j, group in enumerate(groups):
            x = jnp.concatenate([r[...] for r in group], axis=0)
            cross = lax.dot_general(block, x, (((1,), (1,)), ((), ())), preferred_element_type=f32)
            low = jnp.min(squares - 2.0 * cross, axis=0, keepdims=True)
            for k in range(2):
                row = slice(2 * j + k, 2 * j + k + 1)
                out_ref[row, :] = jnp.minimum(out_ref[row, :], low[:, 128 * k : 128 * k + 128])


def nearest(xs, cents, squares=None):
    count, width = cents.shape
    first = squares is None
    rows = sum(x.shape[0] for x in xs)
    out_shape = pltpu.VMEM((rows // 128, 128), f32)
    return pl.pallas_call(
        functools.partial(nearest_kernel, len(xs), first),
        out_shape=(out_shape, pltpu.VMEM((count, 128), f32)) if first else out_shape,
        in_specs=[VM] * (len(xs) + (1 if first else 2)),
        out_specs=(VM, VM) if first else VM,
        cost_estimate=pl.CostEstimate(
            flops=2 * rows * count * width, bytes_accessed=count * width * 2 + rows * width * 2, transcendentals=0
        ),
        compiler_params=LIMIT,
        name="nearest",
    )(*[on_chip(x) for x in xs], on_chip(cents), *([] if first else [on_chip(squares)]))


def halves_of(x):
    high = x.astype(bf16)
    return high, (x - high.astype(f32)).astype(bf16)


def statistics_kernel(where, sub_ref, one_ref, two_ref, *refs):
    gap_refs, (mine_ref, theirs_ref) = refs[:-2], refs[-2:]
    groups, width, rows = sub_ref.shape
    words = 256
    high, low = [], []
    for g in range(groups):
        h, l = halves_of(sub_ref[g])
        high.append(h)
        low.append(l)
    ones = jnp.ones((16, groups * rows), bf16)
    left = jnp.concatenate([jnp.concatenate(high, axis=1), jnp.concatenate(low, axis=1), ones], axis=0)
    word = lax.broadcasted_iota(jnp.int32, (words, groups * rows), 0)
    core = lax.rem(lax.axis_index("cent"), 2)
    odd = core == 1

    def totals(codes_ref):
        hit = (word == codes_ref[...]).astype(f32).astype(bf16)
        out = lax.dot_general(left, hit, (((1,), (1,)), ((), ())), preferred_element_type=f32)
        return out[:width] + out[width : 2 * width], out[2 * width : 2 * width + 8]

    for at, codes_ref in enumerate((one_ref, two_ref)):
        total, count = totals(codes_ref)
        rows_at = slice(width * at, width * at + width)
        a, b = total[:, :128], total[:, 128:]
        mine_ref[rows_at, :] = jnp.where(odd, b, a)
        theirs_ref[rows_at, :] = jnp.where(odd, a, b)
        a, b = count[:4, :128], count[:4, 128:]
        count_at = slice(2 * width + 4 * at, 2 * width + 4 * at + 4)
        mine_ref[count_at, :] = jnp.where(odd, b, a)
        theirs_ref[count_at, :] = jnp.where(odd, a, b)
    for j in range(8):
        for out_ref, d in ((mine_ref, 2 * j), (theirs_ref, 2 * j + 1)):
            k, row = where[d]
            out_ref[STATS + j : STATS + j + 1, :] = gap_refs[k][row : row + 1, :]


def statistics(sub, codes_one, codes_two, lows, where):
    shape = pltpu.VMEM((PAY, 128), f32)
    return pl.pallas_call(
        functools.partial(statistics_kernel, where),
        out_shape=(shape, shape),
        in_specs=[VM] * (3 + len(lows)),
        out_specs=(VM, VM),
        cost_estimate=pl.CostEstimate(
            flops=2 * 2 * sub.size * 512, bytes_accessed=sub.size * 4, transcendentals=0
        ),
        compiler_params=LIMIT,
        name="statistics",
    )(on_chip(sub), codes_one, codes_two, *[on_chip(x) for x in lows])


def join_kernel(shift, a_ref, b_ref, out_ref):
    out_ref[:STATS, :] = a_ref[:STATS, :] + b_ref[:STATS, :]
    keep = PAY - STATS - shift
    out_ref[STATS:PAY, :] = a_ref[STATS:PAY, :]
    out_ref[STATS : STATS + keep, :] = jnp.minimum(
        a_ref[STATS : STATS + keep, :], b_ref[STATS + shift : PAY, :]
    )


def join(a, b, shift):
    return pl.pallas_call(
        functools.partial(join_kernel, shift),
        out_shape=pltpu.VMEM(a.shape, f32),
        in_specs=[VM, VM],
        out_specs=VM,
        cost_estimate=pl.CostEstimate(flops=a.size, bytes_accessed=a.size * 12, transcendentals=0),
        compiler_params=LIMIT,
        name="join",
    )(on_chip(a), on_chip(b))


def update_kernel(width, a_ref, b_ref, c_ref, d_ref, init_ref, squares_ref, books_ref, gap_ref):
    core = lax.rem(lax.axis_index("cent"), 2)
    total = (a_ref[:STATS, :] + b_ref[:STATS, :]) + (c_ref[:STATS, :] + d_ref[:STATS, :])
    init = jnp.where(core == 1, init_ref[:, 128:], init_ref[:, :128])
    count_one = total[2 * width : 2 * width + 1]
    count_two = total[2 * width + 4 : 2 * width + 5]
    one = (total[:width] + prior_weight * init) / (count_one + prior_weight)
    two = (total[width : 2 * width] + prior_weight * one) / (count_two + prior_weight)
    books_ref[:width, :] = one
    books_ref[width:, :] = two
    low = jnp.minimum(
        jnp.minimum(a_ref[STATS : STATS + 1, :], b_ref[STATS + 1 : STATS + 2, :]),
        jnp.minimum(c_ref[STATS + 2 : STATS + 3, :], d_ref[STATS + 3 : STATS + 4, :]),
    )
    gap_ref[...] = (low + squares_ref[...]) * (1.0 / 1024.0)


def update(parts, init, squares):
    width = init.shape[0]
    return pl.pallas_call(
        functools.partial(update_kernel, width),
        out_shape=(
            pltpu.VMEM((2 * width, 128), f32),
            jax.ShapeDtypeStruct((1, 128), f32),
        ),
        in_specs=[VM] * 6,
        out_specs=(VM, VM),
        cost_estimate=pl.CostEstimate(flops=8 * STATS * 128, bytes_accessed=5 * PAY * 512, transcendentals=0),
        compiler_params=LIMIT,
        name="update",
    )(*[on_chip(x) for x in parts], init, on_chip(squares))


def distortion_kernel(sub_ref, two_ref, mine_ref, theirs_ref, one_out_ref, two_out_ref, out_ref):
    groups, width, rows = sub_ref.shape
    odd = lax.rem(lax.axis_index("cent"), 2) == 1
    mine, theirs = mine_ref[...], theirs_ref[...]
    books = jnp.concatenate([jnp.where(odd, theirs, mine), jnp.where(odd, mine, theirs)], axis=1)
    one_out_ref[...] = books[:width]
    book = books[width:]
    two_out_ref[...] = book
    high, low = halves_of(book)
    left = jnp.concatenate([high, low], axis=0)
    words = book.shape[1]
    for g in range(0, groups, 2):
        lanes = slice(rows * g, rows * g + 2 * rows)
        word = lax.broadcasted_iota(jnp.int32, (words, 2 * rows), 0)
        hit = (word == two_ref[:, lanes]).astype(f32).astype(bf16)
        rebuilt = jnp.dot(left, hit, preferred_element_type=f32)
        rebuilt = rebuilt[:width] + rebuilt[width:]
        sub = jnp.concatenate([sub_ref[g], sub_ref[g + 1]], axis=1)
        miss = sub - rebuilt
        out_ref[:, lanes] = jnp.sum(miss * miss, axis=0, keepdims=True) * (1.0 / width)


def distortions(sub, codes_two, mine, theirs):
    groups, width, rows = sub.shape
    return pl.pallas_call(
        distortion_kernel,
        out_shape=(
            jax.ShapeDtypeStruct((width, 256), f32),
            jax.ShapeDtypeStruct((width, 256), f32),
            jax.ShapeDtypeStruct((1, groups * rows), f32),
        ),
        in_specs=[VM] * 4,
        out_specs=(VM, VM, VM),
        cost_estimate=pl.CostEstimate(
            flops=4 * sub.size * 256, bytes_accessed=sub.size * 4, transcendentals=0
        ),
        compiler_params=LIMIT,
        name="distortion",
    )(on_chip(sub), codes_two, on_chip(mine), on_chip(theirs))


def swap(x, offset):
    return lax.ppermute(x, "cent", [(i, i ^ offset) for i in range(16)])


def step(emb_values, emb_scales, coarse_ids, centroids, codes_one, codes_two, codebook_init):
    own_rows, width = emb_values.shape
    count = centroids.shape[0]
    sub_width = codebook_init.shape[2]
    peers = coarse_ids.shape[0]
    slots = 16
    half = own_rows // 2

    centroids = on_chip(centroids)
    q, row_squares = quantize(emb_values, emb_scales)

    core = 1

    a, b, z = swap(q, 2), swap(q, 6), swap(q, 8)
    blocks = {0: [q], core: [swap(q, core)], 2: [a], 6: [b], 8: [z]}

    sent = gather(coarse_ids, centroids, slots).reshape(peers, slots, width)
    fetched = lax.all_to_all(sent, "cent", 0, 0).reshape(peers * slots, width)

    blocks[4] = [swap(b[:half], 2), swap(a[half:], 6)]
    blocks[10], blocks[14] = [swap(z, 2)], [swap(z, 6)]
    blocks[12] = [swap(x, 8) for x in blocks[4]]
    for d in (2, 6, 8, 4, 10, 14, 12):
        blocks[d ^ core] = [swap(x, core) for x in blocks[d]]

    def near(order, squares=None):
        xs = [x for d in order for x in blocks[d]]
        return nearest(xs, centroids, squares)

    orders = ((0, 1, 2, 3), (6, 7, 8, 9), (4, 5, 10, 11, 14, 15, 12, 13))
    first, cent_squares = near(orders[0])
    lows = [first] + [near(orders[k], cent_squares) for k in (1, 2)]
    where = {d: (k, j) for k, order in enumerate(orders) for j, d in enumerate(order)}

    residual = residuals(coarse_ids, fetched, q, count, slots)
    stacked = residual.reshape(width // sub_width, sub_width, own_rows)
    sub = lax.all_to_all(stacked, "rows", 0, 0)

    mine, theirs = statistics(sub, codes_one, codes_two, lows, where)
    mine = join(mine, swap(theirs, 1), 0)
    mine = join(mine, swap(mine, 8), 4)
    parts = [mine] + [swap(mine, d) for d in (2, 4, 6)]
    init = codebook_init[0].T
    books, coarse_gap = update(parts, init, row_squares)
    book_one, book_two, distortion = distortions(sub, codes_two, books, swap(books, 1))
    return coarse_gap[0], book_one.T[None], book_two.T[None], distortion


def solution(mesh):
    placed = (
        P(("cent", "rows"), None),
        P(("cent", "rows"), None),
        P(None, "rows"),
        P("cent", None),
        P("rows", "cent"),
        P("rows", "cent"),
        P("rows", None, None),
    )
    return jax.shard_map(
        step,
        mesh=mesh,
        in_specs=placed,
        out_specs=(
            P(("cent", "rows")),
            P("rows", None, None),
            P("rows", None, None),
            P("rows", "cent"),
        ),
        check_vma=False,
    )
```

```python
import functools

import jax
import jax.numpy as jnp
from jax import lax
from jax.experimental import pallas as pl
from jax.experimental.pallas import tpu as pltpu
from jax.sharding import PartitionSpec as P


bf16 = jnp.bfloat16
f32 = jnp.float32
prior_weight = 8.0
VM = pl.BlockSpec(memory_space=pltpu.VMEM)
HBM = pl.BlockSpec(memory_space=pltpu.HBM)
LIMIT = pltpu.CompilerParams(vmem_limit_bytes=16 << 20)


def off_chip(x):
    return pltpu.with_memory_space_constraint(x, pltpu.HBM)


def on_chip(x):
    return pltpu.with_memory_space_constraint(x, pltpu.VMEM)


STATS = 136
PAY = 144


def quantize_kernel(values_hbm, scales_hbm, top_ref, bottom_ref, squares_ref, values, scales_t, sems):
    copies = (
        pltpu.make_async_copy(values_hbm, values, sems.at[0]),
        pltpu.make_async_copy(scales_hbm, scales_t, sems.at[1]),
    )
    for copy in copies:
        copy.start()
    for copy in copies:
        copy.wait()
    half = top_ref.shape[0]
    scales = scales_t[...].astype(f32).T
    squares = None
    for b in range(scales.shape[1]):
        lanes = slice(128 * b, 128 * b + 128)
        q = (values[:, lanes].astype(f32) * scales[:, b : b + 1]).astype(bf16)
        top_ref[:, lanes] = q[:half]
        bottom_ref[:, lanes] = q[half:]
        wide = q.astype(f32)
        squares = wide * wide if squares is None else squares + wide * wide
    squares_ref[...] = jnp.sum(squares.T, axis=0, keepdims=True)


def quantize(values, scales):
    rows, width = values.shape
    scales = scales.T
    return pl.pallas_call(
        quantize_kernel,
        out_shape=(
            pltpu.VMEM((rows // 2, width), bf16),
            pltpu.VMEM((rows // 2, width), bf16),
            pltpu.VMEM((1, rows), f32),
        ),
        in_specs=[HBM, HBM],
        out_specs=(VM, VM, VM),
        scratch_shapes=[
            pltpu.VMEM(values.shape, bf16),
            pltpu.VMEM(scales.shape, bf16),
            pltpu.SemaphoreType.DMA((2,)),
        ],
        cost_estimate=pl.CostEstimate(flops=rows * width * 3, bytes_accessed=rows * width * 4, transcendentals=0),
        compiler_params=LIMIT,
        name="quantize",
    )(off_chip(values), off_chip(scales))


def gather_kernel(slots, step, ids_hbm, cents_hbm, out_ref, ids_ref, cents_ref, onehot_ref, sems):
    count, width = cents_hbm.shape
    groups, rows = ids_ref.shape
    ids_copy = pltpu.make_async_copy(ids_hbm, ids_ref, sems.at[width // step])
    ids_copy.start()
    copies = [
        pltpu.make_async_copy(
            cents_hbm.at[:, pl.ds(step * j, step)], cents_ref.at[j], sems.at[j]
        )
        for j in range(width // step)
    ]
    for copy in copies:
        copy.start()
    ids_copy.wait()
    local = ids_ref[...] - lax.axis_index("cent") * count
    mine = (local >= 0) & (local < count)
    before = lax.broadcasted_iota(jnp.int32, (rows, rows), 0) <= lax.broadcasted_iota(
        jnp.int32, (rows, rows), 1
    )
    rank = jnp.dot(
        mine.astype(f32).astype(bf16), before.astype(f32).astype(bf16), preferred_element_type=f32
    )
    slot = jnp.where(mine, rank - 1.0, -1.0)
    local = local.astype(f32)
    spread_slot = jnp.concatenate(
        [jnp.broadcast_to(slot[g : g + 1], (slots, rows)) for g in range(groups)], axis=0
    )
    spread_local = jnp.concatenate(
        [jnp.broadcast_to(local[g : g + 1], (slots, rows)) for g in range(groups)], axis=0
    )
    number = lax.rem(lax.broadcasted_iota(jnp.int32, (groups * slots, rows), 0), slots).astype(f32)
    chosen = jnp.sum(jnp.where(spread_slot == number, spread_local + 1.0, 0.0), axis=1, keepdims=True)
    chosen = chosen.astype(jnp.int32) - 1
    for j in range(count // 256):
        at = lax.broadcasted_iota(jnp.int32, (groups * slots, 256), 1) + 256 * j
        onehot_ref[:, 256 * j : 256 * j + 256] = (at == chosen).astype(f32).astype(bf16)
    for j, copy in enumerate(copies):
        copy.wait()
        lanes = slice(step * j, step * j + step)
        out_ref[:, lanes] = jnp.dot(
            onehot_ref[...], cents_ref[j], preferred_element_type=f32
        ).astype(bf16)


def gather(ids, cents, slots):
    groups, _ = ids.shape
    count, width = cents.shape
    step = 256
    return pl.pallas_call(
        functools.partial(gather_kernel, slots, step),
        out_shape=pltpu.VMEM((groups * slots, width), bf16),
        in_specs=[HBM, HBM],
        out_specs=VM,
        scratch_shapes=[
            pltpu.VMEM(ids.shape, jnp.int32),
            pltpu.VMEM((width // step, count, step), bf16),
            pltpu.VMEM((groups * slots, count), bf16),
            pltpu.SemaphoreType.DMA((width // step + 1,)),
        ],
        cost_estimate=pl.CostEstimate(
            flops=2 * groups * slots * count * width, bytes_accessed=count * width * 2, transcendentals=0
        ),
        compiler_params=LIMIT,
        name="gather",
    )(off_chip(ids), off_chip(cents))


def residual_kernel(count, slots, ids_ref, fetched_ref, top_ref, bottom_ref, out_ref):
    width, rows = out_ref.shape
    ids = ids_ref[pl.ds(lax.axis_index("cent"), 1), :]
    owner = lax.div(ids, count)
    across = jnp.broadcast_to(owner, (rows, rows))
    down = across.astype(f32).T.astype(jnp.int32)
    earlier = lax.broadcasted_iota(jnp.int32, (rows, rows), 0) < lax.broadcasted_iota(
        jnp.int32, (rows, rows), 1
    )
    rank = jnp.sum(jnp.where((across == down) & earlier, 1.0, 0.0), axis=0, keepdims=True)
    slot = owner * slots + rank.astype(jnp.int32)
    number = lax.broadcasted_iota(jnp.int32, (fetched_ref.shape[0], rows), 0)
    place = (number == slot).astype(f32).astype(bf16)
    for j in range(width // 128):
        lanes = slice(128 * j, 128 * j + 128)
        fetched = lax.dot_general(
            place, fetched_ref[:, lanes], (((0,), (0,)), ((), ())), preferred_element_type=f32
        )
        q = jnp.concatenate([top_ref[:, lanes], bottom_ref[:, lanes]], axis=0)
        out_ref[lanes, :] = (q.astype(f32) - fetched).T


def residuals(ids, fetched, q, count, slots):
    rows, width = 2 * q[0].shape[0], q[0].shape[1]
    return pl.pallas_call(
        functools.partial(residual_kernel, count, slots),
        out_shape=pltpu.VMEM((width, rows), f32),
        in_specs=[VM] * 4,
        out_specs=VM,
        cost_estimate=pl.CostEstimate(
            flops=2 * fetched.size * rows, bytes_accessed=fetched.size * 2 + rows * width * 6, transcendentals=0
        ),
        compiler_params=LIMIT,
        name="residuals",
    )(ids, on_chip(fetched), *[on_chip(x) for x in q])


def nearest_kernel(step, *refs):
    x_refs, (cents_hbm, out_ref, cents_ref, sems) = refs[:-4], refs[-4:]
    steps = cents_ref.shape[0]

    def copy(i):
        at = pl.ds(pl.multiple_of(i * step, step), step)
        return pltpu.make_async_copy(cents_hbm.at[at, :], cents_ref.at[i], sems.at[i])

    for i in range(steps):
        copy(i).start()
    groups = [[]]
    for ref in x_refs:
        if sum(r.shape[0] for r in groups[-1]) == 256:
            groups.append([])
        groups[-1].append(ref)
    out_ref[...] = jnp.full(out_ref.shape, jnp.inf, f32)

    @pl.loop(0, steps)
    def _(i):
        copy(i).wait()
        block = cents_ref[i]
        total = None
        for b in range(block.shape[1] // 128):
            wide = block[:, 128 * b : 128 * b + 128].astype(f32)
            total = wide * wide if total is None else total + wide * wide
        squares = jnp.broadcast_to(jnp.sum(total, axis=1, keepdims=True), (step, 128))
        squares = jnp.concatenate([squares, squares], axis=1)
        for j, group in enumerate(groups):
            x = jnp.concatenate([r[...] for r in group], axis=0)
            cross = lax.dot_general(block, x, (((1,), (1,)), ((), ())), preferred_element_type=f32)
            low = jnp.min(squares - 2.0 * cross, axis=0, keepdims=True)
            for k in range(2):
                row = slice(2 * j + k, 2 * j + k + 1)
                out_ref[row, :] = jnp.minimum(out_ref[row, :], low[:, 128 * k : 128 * k + 128])


def nearest(xs, cents):
    count, width = cents.shape
    rows = sum(x.shape[0] for x in xs)
    step = 256
    return pl.pallas_call(
        functools.partial(nearest_kernel, step),
        out_shape=pltpu.VMEM((rows // 128, 128), f32),
        in_specs=[VM] * len(xs) + [HBM],
        out_specs=VM,
        scratch_shapes=[
            pltpu.VMEM((count // step, step, width), bf16),
            pltpu.SemaphoreType.DMA((count // step,)),
        ],
        cost_estimate=pl.CostEstimate(
            flops=2 * rows * count * width, bytes_accessed=count * width * 2 + rows * width * 2, transcendentals=0
        ),
        compiler_params=LIMIT,
        name="nearest",
    )(*[on_chip(x) for x in xs], off_chip(cents))


def halves_of(x):
    high = x.astype(bf16)
    return high, (x - high.astype(f32)).astype(bf16)


def statistics_kernel(where, sub_ref, one_ref, two_ref, *refs):
    gap_refs, (mine_ref, theirs_ref) = refs[:-2], refs[-2:]
    groups, width, rows = sub_ref.shape
    words = 256
    high, low = [], []
    for g in range(groups):
        h, l = halves_of(sub_ref[g])
        high.append(h)
        low.append(l)
    ones = jnp.ones((16, groups * rows), bf16)
    left = jnp.concatenate([jnp.concatenate(high, axis=1), jnp.concatenate(low, axis=1), ones], axis=0)
    word = lax.broadcasted_iota(jnp.int32, (words, groups * rows), 0)
    core = lax.rem(lax.axis_index("cent"), 2)
    odd = core == 1

    def totals(codes_ref):
        hit = (word == codes_ref[...]).astype(f32).astype(bf16)
        out = lax.dot_general(left, hit, (((1,), (1,)), ((), ())), preferred_element_type=f32)
        return out[:width] + out[width : 2 * width], out[2 * width : 2 * width + 8]

    for at, codes_ref in enumerate((one_ref, two_ref)):
        total, count = totals(codes_ref)
        rows_at = slice(width * at, width * at + width)
        a, b = total[:, :128], total[:, 128:]
        mine_ref[rows_at, :] = jnp.where(odd, b, a)
        theirs_ref[rows_at, :] = jnp.where(odd, a, b)
        a, b = count[:4, :128], count[:4, 128:]
        count_at = slice(2 * width + 4 * at, 2 * width + 4 * at + 4)
        mine_ref[count_at, :] = jnp.where(odd, b, a)
        theirs_ref[count_at, :] = jnp.where(odd, a, b)
    for j in range(8):
        for out_ref, d in ((mine_ref, 2 * j), (theirs_ref, 2 * j + 1)):
            k, row = where[d]
            out_ref[STATS + j : STATS + j + 1, :] = gap_refs[k][row : row + 1, :]


def statistics(sub, codes_one, codes_two, lows, where):
    shape = pltpu.VMEM((PAY, 128), f32)
    return pl.pallas_call(
        functools.partial(statistics_kernel, where),
        out_shape=(shape, shape),
        in_specs=[VM] * (3 + len(lows)),
        out_specs=(VM, VM),
        cost_estimate=pl.CostEstimate(
            flops=2 * 2 * sub.size * 512, bytes_accessed=sub.size * 4, transcendentals=0
        ),
        compiler_params=LIMIT,
        name="statistics",
    )(on_chip(sub), codes_one, codes_two, *[on_chip(x) for x in lows])


def join_kernel(shift, a_ref, b_ref, out_ref):
    out_ref[:STATS, :] = a_ref[:STATS, :] + b_ref[:STATS, :]
    keep = PAY - STATS - shift
    out_ref[STATS:PAY, :] = a_ref[STATS:PAY, :]
    out_ref[STATS : STATS + keep, :] = jnp.minimum(
        a_ref[STATS : STATS + keep, :], b_ref[STATS + shift : PAY, :]
    )


def join(a, b, shift):
    return pl.pallas_call(
        functools.partial(join_kernel, shift),
        out_shape=pltpu.VMEM(a.shape, f32),
        in_specs=[VM, VM],
        out_specs=VM,
        cost_estimate=pl.CostEstimate(flops=a.size, bytes_accessed=a.size * 12, transcendentals=0),
        compiler_params=LIMIT,
        name="join",
    )(on_chip(a), on_chip(b))


def update_kernel(width, a_ref, b_ref, c_ref, d_ref, init_ref, squares_ref, books_ref, gap_ref):
    core = lax.rem(lax.axis_index("cent"), 2)
    total = (a_ref[:STATS, :] + b_ref[:STATS, :]) + (c_ref[:STATS, :] + d_ref[:STATS, :])
    init = jnp.where(core == 1, init_ref[:, 128:], init_ref[:, :128])
    count_one = total[2 * width : 2 * width + 1]
    count_two = total[2 * width + 4 : 2 * width + 5]
    one = (total[:width] + prior_weight * init) / (count_one + prior_weight)
    two = (total[width : 2 * width] + prior_weight * one) / (count_two + prior_weight)
    books_ref[:width, :] = one
    books_ref[width:, :] = two
    low = jnp.minimum(
        jnp.minimum(a_ref[STATS : STATS + 1, :], b_ref[STATS + 1 : STATS + 2, :]),
        jnp.minimum(c_ref[STATS + 2 : STATS + 3, :], d_ref[STATS + 3 : STATS + 4, :]),
    )
    gap_ref[...] = (low + squares_ref[...]) * (1.0 / 1024.0)


def update(parts, init, squares):
    width = init.shape[0]
    return pl.pallas_call(
        functools.partial(update_kernel, width),
        out_shape=(
            pltpu.VMEM((2 * width, 128), f32),
            jax.ShapeDtypeStruct((1, 128), f32),
        ),
        in_specs=[VM] * 6,
        out_specs=(VM, VM),
        cost_estimate=pl.CostEstimate(flops=8 * STATS * 128, bytes_accessed=5 * PAY * 512, transcendentals=0),
        compiler_params=LIMIT,
        name="update",
    )(*[on_chip(x) for x in parts], init, on_chip(squares))


def distortion_kernel(sub_ref, two_ref, mine_ref, theirs_ref, one_out_ref, two_out_ref, out_ref):
    groups, width, rows = sub_ref.shape
    odd = lax.rem(lax.axis_index("cent"), 2) == 1
    mine, theirs = mine_ref[...], theirs_ref[...]
    books = jnp.concatenate([jnp.where(odd, theirs, mine), jnp.where(odd, mine, theirs)], axis=1)
    one_out_ref[...] = books[:width]
    book = books[width:]
    two_out_ref[...] = book
    high, low = halves_of(book)
    left = jnp.concatenate([high, low], axis=0)
    words = book.shape[1]
    for g in range(0, groups, 2):
        lanes = slice(rows * g, rows * g + 2 * rows)
        word = lax.broadcasted_iota(jnp.int32, (words, 2 * rows), 0)
        hit = (word == two_ref[:, lanes]).astype(f32).astype(bf16)
        rebuilt = jnp.dot(left, hit, preferred_element_type=f32)
        rebuilt = rebuilt[:width] + rebuilt[width:]
        sub = jnp.concatenate([sub_ref[g], sub_ref[g + 1]], axis=1)
        miss = sub - rebuilt
        out_ref[:, lanes] = jnp.sum(miss * miss, axis=0, keepdims=True) * (1.0 / width)


def distortions(sub, codes_two, mine, theirs):
    groups, width, rows = sub.shape
    return pl.pallas_call(
        distortion_kernel,
        out_shape=(
            jax.ShapeDtypeStruct((width, 256), f32),
            jax.ShapeDtypeStruct((width, 256), f32),
            jax.ShapeDtypeStruct((1, groups * rows), f32),
        ),
        in_specs=[VM] * 4,
        out_specs=(VM, VM, VM),
        cost_estimate=pl.CostEstimate(
            flops=4 * sub.size * 256, bytes_accessed=sub.size * 4, transcendentals=0
        ),
        compiler_params=LIMIT,
        name="distortion",
    )(on_chip(sub), codes_two, on_chip(mine), on_chip(theirs))


def swap(x, offset):
    return lax.ppermute(x, "cent", [(i, i ^ offset) for i in range(16)])


def step(emb_values, emb_scales, coarse_ids, centroids, codes_one, codes_two, codebook_init):
    own_rows, width = emb_values.shape
    count = centroids.shape[0]
    sub_width = codebook_init.shape[2]
    peers = coarse_ids.shape[0]
    slots = 16

    *q, row_squares = quantize(emb_values, emb_scales)

    core = 1

    def hop(xs, offset):
        out = []
        for x in xs:
            out.append(swap(x, offset))
        return out

    a = hop(q[::-1], 2)[::-1]
    b = hop(q, 6)
    z = hop(q, 8)
    blocks = {0: q, core: hop(q, core), 2: a, 6: b, 8: z}

    sent = gather(coarse_ids, centroids, slots)
    fetched = lax.all_to_all(sent.reshape(peers, slots, width), "cent", 0, 0)
    fetched = fetched.reshape(peers * slots, width)

    blocks[4] = hop(b[:1], 2) + hop(a[1:], 6)
    blocks[10], blocks[14] = hop(z, 2), hop(z, 6)
    blocks[12] = hop(blocks[14][:1], 2) + hop(blocks[10][1:], 6)
    for d in (2, 6, 8, 4, 10, 14, 12):
        blocks[d ^ core] = hop(blocks[d], core)

    orders = ((0, 1, 2, 3), (6, 7, 8, 9), (4, 5, 10, 11, 14, 15, 12, 13))
    lows = []
    for order in orders:
        lows.append(nearest([x for d in order for x in blocks[d]], centroids))
    where = {d: (k, j) for k, order in enumerate(orders) for j, d in enumerate(order)}

    residual = residuals(coarse_ids, fetched, q, count, slots)
    stacked = residual.reshape(width // sub_width, sub_width, own_rows)
    sub = lax.all_to_all(stacked, "rows", 0, 0)

    mine, theirs = statistics(sub, codes_one, codes_two, lows, where)
    mine = join(mine, swap(theirs, 1), 0)
    mine = join(mine, swap(mine, 8), 4)
    parts = [mine] + [swap(mine, d) for d in (2, 4, 6)]
    init = codebook_init[0].T
    books, coarse_gap = update(parts, init, row_squares)
    book_one, book_two, distortion = distortions(sub, codes_two, books, swap(books, 1))
    return coarse_gap[0], book_one.T[None], book_two.T[None], distortion


def solution(mesh):
    placed = (
        P(("cent", "rows"), None),
        P(("cent", "rows"), None),
        P(None, "rows"),
        P("cent", None),
        P("rows", "cent"),
        P("rows", "cent"),
        P("rows", None, None),
    )
    return jax.shard_map(
        step,
        mesh=mesh,
        in_specs=placed,
        out_specs=(
            P(("cent", "rows")),
            P("rows", None, None),
            P("rows", None, None),
            P("rows", "cent"),
        ),
        check_vma=False,
    )
```

```python
import functools

import jax
import jax.numpy as jnp
from jax import lax
from jax.experimental import pallas as pl
from jax.experimental.pallas import tpu as pltpu
from jax.sharding import PartitionSpec as P


bf16 = jnp.bfloat16
f32 = jnp.float32
prior_weight = 8.0
VM = pl.BlockSpec(memory_space=pltpu.VMEM)
HBM = pl.BlockSpec(memory_space=pltpu.HBM)
LIMIT = pltpu.CompilerParams(vmem_limit_bytes=16 << 20)


def off_chip(x):
    return pltpu.with_memory_space_constraint(x, pltpu.HBM)


def on_chip(x):
    return pltpu.with_memory_space_constraint(x, pltpu.VMEM)


STATS = 136
PAY = 144


def quantize_kernel(values_hbm, scales_hbm, q_ref, squares_ref, values, scales_t, sems):
    copies = (
        pltpu.make_async_copy(values_hbm, values, sems.at[0]),
        pltpu.make_async_copy(scales_hbm, scales_t, sems.at[1]),
    )
    for copy in copies:
        copy.start()
    for copy in copies:
        copy.wait()
    scales = scales_t[...].astype(f32).T
    squares = None
    for b in range(scales.shape[1]):
        lanes = slice(128 * b, 128 * b + 128)
        q = (values[:, lanes].astype(f32) * scales[:, b : b + 1]).astype(bf16)
        q_ref[:, lanes] = q
        wide = q.astype(f32)
        squares = wide * wide if squares is None else squares + wide * wide
    squares_ref[...] = jnp.sum(squares.T, axis=0, keepdims=True)


def quantize(values, scales):
    rows, width = values.shape
    scales = scales.T
    return pl.pallas_call(
        quantize_kernel,
        out_shape=(
            pltpu.VMEM((rows, width), bf16),
            pltpu.VMEM((1, rows), f32),
        ),
        in_specs=[HBM, HBM],
        out_specs=(VM, VM),
        scratch_shapes=[
            pltpu.VMEM(values.shape, bf16),
            pltpu.VMEM(scales.shape, bf16),
            pltpu.SemaphoreType.DMA((2,)),
        ],
        cost_estimate=pl.CostEstimate(flops=rows * width * 3, bytes_accessed=rows * width * 4, transcendentals=0),
        compiler_params=LIMIT,
        name="quantize",
    )(off_chip(values), off_chip(scales))


def gather_kernel(slots, step, ids_hbm, cents_hbm, out_ref, ids_ref, cents_ref, onehot_ref, sems):
    count, width = cents_hbm.shape
    groups, rows = ids_ref.shape
    ids_copy = pltpu.make_async_copy(ids_hbm, ids_ref, sems.at[width // step])
    ids_copy.start()
    copies = [
        pltpu.make_async_copy(
            cents_hbm.at[:, pl.ds(step * j, step)], cents_ref.at[j], sems.at[j]
        )
        for j in range(width // step)
    ]
    for copy in copies[:2]:
        copy.start()
    ids_copy.wait()
    local = ids_ref[...] - lax.axis_index("cent") * count
    mine = (local >= 0) & (local < count)
    before = lax.broadcasted_iota(jnp.int32, (rows, rows), 0) <= lax.broadcasted_iota(
        jnp.int32, (rows, rows), 1
    )
    rank = jnp.dot(
        mine.astype(f32).astype(bf16), before.astype(f32).astype(bf16), preferred_element_type=f32
    )
    slot = jnp.where(mine, rank - 1.0, -1.0)
    local = local.astype(f32)
    spread_slot = jnp.concatenate(
        [jnp.broadcast_to(slot[g : g + 1], (slots, rows)) for g in range(groups)], axis=0
    )
    spread_local = jnp.concatenate(
        [jnp.broadcast_to(local[g : g + 1], (slots, rows)) for g in range(groups)], axis=0
    )
    number = lax.rem(lax.broadcasted_iota(jnp.int32, (groups * slots, rows), 0), slots).astype(f32)
    chosen = jnp.sum(jnp.where(spread_slot == number, spread_local + 1.0, 0.0), axis=1, keepdims=True)
    chosen = chosen.astype(jnp.int32) - 1
    for j in range(count // 256):
        at = lax.broadcasted_iota(jnp.int32, (groups * slots, 256), 1) + 256 * j
        onehot_ref[:, 256 * j : 256 * j + 256] = (at == chosen).astype(f32).astype(bf16)
    for j, copy in enumerate(copies):
        copy.wait()
        if j + 2 < len(copies):
            copies[j + 2].start()
        lanes = slice(step * j, step * j + step)
        out_ref[:, lanes] = jnp.dot(
            onehot_ref[...], cents_ref[j], preferred_element_type=f32
        ).astype(bf16)


def gather(ids, cents, slots):
    groups, _ = ids.shape
    count, width = cents.shape
    step = 256
    return pl.pallas_call(
        functools.partial(gather_kernel, slots, step),
        out_shape=pltpu.VMEM((groups * slots, width), bf16),
        in_specs=[HBM, HBM],
        out_specs=VM,
        scratch_shapes=[
            pltpu.VMEM(ids.shape, jnp.int32),
            pltpu.VMEM((width // step, count, step), bf16),
            pltpu.VMEM((groups * slots, count), bf16),
            pltpu.SemaphoreType.DMA((width // step + 1,)),
        ],
        cost_estimate=pl.CostEstimate(
            flops=2 * groups * slots * count * width, bytes_accessed=count * width * 2, transcendentals=0
        ),
        compiler_params=LIMIT,
        name="gather",
    )(off_chip(ids), off_chip(cents))


def residual_kernel(count, slots, ids_ref, fetched_ref, q_ref, out_ref):
    width, rows = out_ref.shape
    ids = ids_ref[pl.ds(lax.axis_index("cent"), 1), :]
    owner = lax.div(ids, count)
    across = jnp.broadcast_to(owner, (rows, rows))
    down = across.astype(f32).T.astype(jnp.int32)
    earlier = lax.broadcasted_iota(jnp.int32, (rows, rows), 0) < lax.broadcasted_iota(
        jnp.int32, (rows, rows), 1
    )
    rank = jnp.sum(jnp.where((across == down) & earlier, 1.0, 0.0), axis=0, keepdims=True)
    slot = owner * slots + rank.astype(jnp.int32)
    number = lax.broadcasted_iota(jnp.int32, (fetched_ref.shape[0], rows), 0)
    place = (number == slot).astype(f32).astype(bf16)
    for j in range(width // 128):
        lanes = slice(128 * j, 128 * j + 128)
        fetched = lax.dot_general(
            place, fetched_ref[:, lanes], (((0,), (0,)), ((), ())), preferred_element_type=f32
        )
        out_ref[lanes, :] = (q_ref[:, lanes].astype(f32) - fetched).T


def residuals(ids, fetched, q, count, slots):
    rows, width = q.shape
    return pl.pallas_call(
        functools.partial(residual_kernel, count, slots),
        out_shape=pltpu.VMEM((width, rows), f32),
        in_specs=[VM] * 3,
        out_specs=VM,
        cost_estimate=pl.CostEstimate(
            flops=2 * fetched.size * rows, bytes_accessed=fetched.size * 2 + rows * width * 6, transcendentals=0
        ),
        compiler_params=LIMIT,
        name="residuals",
    )(ids, on_chip(fetched), on_chip(q))


def nearest_kernel(step, ahead, *refs):
    x_refs, (cents_hbm, out_ref, cents_ref, sems) = refs[:-4], refs[-4:]
    half = step // 2
    copies = [
        pltpu.make_async_copy(cents_hbm.at[pl.ds(half * i, half), :], cents_ref.at[i], sems.at[i])
        for i in range(cents_ref.shape[0])
    ]
    for copy in copies[:ahead]:
        copy.start()
    best = [None] * (len(x_refs) // 2)
    for i in range(0, len(copies), 2):
        for k in (i, i + 1):
            copies[k].wait()
            if k + ahead < len(copies):
                copies[k + ahead].start()
        block = jnp.concatenate([cents_ref[i], cents_ref[i + 1]], axis=0)
        total = None
        for b in range(block.shape[1] // 128):
            wide = block[:, 128 * b : 128 * b + 128].astype(f32)
            total = wide * wide if total is None else total + wide * wide
        squares = jnp.broadcast_to(jnp.sum(total, axis=1, keepdims=True), (step, 128))
        squares = jnp.concatenate([squares, squares], axis=1)
        for j in range(len(best)):
            x = jnp.concatenate([x_refs[2 * j][...], x_refs[2 * j + 1][...]], axis=0)
            cross = lax.dot_general(block, x, (((1,), (1,)), ((), ())), preferred_element_type=f32)
            low = jnp.min(squares - 2.0 * cross, axis=0, keepdims=True)
            best[j] = low if best[j] is None else jnp.minimum(best[j], low)
    for j, low in enumerate(best):
        for k in range(2):
            out_ref[2 * j + k : 2 * j + k + 1, :] = low[:, 128 * k : 128 * k + 128]


def nearest(xs, cents):
    count, width = cents.shape
    rows = sum(x.shape[0] for x in xs)
    step = 512
    return pl.pallas_call(
        functools.partial(nearest_kernel, step, 3),
        out_shape=pltpu.VMEM((rows // 128, 128), f32),
        in_specs=[VM] * len(xs) + [HBM],
        out_specs=VM,
        scratch_shapes=[
            pltpu.VMEM((2 * count // step, step // 2, width), bf16),
            pltpu.SemaphoreType.DMA((2 * count // step,)),
        ],
        cost_estimate=pl.CostEstimate(
            flops=2 * rows * count * width, bytes_accessed=count * width * 2 + rows * width * 2, transcendentals=0
        ),
        compiler_params=LIMIT,
        name="nearest",
    )(*[on_chip(x) for x in xs], off_chip(cents))


def halves_of(x):
    high = x.astype(bf16)
    return high, (x - high.astype(f32)).astype(bf16)


def statistics_kernel(where, sub_ref, one_ref, two_ref, *refs):
    gap_refs, (mine_ref, theirs_ref) = refs[:-2], refs[-2:]
    groups, width, rows = sub_ref.shape
    words = 256
    high, low = [], []
    for g in range(groups):
        h, l = halves_of(sub_ref[g])
        high.append(h)
        low.append(l)
    ones = jnp.ones((16, groups * rows), bf16)
    left = jnp.concatenate([jnp.concatenate(high, axis=1), jnp.concatenate(low, axis=1), ones], axis=0)
    word = lax.broadcasted_iota(jnp.int32, (words, groups * rows), 0)
    core = lax.rem(lax.axis_index("cent"), 2)
    odd = core == 1

    def totals(codes_ref):
        hit = (word == codes_ref[...]).astype(f32).astype(bf16)
        out = lax.dot_general(left, hit, (((1,), (1,)), ((), ())), preferred_element_type=f32)
        return out[:width] + out[width : 2 * width], out[2 * width : 2 * width + 8]

    for at, codes_ref in enumerate((one_ref, two_ref)):
        total, count = totals(codes_ref)
        rows_at = slice(width * at, width * at + width)
        a, b = total[:, :128], total[:, 128:]
        mine_ref[rows_at, :] = jnp.where(odd, b, a)
        theirs_ref[rows_at, :] = jnp.where(odd, a, b)
        a, b = count[:4, :128], count[:4, 128:]
        count_at = slice(2 * width + 4 * at, 2 * width + 4 * at + 4)
        mine_ref[count_at, :] = jnp.where(odd, b, a)
        theirs_ref[count_at, :] = jnp.where(odd, a, b)
    for j in range(8):
        for out_ref, d in ((mine_ref, 2 * j), (theirs_ref, 2 * j + 1)):
            k, row = where[d]
            out_ref[STATS + j : STATS + j + 1, :] = gap_refs[k][row : row + 1, :]


def statistics(sub, codes_one, codes_two, lows, where):
    shape = pltpu.VMEM((PAY, 128), f32)
    return pl.pallas_call(
        functools.partial(statistics_kernel, where),
        out_shape=(shape, shape),
        in_specs=[VM] * (3 + len(lows)),
        out_specs=(VM, VM),
        cost_estimate=pl.CostEstimate(
            flops=2 * 2 * sub.size * 512, bytes_accessed=sub.size * 4, transcendentals=0
        ),
        compiler_params=LIMIT,
        name="statistics",
    )(on_chip(sub), codes_one, codes_two, *[on_chip(x) for x in lows])


def join_kernel(shift, a_ref, b_ref, out_ref):
    out_ref[:STATS, :] = a_ref[:STATS, :] + b_ref[:STATS, :]
    keep = PAY - STATS - shift
    out_ref[STATS:PAY, :] = a_ref[STATS:PAY, :]
    out_ref[STATS : STATS + keep, :] = jnp.minimum(
        a_ref[STATS : STATS + keep, :], b_ref[STATS + shift : PAY, :]
    )


def join(a, b, shift):
    return pl.pallas_call(
        functools.partial(join_kernel, shift),
        out_shape=pltpu.VMEM(a.shape, f32),
        in_specs=[VM, VM],
        out_specs=VM,
        cost_estimate=pl.CostEstimate(flops=a.size, bytes_accessed=a.size * 12, transcendentals=0),
        compiler_params=LIMIT,
        name="join",
    )(on_chip(a), on_chip(b))


def update_kernel(width, a_ref, b_ref, c_ref, d_ref, init_ref, squares_ref, books_ref, gap_ref):
    core = lax.rem(lax.axis_index("cent"), 2)
    total = (a_ref[:STATS, :] + b_ref[:STATS, :]) + (c_ref[:STATS, :] + d_ref[:STATS, :])
    init = jnp.where(core == 1, init_ref[:, 128:], init_ref[:, :128])
    count_one = total[2 * width : 2 * width + 1]
    count_two = total[2 * width + 4 : 2 * width + 5]
    one = (total[:width] + prior_weight * init) / (count_one + prior_weight)
    two = (total[width : 2 * width] + prior_weight * one) / (count_two + prior_weight)
    books_ref[:width, :] = one
    books_ref[width:, :] = two
    low = jnp.minimum(
        jnp.minimum(a_ref[STATS : STATS + 1, :], b_ref[STATS + 1 : STATS + 2, :]),
        jnp.minimum(c_ref[STATS + 2 : STATS + 3, :], d_ref[STATS + 3 : STATS + 4, :]),
    )
    gap_ref[...] = (low + squares_ref[...]) * (1.0 / 1024.0)


def update(parts, init, squares):
    width = init.shape[0]
    return pl.pallas_call(
        functools.partial(update_kernel, width),
        out_shape=(
            pltpu.VMEM((2 * width, 128), f32),
            jax.ShapeDtypeStruct((1, 128), f32),
        ),
        in_specs=[VM] * 6,
        out_specs=(VM, VM),
        cost_estimate=pl.CostEstimate(flops=8 * STATS * 128, bytes_accessed=5 * PAY * 512, transcendentals=0),
        compiler_params=LIMIT,
        name="update",
    )(*[on_chip(x) for x in parts], init, on_chip(squares))


def distortion_kernel(sub_ref, two_ref, mine_ref, theirs_ref, one_out_ref, two_out_ref, out_ref):
    groups, width, rows = sub_ref.shape
    odd = lax.rem(lax.axis_index("cent"), 2) == 1
    mine, theirs = mine_ref[...], theirs_ref[...]
    books = jnp.concatenate([jnp.where(odd, theirs, mine), jnp.where(odd, mine, theirs)], axis=1)
    one_out_ref[...] = books[:width]
    book = books[width:]
    two_out_ref[...] = book
    high, low = halves_of(book)
    left = jnp.concatenate([high, low], axis=0)
    words = book.shape[1]
    for g in range(0, groups, 2):
        lanes = slice(rows * g, rows * g + 2 * rows)
        word = lax.broadcasted_iota(jnp.int32, (words, 2 * rows), 0)
        hit = (word == two_ref[:, lanes]).astype(f32).astype(bf16)
        rebuilt = jnp.dot(left, hit, preferred_element_type=f32)
        rebuilt = rebuilt[:width] + rebuilt[width:]
        sub = jnp.concatenate([sub_ref[g], sub_ref[g + 1]], axis=1)
        miss = sub - rebuilt
        out_ref[:, lanes] = jnp.sum(miss * miss, axis=0, keepdims=True) * (1.0 / width)


def distortions(sub, codes_two, mine, theirs):
    groups, width, rows = sub.shape
    return pl.pallas_call(
        distortion_kernel,
        out_shape=(
            jax.ShapeDtypeStruct((width, 256), f32),
            jax.ShapeDtypeStruct((width, 256), f32),
            jax.ShapeDtypeStruct((1, groups * rows), f32),
        ),
        in_specs=[VM] * 4,
        out_specs=(VM, VM, VM),
        cost_estimate=pl.CostEstimate(
            flops=4 * sub.size * 256, bytes_accessed=sub.size * 4, transcendentals=0
        ),
        compiler_params=LIMIT,
        name="distortion",
    )(on_chip(sub), codes_two, on_chip(mine), on_chip(theirs))


def swap(x, offset):
    return lax.ppermute(x, "cent", [(i, i ^ offset) for i in range(16)])


def step(emb_values, emb_scales, coarse_ids, centroids, codes_one, codes_two, codebook_init):
    own_rows, width = emb_values.shape
    count = centroids.shape[0]
    sub_width = codebook_init.shape[2]
    peers = coarse_ids.shape[0]
    slots = 16

    q, row_squares = quantize(emb_values, emb_scales)

    core = 1

    blocks = {0: q, 2: swap(q, 2), 6: swap(q, 6), 8: swap(q, 8)}
    blocks[core] = swap(q, core)

    sent = gather(coarse_ids, centroids, slots)
    fetched = lax.all_to_all(sent.reshape(peers, slots, width), "cent", 0, 0)
    fetched = fetched.reshape(peers * slots, width)

    blocks[14] = swap(blocks[8], 6)
    blocks[10] = swap(blocks[8], 2)
    blocks[4] = swap(blocks[6], 2)
    blocks[12] = swap(blocks[14], 2)
    for d in (2, 6, 8, 4, 10, 14, 12):
        blocks[d ^ core] = swap(blocks[d], core)

    orders = ((0, 1, 2, 3, 6, 7, 8, 9), (4, 5, 10, 11, 14, 15, 12, 13))
    lows = []
    for order in orders:
        lows.append(nearest([blocks[d] for d in order], centroids))
    where = {d: (k, j) for k, order in enumerate(orders) for j, d in enumerate(order)}

    residual = residuals(coarse_ids, fetched, q, count, slots)
    stacked = residual.reshape(width // sub_width, sub_width, own_rows)
    sub = lax.all_to_all(stacked, "rows", 0, 0)

    mine, theirs = statistics(sub, codes_one, codes_two, lows, where)
    mine = join(mine, swap(theirs, 1), 0)
    mine = join(mine, swap(mine, 8), 4)
    parts = [mine] + [swap(mine, d) for d in (2, 4, 6)]
    init = codebook_init[0].T
    books, coarse_gap = update(parts, init, row_squares)
    book_one, book_two, distortion = distortions(sub, codes_two, books, swap(books, 1))
    return coarse_gap[0], book_one.T[None], book_two.T[None], distortion


def solution(mesh):
    placed = (
        P(("cent", "rows"), None),
        P(("cent", "rows"), None),
        P(None, "rows"),
        P("cent", None),
        P("rows", "cent"),
        P("rows", "cent"),
        P("rows", None, None),
    )
    return jax.shard_map(
        step,
        mesh=mesh,
        in_specs=placed,
        out_specs=(
            P(("cent", "rows")),
            P("rows", None, None),
            P("rows", None, None),
            P("rows", "cent"),
        ),
        check_vma=False,
    )
```

```python
import functools

import jax
import jax.numpy as jnp
from jax import lax
from jax.experimental import pallas as pl
from jax.experimental.pallas import tpu as pltpu
from jax.sharding import PartitionSpec as P


bf16 = jnp.bfloat16
f32 = jnp.float32
prior_weight = 8.0
VM = pl.BlockSpec(memory_space=pltpu.VMEM)
HBM = pl.BlockSpec(memory_space=pltpu.HBM)
LIMIT = pltpu.CompilerParams(vmem_limit_bytes=16 << 20)


def off_chip(x):
    return pltpu.with_memory_space_constraint(x, pltpu.HBM)


def on_chip(x):
    return pltpu.with_memory_space_constraint(x, pltpu.VMEM)


STATS = 136
PAY = 144


def prepare_kernel(
    slots, step, values_hbm, scales_hbm, ids_hbm, cents_hbm, q_ref, squares_ref, out_ref,
    values, scales_t, ids_ref, cents_ref, onehot_ref, sems,
):
    count, width = cents_hbm.shape
    groups, rows = ids_ref.shape
    small = (
        pltpu.make_async_copy(ids_hbm, ids_ref, sems.at[0]),
        pltpu.make_async_copy(scales_hbm, scales_t, sems.at[1]),
        pltpu.make_async_copy(values_hbm, values, sems.at[2]),
    )
    large = [
        pltpu.make_async_copy(cents_hbm.at[:, pl.ds(step * j, step)], cents_ref.at[j], sems.at[3 + j])
        for j in range(width // step)
    ]
    for copy in small:
        copy.start()
    for copy in large[:2]:
        copy.start()

    small[0].wait()
    local = ids_ref[...] - lax.axis_index("cent") * count
    mine = (local >= 0) & (local < count)
    before = lax.broadcasted_iota(jnp.int32, (rows, rows), 0) <= lax.broadcasted_iota(
        jnp.int32, (rows, rows), 1
    )
    rank = jnp.dot(
        mine.astype(f32).astype(bf16), before.astype(f32).astype(bf16), preferred_element_type=f32
    )
    slot = jnp.where(mine, rank - 1.0, -1.0)
    local = local.astype(f32)
    spread_slot = jnp.concatenate(
        [jnp.broadcast_to(slot[g : g + 1], (slots, rows)) for g in range(groups)], axis=0
    )
    spread_local = jnp.concatenate(
        [jnp.broadcast_to(local[g : g + 1], (slots, rows)) for g in range(groups)], axis=0
    )
    number = lax.rem(lax.broadcasted_iota(jnp.int32, (groups * slots, rows), 0), slots).astype(f32)
    chosen = jnp.sum(jnp.where(spread_slot == number, spread_local + 1.0, 0.0), axis=1, keepdims=True)
    chosen = chosen.astype(jnp.int32) - 1

    small[1].wait()
    small[2].wait()
    scales = scales_t[...].astype(f32).T
    squares = None
    for b in range(scales.shape[1]):
        lanes = slice(128 * b, 128 * b + 128)
        q = (values[:, lanes].astype(f32) * scales[:, b : b + 1]).astype(bf16)
        q_ref[:, lanes] = q
        wide = q.astype(f32)
        squares = wide * wide if squares is None else squares + wide * wide
    squares_ref[...] = jnp.sum(squares.T, axis=0, keepdims=True)

    for j in range(count // 256):
        at = lax.broadcasted_iota(jnp.int32, (groups * slots, 256), 1) + 256 * j
        onehot_ref[:, 256 * j : 256 * j + 256] = (at == chosen).astype(f32).astype(bf16)
    for j, copy in enumerate(large):
        copy.wait()
        if j + 2 < len(large):
            large[j + 2].start()
        lanes = slice(step * j, step * j + step)
        out_ref[:, lanes] = jnp.dot(
            onehot_ref[...], cents_ref[j], preferred_element_type=f32
        ).astype(bf16)


def prepare(values, scales, ids, cents, slots):
    rows, width = values.shape
    groups = ids.shape[0]
    count = cents.shape[0]
    scales = scales.T
    step = 256
    return pl.pallas_call(
        functools.partial(prepare_kernel, slots, step),
        out_shape=(
            pltpu.VMEM((rows, width), bf16),
            pltpu.VMEM((1, rows), f32),
            pltpu.VMEM((groups * slots, width), bf16),
        ),
        in_specs=[HBM] * 4,
        out_specs=(VM, VM, VM),
        scratch_shapes=[
            pltpu.VMEM(values.shape, bf16),
            pltpu.VMEM(scales.shape, bf16),
            pltpu.VMEM(ids.shape, jnp.int32),
            pltpu.VMEM((width // step, count, step), bf16),
            pltpu.VMEM((groups * slots, count), bf16),
            pltpu.SemaphoreType.DMA((width // step + 3,)),
        ],
        cost_estimate=pl.CostEstimate(
            flops=2 * groups * slots * count * width, bytes_accessed=count * width * 2, transcendentals=0
        ),
        compiler_params=LIMIT,
        name="prepare",
    )(off_chip(values), off_chip(scales), off_chip(ids), off_chip(cents))


def residual_kernel(count, slots, ids_ref, fetched_ref, q_ref, out_ref):
    width, rows = out_ref.shape
    ids = ids_ref[pl.ds(lax.axis_index("cent"), 1), :]
    owner = lax.div(ids, count)
    across = jnp.broadcast_to(owner, (rows, rows))
    down = across.astype(f32).T.astype(jnp.int32)
    earlier = lax.broadcasted_iota(jnp.int32, (rows, rows), 0) < lax.broadcasted_iota(
        jnp.int32, (rows, rows), 1
    )
    rank = jnp.sum(jnp.where((across == down) & earlier, 1.0, 0.0), axis=0, keepdims=True)
    slot = owner * slots + rank.astype(jnp.int32)
    number = lax.broadcasted_iota(jnp.int32, (fetched_ref.shape[0], rows), 0)
    place = (number == slot).astype(f32).astype(bf16)
    for j in range(width // 128):
        lanes = slice(128 * j, 128 * j + 128)
        fetched = lax.dot_general(
            place, fetched_ref[:, lanes], (((0,), (0,)), ((), ())), preferred_element_type=f32
        )
        out_ref[lanes, :] = (q_ref[:, lanes].astype(f32) - fetched).T


def residuals(ids, fetched, q, count, slots):
    rows, width = q.shape
    return pl.pallas_call(
        functools.partial(residual_kernel, count, slots),
        out_shape=pltpu.VMEM((width, rows), f32),
        in_specs=[VM] * 3,
        out_specs=VM,
        cost_estimate=pl.CostEstimate(
            flops=2 * fetched.size * rows, bytes_accessed=fetched.size * 2 + rows * width * 6, transcendentals=0
        ),
        compiler_params=LIMIT,
        name="residuals",
    )(ids, on_chip(fetched), on_chip(q))


def nearest_kernel(step, ahead, blocks, mode, *refs):
    x_refs, refs = refs[:blocks], refs[blocks:]
    if mode == "again":
        cents_ref, squares_ref, out_ref = refs
        copies = []
    else:
        cents_hbm, out_ref, cents_ref, squares_ref, sems = refs
        half = step // 2
        copies = [
            pltpu.make_async_copy(cents_hbm.at[pl.ds(half * i, half), :], cents_ref.at[i], sems.at[i])
            for i in range(cents_ref.shape[0])
        ]
    for copy in copies[:ahead]:
        copy.start()
    best = [None] * (blocks // 2)
    for i in range(0, cents_ref.shape[0], 2):
        for k in (i, i + 1) if copies else ():
            copies[k].wait()
            if k + ahead < len(copies):
                copies[k + ahead].start()
        block = jnp.concatenate([cents_ref[i], cents_ref[i + 1]], axis=0)
        at = slice(step // 2 * i, step // 2 * i + step)
        if mode == "again":
            squares = squares_ref[at, :]
        else:
            total = None
            for b in range(block.shape[1] // 128):
                wide = block[:, 128 * b : 128 * b + 128].astype(f32)
                total = wide * wide if total is None else total + wide * wide
            squares = jnp.broadcast_to(jnp.sum(total, axis=1, keepdims=True), (step, 128))
            squares_ref[at, :] = squares
        squares = jnp.concatenate([squares, squares], axis=1)
        for j in range(len(best)):
            x = jnp.concatenate([x_refs[2 * j][...], x_refs[2 * j + 1][...]], axis=0)
            cross = lax.dot_general(block, x, (((1,), (1,)), ((), ())), preferred_element_type=f32)
            low = jnp.min(squares - 2.0 * cross, axis=0, keepdims=True)
            best[j] = low if best[j] is None else jnp.minimum(best[j], low)
    for j, low in enumerate(best):
        for k in range(2):
            out_ref[2 * j + k : 2 * j + k + 1, :] = low[:, 128 * k : 128 * k + 128]


def nearest(xs, cents, mode, kept=()):
    count, width = cents.shape
    rows = sum(x.shape[0] for x in xs)
    step = 512
    out = [pltpu.VMEM((rows // 128, 128), f32)]
    held = [pltpu.VMEM((2 * count // step, step // 2, width), bf16), pltpu.VMEM((count, 128), f32)]
    sems = [pltpu.SemaphoreType.DMA((2 * count // step,))]
    more = {
        "once": ([HBM], out, held + sems),
        "keep": ([HBM], out + held, sems),
        "again": ([VM, VM], out, []),
    }
    ins, outs, scratch = more[mode]
    result = pl.pallas_call(
        functools.partial(nearest_kernel, step, 3, len(xs), mode),
        out_shape=tuple(outs),
        in_specs=[VM] * len(xs) + ins,
        out_specs=tuple([VM] * len(outs)),
        scratch_shapes=scratch,
        cost_estimate=pl.CostEstimate(
            flops=2 * rows * count * width, bytes_accessed=count * width * 2 + rows * width * 2, transcendentals=0
        ),
        compiler_params=LIMIT,
        name="nearest",
    )(*[on_chip(x) for x in xs], *([on_chip(x) for x in kept] or [off_chip(cents)]))
    return result[0], result[1:]


def halves_of(x):
    high = x.astype(bf16)
    return high, (x - high.astype(f32)).astype(bf16)


def statistics_kernel(where, sub_ref, one_ref, two_ref, *refs):
    gap_refs, (mine_ref, theirs_ref) = refs[:-2], refs[-2:]
    groups, width, rows = sub_ref.shape
    words = 256
    high, low = [], []
    for g in range(groups):
        h, l = halves_of(sub_ref[g])
        high.append(h)
        low.append(l)
    ones = jnp.ones((16, groups * rows), bf16)
    left = jnp.concatenate([jnp.concatenate(high, axis=1), jnp.concatenate(low, axis=1), ones], axis=0)
    word = lax.broadcasted_iota(jnp.int32, (words, groups * rows), 0)
    core = lax.rem(lax.axis_index("cent"), 2)
    odd = core == 1

    def totals(codes_ref):
        hit = (word == codes_ref[...]).astype(f32).astype(bf16)
        out = lax.dot_general(left, hit, (((1,), (1,)), ((), ())), preferred_element_type=f32)
        return out[:width] + out[width : 2 * width], out[2 * width : 2 * width + 8]

    for at, codes_ref in enumerate((one_ref, two_ref)):
        total, count = totals(codes_ref)
        rows_at = slice(width * at, width * at + width)
        a, b = total[:, :128], total[:, 128:]
        mine_ref[rows_at, :] = jnp.where(odd, b, a)
        theirs_ref[rows_at, :] = jnp.where(odd, a, b)
        a, b = count[:4, :128], count[:4, 128:]
        count_at = slice(2 * width + 4 * at, 2 * width + 4 * at + 4)
        mine_ref[count_at, :] = jnp.where(odd, b, a)
        theirs_ref[count_at, :] = jnp.where(odd, a, b)
    for j in range(8):
        for out_ref, d in ((mine_ref, 2 * j), (theirs_ref, 2 * j + 1)):
            k, row = where[d]
            out_ref[STATS + j : STATS + j + 1, :] = gap_refs[k][row : row + 1, :]


def statistics(sub, codes_one, codes_two, lows, where):
    shape = pltpu.VMEM((PAY, 128), f32)
    return pl.pallas_call(
        functools.partial(statistics_kernel, where),
        out_shape=(shape, shape),
        in_specs=[VM] * (3 + len(lows)),
        out_specs=(VM, VM),
        cost_estimate=pl.CostEstimate(
            flops=2 * 2 * sub.size * 512, bytes_accessed=sub.size * 4, transcendentals=0
        ),
        compiler_params=LIMIT,
        name="statistics",
    )(on_chip(sub), codes_one, codes_two, *[on_chip(x) for x in lows])


def join_kernel(shift, a_ref, b_ref, out_ref):
    out_ref[:STATS, :] = a_ref[:STATS, :] + b_ref[:STATS, :]
    keep = PAY - STATS - shift
    out_ref[STATS:PAY, :] = a_ref[STATS:PAY, :]
    out_ref[STATS : STATS + keep, :] = jnp.minimum(
        a_ref[STATS : STATS + keep, :], b_ref[STATS + shift : PAY, :]
    )


def join(a, b, shift):
    return pl.pallas_call(
        functools.partial(join_kernel, shift),
        out_shape=pltpu.VMEM(a.shape, f32),
        in_specs=[VM, VM],
        out_specs=VM,
        cost_estimate=pl.CostEstimate(flops=a.size, bytes_accessed=a.size * 12, transcendentals=0),
        compiler_params=LIMIT,
        name="join",
    )(on_chip(a), on_chip(b))


def update_kernel(width, a_ref, b_ref, c_ref, d_ref, init_ref, squares_ref, books_ref, gap_ref):
    core = lax.rem(lax.axis_index("cent"), 2)
    total = (a_ref[:STATS, :] + b_ref[:STATS, :]) + (c_ref[:STATS, :] + d_ref[:STATS, :])
    init = jnp.where(core == 1, init_ref[:, 128:], init_ref[:, :128])
    count_one = total[2 * width : 2 * width + 1]
    count_two = total[2 * width + 4 : 2 * width + 5]
    one = (total[:width] + prior_weight * init) / (count_one + prior_weight)
    two = (total[width : 2 * width] + prior_weight * one) / (count_two + prior_weight)
    books_ref[:width, :] = one
    books_ref[width:, :] = two
    low = jnp.minimum(
        jnp.minimum(a_ref[STATS : STATS + 1, :], b_ref[STATS + 1 : STATS + 2, :]),
        jnp.minimum(c_ref[STATS + 2 : STATS + 3, :], d_ref[STATS + 3 : STATS + 4, :]),
    )
    gap_ref[...] = (low + squares_ref[...]) * (1.0 / 1024.0)


def update(parts, init, squares):
    width = init.shape[0]
    return pl.pallas_call(
        functools.partial(update_kernel, width),
        out_shape=(
            pltpu.VMEM((2 * width, 128), f32),
            jax.ShapeDtypeStruct((1, 128), f32),
        ),
        in_specs=[VM] * 6,
        out_specs=(VM, VM),
        cost_estimate=pl.CostEstimate(flops=8 * STATS * 128, bytes_accessed=5 * PAY * 512, transcendentals=0),
        compiler_params=LIMIT,
        name="update",
    )(*[on_chip(x) for x in parts], init, on_chip(squares))


def distortion_kernel(sub_ref, two_ref, mine_ref, theirs_ref, one_out_ref, two_out_ref, out_ref):
    groups, width, rows = sub_ref.shape
    odd = lax.rem(lax.axis_index("cent"), 2) == 1
    mine, theirs = mine_ref[...], theirs_ref[...]
    books = jnp.concatenate([jnp.where(odd, theirs, mine), jnp.where(odd, mine, theirs)], axis=1)
    one_out_ref[...] = books[:width]
    book = books[width:]
    two_out_ref[...] = book
    high, low = halves_of(book)
    left = jnp.concatenate([high, low], axis=0)
    words = book.shape[1]
    for g in range(0, groups, 2):
        lanes = slice(rows * g, rows * g + 2 * rows)
        word = lax.broadcasted_iota(jnp.int32, (words, 2 * rows), 0)
        hit = (word == two_ref[:, lanes]).astype(f32).astype(bf16)
        rebuilt = jnp.dot(left, hit, preferred_element_type=f32)
        rebuilt = rebuilt[:width] + rebuilt[width:]
        sub = jnp.concatenate([sub_ref[g], sub_ref[g + 1]], axis=1)
        miss = sub - rebuilt
        out_ref[:, lanes] = jnp.sum(miss * miss, axis=0, keepdims=True) * (1.0 / width)


def distortions(sub, codes_two, mine, theirs):
    groups, width, rows = sub.shape
    return pl.pallas_call(
        distortion_kernel,
        out_shape=(
            jax.ShapeDtypeStruct((width, 256), f32),
            jax.ShapeDtypeStruct((width, 256), f32),
            jax.ShapeDtypeStruct((1, groups * rows), f32),
        ),
        in_specs=[VM] * 4,
        out_specs=(VM, VM, VM),
        cost_estimate=pl.CostEstimate(
            flops=4 * sub.size * 256, bytes_accessed=sub.size * 4, transcendentals=0
        ),
        compiler_params=LIMIT,
        name="distortion",
    )(on_chip(sub), codes_two, on_chip(mine), on_chip(theirs))


def swap(x, offset):
    return lax.ppermute(x, "cent", [(i, i ^ offset) for i in range(16)])


def step(emb_values, emb_scales, coarse_ids, centroids, codes_one, codes_two, codebook_init):
    own_rows, width = emb_values.shape
    count = centroids.shape[0]
    sub_width = codebook_init.shape[2]
    peers = coarse_ids.shape[0]
    slots = 16

    q, row_squares, sent = prepare(emb_values, emb_scales, coarse_ids, centroids, slots)

    core = 1

    blocks = {0: q, 2: swap(q, 2), 6: swap(q, 6), 8: swap(q, 8)}
    blocks[core] = swap(q, core)

    fetched = lax.all_to_all(sent.reshape(peers, slots, width), "cent", 0, 0)
    fetched = fetched.reshape(peers * slots, width)

    blocks[14] = swap(blocks[8], 6)
    blocks[10] = swap(blocks[8], 2)
    blocks[4] = swap(blocks[6], 2)
    blocks[12] = swap(blocks[14], 2)
    for d in (2, 6, 8, 4, 10, 14, 12):
        blocks[d ^ core] = swap(blocks[d], core)

    orders = ((0, 1, 2, 3), (6, 7, 8, 9, 4, 5, 10, 11, 14, 15), (12, 13))
    lows, kept = [], ()
    for order, mode in zip(orders, ("once", "keep", "again")):
        low, kept = nearest([blocks[d] for d in order], centroids, mode, kept)
        lows.append(low)
    where = {d: (k, j) for k, order in enumerate(orders) for j, d in enumerate(order)}

    residual = residuals(coarse_ids, fetched, q, count, slots)
    stacked = residual.reshape(width // sub_width, sub_width, own_rows)
    sub = lax.all_to_all(stacked, "rows", 0, 0)

    mine, theirs = statistics(sub, codes_one, codes_two, lows, where)
    mine = join(mine, swap(theirs, 1), 0)
    mine = join(mine, swap(mine, 8), 4)
    parts = [mine] + [swap(mine, d) for d in (2, 4, 6)]
    init = codebook_init[0].T
    books, coarse_gap = update(parts, init, row_squares)
    book_one, book_two, distortion = distortions(sub, codes_two, books, swap(books, 1))
    return coarse_gap[0], book_one.T[None], book_two.T[None], distortion


def solution(mesh):
    placed = (
        P(("cent", "rows"), None),
        P(("cent", "rows"), None),
        P(None, "rows"),
        P("cent", None),
        P("rows", "cent"),
        P("rows", "cent"),
        P("rows", None, None),
    )
    return jax.shard_map(
        step,
        mesh=mesh,
        in_specs=placed,
        out_specs=(
            P(("cent", "rows")),
            P("rows", None, None),
            P("rows", None, None),
            P("rows", "cent"),
        ),
        check_vma=False,
    )
```

```python
import functools

import jax
import jax.numpy as jnp
from jax import lax
from jax.experimental import pallas as pl
from jax.experimental.pallas import tpu as pltpu
from jax.sharding import PartitionSpec as P


bf16 = jnp.bfloat16
f32 = jnp.float32
prior_weight = 8.0
VM = pl.BlockSpec(memory_space=pltpu.VMEM)
HBM = pl.BlockSpec(memory_space=pltpu.HBM)
LIMIT = pltpu.CompilerParams(vmem_limit_bytes=16 << 20)


def off_chip(x):
    return pltpu.with_memory_space_constraint(x, pltpu.HBM)


def on_chip(x):
    return pltpu.with_memory_space_constraint(x, pltpu.VMEM)


STATS = 136
PAY = 144


def prepare_kernel(
    slots, step, values_hbm, scales_hbm, ids_hbm, cents_hbm, q_ref, squares_ref, out_ref,
    values, scales_t, ids_ref, cents_ref, onehot_ref, sems,
):
    count, width = cents_hbm.shape
    groups, rows = ids_ref.shape
    small = (
        pltpu.make_async_copy(ids_hbm, ids_ref, sems.at[0]),
        pltpu.make_async_copy(scales_hbm, scales_t, sems.at[1]),
        pltpu.make_async_copy(values_hbm, values, sems.at[2]),
    )
    large = [
        pltpu.make_async_copy(cents_hbm.at[:, pl.ds(step * j, step)], cents_ref.at[j], sems.at[3 + j])
        for j in range(width // step)
    ]
    for copy in small:
        copy.start()
    for copy in large:
        copy.start()

    small[0].wait()
    local = ids_ref[...] - lax.axis_index("cent") * count
    mine = (local >= 0) & (local < count)
    before = lax.broadcasted_iota(jnp.int32, (rows, rows), 0) <= lax.broadcasted_iota(
        jnp.int32, (rows, rows), 1
    )
    rank = jnp.dot(
        mine.astype(f32).astype(bf16), before.astype(f32).astype(bf16), preferred_element_type=f32
    )
    slot = jnp.where(mine, rank - 1.0, -1.0)
    local = local.astype(f32)
    spread_slot = jnp.concatenate(
        [jnp.broadcast_to(slot[g : g + 1], (slots, rows)) for g in range(groups)], axis=0
    )
    spread_local = jnp.concatenate(
        [jnp.broadcast_to(local[g : g + 1], (slots, rows)) for g in range(groups)], axis=0
    )
    number = lax.rem(lax.broadcasted_iota(jnp.int32, (groups * slots, rows), 0), slots).astype(f32)
    chosen = jnp.sum(jnp.where(spread_slot == number, spread_local + 1.0, 0.0), axis=1, keepdims=True)
    chosen = chosen.astype(jnp.int32) - 1

    small[1].wait()
    small[2].wait()
    scales = scales_t[...].astype(f32).T
    squares = None
    for b in range(scales.shape[1]):
        lanes = slice(128 * b, 128 * b + 128)
        q = (values[:, lanes].astype(f32) * scales[:, b : b + 1]).astype(bf16)
        q_ref[:, lanes] = q
        wide = q.astype(f32)
        squares = wide * wide if squares is None else squares + wide * wide
    squares_ref[...] = jnp.sum(squares.T, axis=0, keepdims=True)

    for j in range(count // 256):
        at = lax.broadcasted_iota(jnp.int32, (groups * slots, 256), 1) + 256 * j
        onehot_ref[:, 256 * j : 256 * j + 256] = (at == chosen).astype(f32).astype(bf16)
    for j, copy in enumerate(large):
        copy.wait()
        lanes = slice(step * j, step * j + step)
        out_ref[:, lanes] = jnp.dot(
            onehot_ref[...], cents_ref[j], preferred_element_type=f32
        ).astype(bf16)


def prepare(values, scales, ids, cents, slots):
    rows, width = values.shape
    groups = ids.shape[0]
    count = cents.shape[0]
    scales = scales.T
    step = 256
    return pl.pallas_call(
        functools.partial(prepare_kernel, slots, step),
        out_shape=(
            pltpu.VMEM((rows, width), bf16),
            pltpu.VMEM((1, rows), f32),
            pltpu.VMEM((groups * slots, width), bf16),
        ),
        in_specs=[HBM] * 4,
        out_specs=(VM, VM, VM),
        scratch_shapes=[
            pltpu.VMEM(values.shape, bf16),
            pltpu.VMEM(scales.shape, bf16),
            pltpu.VMEM(ids.shape, jnp.int32),
            pltpu.VMEM((width // step, count, step), bf16),
            pltpu.VMEM((groups * slots, count), bf16),
            pltpu.SemaphoreType.DMA((width // step + 3,)),
        ],
        cost_estimate=pl.CostEstimate(
            flops=2 * groups * slots * count * width, bytes_accessed=count * width * 2, transcendentals=0
        ),
        compiler_params=LIMIT,
        name="prepare",
    )(off_chip(values), off_chip(scales), off_chip(ids), off_chip(cents))


def residual_kernel(count, slots, ids_ref, fetched_ref, q_ref, out_ref):
    width, rows = out_ref.shape
    ids = ids_ref[pl.ds(lax.axis_index("cent"), 1), :]
    owner = lax.div(ids, count)
    across = jnp.broadcast_to(owner, (rows, rows))
    down = across.astype(f32).T.astype(jnp.int32)
    earlier = lax.broadcasted_iota(jnp.int32, (rows, rows), 0) < lax.broadcasted_iota(
        jnp.int32, (rows, rows), 1
    )
    rank = jnp.sum(jnp.where((across == down) & earlier, 1.0, 0.0), axis=0, keepdims=True)
    slot = owner * slots + rank.astype(jnp.int32)
    number = lax.broadcasted_iota(jnp.int32, (fetched_ref.shape[0], rows), 0)
    place = (number == slot).astype(f32).astype(bf16)
    for j in range(width // 128):
        lanes = slice(128 * j, 128 * j + 128)
        fetched = lax.dot_general(
            place, fetched_ref[:, lanes], (((0,), (0,)), ((), ())), preferred_element_type=f32
        )
        out_ref[lanes, :] = (q_ref[:, lanes].astype(f32) - fetched).T


def residuals(ids, fetched, q, count, slots):
    rows, width = q.shape
    return pl.pallas_call(
        functools.partial(residual_kernel, count, slots),
        out_shape=pltpu.VMEM((width, rows), f32),
        in_specs=[VM] * 3,
        out_specs=VM,
        cost_estimate=pl.CostEstimate(
            flops=2 * fetched.size * rows, bytes_accessed=fetched.size * 2 + rows * width * 6, transcendentals=0
        ),
        compiler_params=LIMIT,
        name="residuals",
    )(ids, on_chip(fetched), on_chip(q))


def nearest_kernel(step, ahead, blocks, mode, *refs):
    x_refs, refs = refs[:blocks], refs[blocks:]
    if mode == "again":
        cents_ref, squares_ref, out_ref = refs
        copies = []
    else:
        cents_hbm, out_ref, cents_ref, squares_ref, sems = refs
        half = step // 2
        copies = [
            pltpu.make_async_copy(cents_hbm.at[pl.ds(half * i, half), :], cents_ref.at[i], sems.at[i])
            for i in range(cents_ref.shape[0])
        ]
    for copy in copies[:ahead]:
        copy.start()
    best = [None] * (blocks // 2)
    for i in range(0, cents_ref.shape[0], 2):
        for k in (i, i + 1) if copies else ():
            copies[k].wait()
            if k + ahead < len(copies):
                copies[k + ahead].start()
        block = jnp.concatenate([cents_ref[i], cents_ref[i + 1]], axis=0)
        at = slice(step // 2 * i, step // 2 * i + step)
        if mode == "again":
            squares = squares_ref[at, :]
        else:
            total = None
            for b in range(block.shape[1] // 128):
                wide = block[:, 128 * b : 128 * b + 128].astype(f32)
                total = wide * wide if total is None else total + wide * wide
            squares = jnp.broadcast_to(jnp.sum(total, axis=1, keepdims=True), (step, 128))
            squares_ref[at, :] = squares
        squares = jnp.concatenate([squares, squares], axis=1)
        for j in range(len(best)):
            x = jnp.concatenate([x_refs[2 * j][...], x_refs[2 * j + 1][...]], axis=0)
            cross = lax.dot_general(block, x, (((1,), (1,)), ((), ())), preferred_element_type=f32)
            low = jnp.min(squares - 2.0 * cross, axis=0, keepdims=True)
            best[j] = low if best[j] is None else jnp.minimum(best[j], low)
    for j, low in enumerate(best):
        for k in range(2):
            out_ref[2 * j + k : 2 * j + k + 1, :] = low[:, 128 * k : 128 * k + 128]


def nearest(xs, cents, mode, kept=()):
    count, width = cents.shape
    rows = sum(x.shape[0] for x in xs)
    step = 512
    out = [pltpu.VMEM((rows // 128, 128), f32)]
    held = [pltpu.VMEM((2 * count // step, step // 2, width), bf16), pltpu.VMEM((count, 128), f32)]
    sems = [pltpu.SemaphoreType.DMA((2 * count // step,))]
    more = {
        "keep": ([HBM], out + held, sems),
        "again": ([VM, VM], out, []),
    }
    ins, outs, scratch = more[mode]
    result = pl.pallas_call(
        functools.partial(nearest_kernel, step, 3, len(xs), mode),
        out_shape=tuple(outs),
        in_specs=[VM] * len(xs) + ins,
        out_specs=tuple([VM] * len(outs)),
        scratch_shapes=scratch,
        cost_estimate=pl.CostEstimate(
            flops=2 * rows * count * width, bytes_accessed=count * width * 2 + rows * width * 2, transcendentals=0
        ),
        compiler_params=LIMIT,
        name="nearest",
    )(*[on_chip(x) for x in xs], *([on_chip(x) for x in kept] or [off_chip(cents)]))
    return result[0], result[1:]


def halves_of(x):
    high = x.astype(bf16)
    return high, (x - high.astype(f32)).astype(bf16)


def statistics_kernel(where, sub_ref, one_ref, two_ref, *refs):
    gap_refs, (mine_ref, theirs_ref) = refs[:-2], refs[-2:]
    groups, width, rows = sub_ref.shape
    words = 256
    high, low = [], []
    for g in range(groups):
        h, l = halves_of(sub_ref[g])
        high.append(h)
        low.append(l)
    ones = jnp.ones((16, groups * rows), bf16)
    left = jnp.concatenate([jnp.concatenate(high, axis=1), jnp.concatenate(low, axis=1), ones], axis=0)
    word = lax.broadcasted_iota(jnp.int32, (words, groups * rows), 0)
    core = lax.rem(lax.axis_index("cent"), 2)
    odd = core == 1

    def totals(codes_ref):
        hit = (word == codes_ref[...]).astype(f32).astype(bf16)
        out = lax.dot_general(left, hit, (((1,), (1,)), ((), ())), preferred_element_type=f32)
        return out[:width] + out[width : 2 * width], out[2 * width : 2 * width + 8]

    for at, codes_ref in enumerate((one_ref, two_ref)):
        total, count = totals(codes_ref)
        rows_at = slice(width * at, width * at + width)
        a, b = total[:, :128], total[:, 128:]
        mine_ref[rows_at, :] = jnp.where(odd, b, a)
        theirs_ref[rows_at, :] = jnp.where(odd, a, b)
        a, b = count[:4, :128], count[:4, 128:]
        count_at = slice(2 * width + 4 * at, 2 * width + 4 * at + 4)
        mine_ref[count_at, :] = jnp.where(odd, b, a)
        theirs_ref[count_at, :] = jnp.where(odd, a, b)
    for j in range(8):
        for out_ref, d in ((mine_ref, 2 * j), (theirs_ref, 2 * j + 1)):
            k, row = where[d]
            out_ref[STATS + j : STATS + j + 1, :] = gap_refs[k][row : row + 1, :]


def statistics(sub, codes_one, codes_two, lows, where):
    shape = pltpu.VMEM((PAY, 128), f32)
    return pl.pallas_call(
        functools.partial(statistics_kernel, where),
        out_shape=(shape, shape),
        in_specs=[VM] * (3 + len(lows)),
        out_specs=(VM, VM),
        cost_estimate=pl.CostEstimate(
            flops=2 * 2 * sub.size * 512, bytes_accessed=sub.size * 4, transcendentals=0
        ),
        compiler_params=LIMIT,
        name="statistics",
    )(on_chip(sub), codes_one, codes_two, *[on_chip(x) for x in lows])


def join_kernel(shift, a_ref, b_ref, out_ref):
    out_ref[:STATS, :] = a_ref[:STATS, :] + b_ref[:STATS, :]
    keep = PAY - STATS - shift
    out_ref[STATS:PAY, :] = a_ref[STATS:PAY, :]
    out_ref[STATS : STATS + keep, :] = jnp.minimum(
        a_ref[STATS : STATS + keep, :], b_ref[STATS + shift : PAY, :]
    )


def join(a, b, shift):
    return pl.pallas_call(
        functools.partial(join_kernel, shift),
        out_shape=pltpu.VMEM(a.shape, f32),
        in_specs=[VM, VM],
        out_specs=VM,
        cost_estimate=pl.CostEstimate(flops=a.size, bytes_accessed=a.size * 12, transcendentals=0),
        compiler_params=LIMIT,
        name="join",
    )(on_chip(a), on_chip(b))


def update_kernel(width, a_ref, b_ref, c_ref, d_ref, init_ref, squares_ref, books_ref, gap_ref):
    core = lax.rem(lax.axis_index("cent"), 2)
    total = (a_ref[:STATS, :] + b_ref[:STATS, :]) + (c_ref[:STATS, :] + d_ref[:STATS, :])
    init = jnp.where(core == 1, init_ref[:, 128:], init_ref[:, :128])
    count_one = total[2 * width : 2 * width + 1]
    count_two = total[2 * width + 4 : 2 * width + 5]
    one = (total[:width] + prior_weight * init) / (count_one + prior_weight)
    two = (total[width : 2 * width] + prior_weight * one) / (count_two + prior_weight)
    books_ref[:width, :] = one
    books_ref[width:, :] = two
    low = jnp.minimum(
        jnp.minimum(a_ref[STATS : STATS + 1, :], b_ref[STATS + 1 : STATS + 2, :]),
        jnp.minimum(c_ref[STATS + 2 : STATS + 3, :], d_ref[STATS + 3 : STATS + 4, :]),
    )
    gap_ref[...] = (low + squares_ref[...]) * (1.0 / 1024.0)


def update(parts, init, squares):
    width = init.shape[0]
    return pl.pallas_call(
        functools.partial(update_kernel, width),
        out_shape=(
            pltpu.VMEM((2 * width, 128), f32),
            jax.ShapeDtypeStruct((1, 128), f32),
        ),
        in_specs=[VM] * 6,
        out_specs=(VM, VM),
        cost_estimate=pl.CostEstimate(flops=8 * STATS * 128, bytes_accessed=5 * PAY * 512, transcendentals=0),
        compiler_params=LIMIT,
        name="update",
    )(*[on_chip(x) for x in parts], init, on_chip(squares))


def distortion_kernel(sub_ref, two_ref, mine_ref, theirs_ref, one_out_ref, two_out_ref, out_ref):
    groups, width, rows = sub_ref.shape
    odd = lax.rem(lax.axis_index("cent"), 2) == 1
    mine, theirs = mine_ref[...], theirs_ref[...]
    books = jnp.concatenate([jnp.where(odd, theirs, mine), jnp.where(odd, mine, theirs)], axis=1)
    one_out_ref[...] = books[:width]
    book = books[width:]
    two_out_ref[...] = book
    high, low = halves_of(book)
    left = jnp.concatenate([high, low], axis=0)
    words = book.shape[1]
    for g in range(0, groups, 2):
        lanes = slice(rows * g, rows * g + 2 * rows)
        word = lax.broadcasted_iota(jnp.int32, (words, 2 * rows), 0)
        hit = (word == two_ref[:, lanes]).astype(f32).astype(bf16)
        rebuilt = jnp.dot(left, hit, preferred_element_type=f32)
        rebuilt = rebuilt[:width] + rebuilt[width:]
        sub = jnp.concatenate([sub_ref[g], sub_ref[g + 1]], axis=1)
        miss = sub - rebuilt
        out_ref[:, lanes] = jnp.sum(miss * miss, axis=0, keepdims=True) * (1.0 / width)


def distortions(sub, codes_two, mine, theirs):
    groups, width, rows = sub.shape
    return pl.pallas_call(
        distortion_kernel,
        out_shape=(
            jax.ShapeDtypeStruct((width, 256), f32),
            jax.ShapeDtypeStruct((width, 256), f32),
            jax.ShapeDtypeStruct((1, groups * rows), f32),
        ),
        in_specs=[VM] * 4,
        out_specs=(VM, VM, VM),
        cost_estimate=pl.CostEstimate(
            flops=4 * sub.size * 256, bytes_accessed=sub.size * 4, transcendentals=0
        ),
        compiler_params=LIMIT,
        name="distortion",
    )(on_chip(sub), codes_two, on_chip(mine), on_chip(theirs))


def swap(x, offset):
    return lax.ppermute(x, "cent", [(i, i ^ offset) for i in range(16)])


def step(emb_values, emb_scales, coarse_ids, centroids, codes_one, codes_two, codebook_init):
    own_rows, width = emb_values.shape
    count = centroids.shape[0]
    sub_width = codebook_init.shape[2]
    peers = coarse_ids.shape[0]
    slots = 16

    q, row_squares, sent = prepare(emb_values, emb_scales, coarse_ids, centroids, slots)

    core = 1

    blocks = {0: q, 2: swap(q, 2), 6: swap(q, 6), 8: swap(q, 8)}
    blocks[core] = swap(q, core)

    fetched = lax.all_to_all(sent.reshape(peers, slots, width), "cent", 0, 0)
    fetched = fetched.reshape(peers * slots, width)

    blocks[14] = swap(blocks[8], 6)
    blocks[10] = swap(blocks[8], 2)
    blocks[4] = swap(blocks[6], 2)
    blocks[12] = swap(blocks[14], 2)
    for d in (2, 6, 8, 4, 10, 14, 12):
        blocks[d ^ core] = swap(blocks[d], core)

    orders = ((0, 1, 2, 3, 6, 7, 8, 9), (4, 5, 10, 11, 14, 15, 12, 13))
    lows, kept = [], ()
    for order, mode in zip(orders, ("keep", "again")):
        low, kept = nearest([blocks[d] for d in order], centroids, mode, kept)
        lows.append(low)
    where = {d: (k, j) for k, order in enumerate(orders) for j, d in enumerate(order)}

    residual = residuals(coarse_ids, fetched, q, count, slots)
    stacked = residual.reshape(width // sub_width, sub_width, own_rows)
    sub = lax.all_to_all(stacked, "rows", 0, 0)

    mine, theirs = statistics(sub, codes_one, codes_two, lows, where)
    mine = join(mine, swap(theirs, 1), 0)
    mine = join(mine, swap(mine, 8), 4)
    parts = [mine] + [swap(mine, d) for d in (2, 4, 6)]
    init = codebook_init[0].T
    books, coarse_gap = update(parts, init, row_squares)
    book_one, book_two, distortion = distortions(sub, codes_two, books, swap(books, 1))
    return coarse_gap[0], book_one.T[None], book_two.T[None], distortion


def solution(mesh):
    placed = (
        P(("cent", "rows"), None),
        P(("cent", "rows"), None),
        P(None, "rows"),
        P("cent", None),
        P("rows", "cent"),
        P("rows", "cent"),
        P("rows", None, None),
    )
    return jax.shard_map(
        step,
        mesh=mesh,
        in_specs=placed,
        out_specs=(
            P(("cent", "rows")),
            P("rows", None, None),
            P("rows", None, None),
            P("rows", "cent"),
        ),
        check_vma=False,
    )
```

```python
import functools

import jax
import jax.numpy as jnp
from jax import lax
from jax.experimental import pallas as pl
from jax.experimental.pallas import tpu as pltpu
from jax.sharding import PartitionSpec as P


bf16 = jnp.bfloat16
f32 = jnp.float32
prior_weight = 8.0
VM = pl.BlockSpec(memory_space=pltpu.VMEM)
HBM = pl.BlockSpec(memory_space=pltpu.HBM)
LIMIT = pltpu.CompilerParams(vmem_limit_bytes=16 << 20)


def off_chip(x):
    return pltpu.with_memory_space_constraint(x, pltpu.HBM)


def on_chip(x):
    return pltpu.with_memory_space_constraint(x, pltpu.VMEM)


STATS = 136
PAY = 144


def prepare_kernel(
    slots, step, values_hbm, scales_hbm, ids_hbm, cents_hbm, q_ref, squares_ref, out_ref,
    values, scales_t, ids_ref, cents_ref, onehot_ref, sems,
):
    count, width = cents_hbm.shape
    groups, rows = ids_ref.shape
    small = (
        pltpu.make_async_copy(ids_hbm, ids_ref, sems.at[0]),
        pltpu.make_async_copy(scales_hbm, scales_t, sems.at[1]),
        pltpu.make_async_copy(values_hbm, values, sems.at[2]),
    )
    large = [
        pltpu.make_async_copy(cents_hbm.at[:, pl.ds(step * j, step)], cents_ref.at[j], sems.at[3 + j])
        for j in range(width // step)
    ]
    for copy in small:
        copy.start()
    for copy in large:
        copy.start()

    small[0].wait()
    local = ids_ref[...] - lax.axis_index("cent") * count
    mine = (local >= 0) & (local < count)
    before = lax.broadcasted_iota(jnp.int32, (rows, rows), 0) <= lax.broadcasted_iota(
        jnp.int32, (rows, rows), 1
    )
    rank = jnp.dot(
        mine.astype(f32).astype(bf16), before.astype(f32).astype(bf16), preferred_element_type=f32
    )
    slot = jnp.where(mine, rank - 1.0, -1.0)
    local = local.astype(f32)
    spread_slot = jnp.concatenate(
        [jnp.broadcast_to(slot[g : g + 1], (slots, rows)) for g in range(groups)], axis=0
    )
    spread_local = jnp.concatenate(
        [jnp.broadcast_to(local[g : g + 1], (slots, rows)) for g in range(groups)], axis=0
    )
    number = lax.rem(lax.broadcasted_iota(jnp.int32, (groups * slots, rows), 0), slots).astype(f32)
    chosen = jnp.sum(jnp.where(spread_slot == number, spread_local + 1.0, 0.0), axis=1, keepdims=True)
    chosen = chosen.astype(jnp.int32) - 1

    small[1].wait()
    small[2].wait()
    scales = scales_t[...].astype(f32).T
    squares = None
    for b in range(scales.shape[1]):
        lanes = slice(128 * b, 128 * b + 128)
        q = (values[:, lanes].astype(f32) * scales[:, b : b + 1]).astype(bf16)
        q_ref[:, lanes] = q
        wide = q.astype(f32)
        squares = wide * wide if squares is None else squares + wide * wide
    squares_ref[...] = jnp.sum(squares.T, axis=0, keepdims=True)

    for j in range(count // 256):
        at = lax.broadcasted_iota(jnp.int32, (groups * slots, 256), 1) + 256 * j
        onehot_ref[:, 256 * j : 256 * j + 256] = (at == chosen).astype(f32).astype(bf16)
    for j, copy in enumerate(large):
        copy.wait()
        lanes = slice(step * j, step * j + step)
        out_ref[:, lanes] = jnp.dot(
            onehot_ref[...], cents_ref[j], preferred_element_type=f32
        ).astype(bf16)


def prepare(values, scales, ids, cents, slots):
    rows, width = values.shape
    groups = ids.shape[0]
    count = cents.shape[0]
    scales = scales.T
    step = 256
    return pl.pallas_call(
        functools.partial(prepare_kernel, slots, step),
        out_shape=(
            pltpu.VMEM((rows, width), bf16),
            pltpu.VMEM((1, rows), f32),
            pltpu.VMEM((groups * slots, width), bf16),
        ),
        in_specs=[HBM] * 4,
        out_specs=(VM, VM, VM),
        scratch_shapes=[
            pltpu.VMEM(values.shape, bf16),
            pltpu.VMEM(scales.shape, bf16),
            pltpu.VMEM(ids.shape, jnp.int32),
            pltpu.VMEM((width // step, count, step), bf16),
            pltpu.VMEM((groups * slots, count), bf16),
            pltpu.SemaphoreType.DMA((width // step + 3,)),
        ],
        cost_estimate=pl.CostEstimate(
            flops=2 * groups * slots * count * width, bytes_accessed=count * width * 2, transcendentals=0
        ),
        compiler_params=LIMIT,
        name="prepare",
    )(off_chip(values), off_chip(scales), off_chip(ids), off_chip(cents))


def pack(out_ref, first, residual, sub_width):
    half = sub_width // 2
    for k in range(residual.shape[0] // sub_width):
        part = residual[sub_width * k : sub_width * (k + 1)]
        most = jnp.maximum(jnp.max(jnp.abs(part), axis=0, keepdims=True), 1e-30)
        power = jnp.floor(jnp.log2(most)) + 1.0
        coded = jnp.clip(jnp.round(part * jnp.exp2(15.0 - power)), -32767.0, 32767.0).astype(jnp.int32)
        word = lax.shift_left(coded[:half], 16) | (coded[half:] & 0xFFFF)
        out_ref[first + k, :half, :] = word
        out_ref[first + k, half:, :] = jnp.broadcast_to(power.astype(jnp.int32), (8, part.shape[1]))


def unpack(words):
    half = words.shape[0] - 8
    unit = jnp.exp2(words[half : half + 1].astype(f32) - 15.0)
    words = words[:half]
    high = lax.shift_right_arithmetic(words, 16)
    low = lax.shift_right_arithmetic(lax.shift_left(words, 16), 16)
    return jnp.concatenate([high, low], axis=0).astype(f32) * unit


def residual_kernel(count, slots, sub_width, ids_ref, fetched_ref, q_ref, out_ref):
    rows, width = q_ref.shape
    ids = ids_ref[pl.ds(lax.axis_index("cent"), 1), :]
    owner = lax.div(ids, count)
    across = jnp.broadcast_to(owner, (rows, rows))
    down = across.astype(f32).T.astype(jnp.int32)
    earlier = lax.broadcasted_iota(jnp.int32, (rows, rows), 0) < lax.broadcasted_iota(
        jnp.int32, (rows, rows), 1
    )
    rank = jnp.sum(jnp.where((across == down) & earlier, 1.0, 0.0), axis=0, keepdims=True)
    slot = owner * slots + rank.astype(jnp.int32)
    number = lax.broadcasted_iota(jnp.int32, (fetched_ref.shape[0], rows), 0)
    place = (number == slot).astype(f32).astype(bf16)
    for j in range(width // 128):
        lanes = slice(128 * j, 128 * j + 128)
        fetched = lax.dot_general(
            place, fetched_ref[:, lanes], (((0,), (0,)), ((), ())), preferred_element_type=f32
        )
        pack(out_ref, 2 * j, (q_ref[:, lanes].astype(f32) - fetched).T, sub_width)


def residuals(ids, fetched, q, count, slots, sub_width):
    rows, width = q.shape
    return pl.pallas_call(
        functools.partial(residual_kernel, count, slots, sub_width),
        out_shape=pltpu.VMEM((width // sub_width, sub_width // 2 + 8, rows), jnp.int32),
        in_specs=[VM] * 3,
        out_specs=VM,
        cost_estimate=pl.CostEstimate(
            flops=2 * fetched.size * rows, bytes_accessed=fetched.size * 2 + rows * width * 6, transcendentals=0
        ),
        compiler_params=LIMIT,
        name="residuals",
    )(ids, on_chip(fetched), on_chip(q))


def nearest_kernel(step, ahead, blocks, mode, *refs):
    x_refs, refs = refs[:blocks], refs[blocks:]
    if mode == "again":
        cents_ref, squares_ref, out_ref = refs
        copies = []
    else:
        cents_hbm, out_ref, cents_ref, squares_ref, sems = refs
        half = step // 2
        copies = [
            pltpu.make_async_copy(cents_hbm.at[pl.ds(half * i, half), :], cents_ref.at[i], sems.at[i])
            for i in range(cents_ref.shape[0])
        ]
    for copy in copies[:ahead]:
        copy.start()
    best = [None] * (blocks // 2)
    for i in range(0, cents_ref.shape[0], 2):
        for k in (i, i + 1) if copies else ():
            copies[k].wait()
            if k + ahead < len(copies):
                copies[k + ahead].start()
        block = jnp.concatenate([cents_ref[i], cents_ref[i + 1]], axis=0)
        at = slice(step // 2 * i, step // 2 * i + step)
        if mode == "again":
            squares = squares_ref[at, :]
        else:
            total = None
            for b in range(block.shape[1] // 128):
                wide = block[:, 128 * b : 128 * b + 128].astype(f32)
                total = wide * wide if total is None else total + wide * wide
            squares = jnp.broadcast_to(jnp.sum(total, axis=1, keepdims=True), (step, 128))
            squares_ref[at, :] = squares
        squares = jnp.concatenate([squares, squares], axis=1)
        for j in range(len(best)):
            x = jnp.concatenate([x_refs[2 * j][...], x_refs[2 * j + 1][...]], axis=0)
            cross = lax.dot_general(block, x, (((1,), (1,)), ((), ())), preferred_element_type=f32)
            low = jnp.min(squares - 2.0 * cross, axis=0, keepdims=True)
            best[j] = low if best[j] is None else jnp.minimum(best[j], low)
    for j, low in enumerate(best):
        for k in range(2):
            out_ref[2 * j + k : 2 * j + k + 1, :] = low[:, 128 * k : 128 * k + 128]


def nearest(xs, cents, mode, kept=()):
    count, width = cents.shape
    rows = sum(x.shape[0] for x in xs)
    step = 512
    out = [pltpu.VMEM((rows // 128, 128), f32)]
    held = [pltpu.VMEM((2 * count // step, step // 2, width), bf16), pltpu.VMEM((count, 128), f32)]
    sems = [pltpu.SemaphoreType.DMA((2 * count // step,))]
    more = {
        "once": ([HBM], out, held + sems),
        "keep": ([HBM], out + held, sems),
        "again": ([VM, VM], out, []),
    }
    ins, outs, scratch = more[mode]
    result = pl.pallas_call(
        functools.partial(nearest_kernel, step, 3, len(xs), mode),
        out_shape=tuple(outs),
        in_specs=[VM] * len(xs) + ins,
        out_specs=tuple([VM] * len(outs)),
        scratch_shapes=scratch,
        cost_estimate=pl.CostEstimate(
            flops=2 * rows * count * width, bytes_accessed=count * width * 2 + rows * width * 2, transcendentals=0
        ),
        compiler_params=LIMIT,
        name="nearest",
    )(*[on_chip(x) for x in xs], *([on_chip(x) for x in kept] or [off_chip(cents)]))
    return result[0], result[1:]


def halves_of(x):
    high = x.astype(bf16)
    return high, (x - high.astype(f32)).astype(bf16)


def statistics_kernel(where, coded_ref, one_ref, two_ref, *refs):
    gap_refs, (mine_ref, theirs_ref, sub_out_ref) = refs[:-3], refs[-3:]
    groups, width, rows = sub_out_ref.shape
    words = 256
    high, low = [], []
    for g in range(groups):
        sub = unpack(coded_ref[g])
        sub_out_ref[g] = sub
        h, l = halves_of(sub)
        high.append(h)
        low.append(l)
    ones = jnp.ones((16, groups * rows), bf16)
    left = jnp.concatenate([jnp.concatenate(high, axis=1), jnp.concatenate(low, axis=1), ones], axis=0)
    word = lax.broadcasted_iota(jnp.int32, (words, groups * rows), 0)
    core = lax.rem(lax.axis_index("cent"), 2)
    odd = core == 1

    def totals(codes_ref):
        hit = (word == codes_ref[...]).astype(f32).astype(bf16)
        out = lax.dot_general(left, hit, (((1,), (1,)), ((), ())), preferred_element_type=f32)
        return out[:width] + out[width : 2 * width], out[2 * width : 2 * width + 8]

    for at, codes_ref in enumerate((one_ref, two_ref)):
        total, count = totals(codes_ref)
        rows_at = slice(width * at, width * at + width)
        a, b = total[:, :128], total[:, 128:]
        mine_ref[rows_at, :] = jnp.where(odd, b, a)
        theirs_ref[rows_at, :] = jnp.where(odd, a, b)
        a, b = count[:4, :128], count[:4, 128:]
        count_at = slice(2 * width + 4 * at, 2 * width + 4 * at + 4)
        mine_ref[count_at, :] = jnp.where(odd, b, a)
        theirs_ref[count_at, :] = jnp.where(odd, a, b)
    for j in range(8):
        for out_ref, d in ((mine_ref, 2 * j), (theirs_ref, 2 * j + 1)):
            k, row = where[d]
            out_ref[STATS + j : STATS + j + 1, :] = gap_refs[k][row : row + 1, :]


def statistics(coded, codes_one, codes_two, lows, where):
    groups, words, rows = coded.shape
    sub = jax.ShapeDtypeStruct((groups, 2 * (words - 8), rows), f32)
    shape = pltpu.VMEM((PAY, 128), f32)
    return pl.pallas_call(
        functools.partial(statistics_kernel, where),
        out_shape=(shape, shape, pltpu.VMEM(sub.shape, f32)),
        in_specs=[VM] * (3 + len(lows)),
        out_specs=(VM, VM, VM),
        cost_estimate=pl.CostEstimate(
            flops=2 * 2 * sub.size * 512, bytes_accessed=sub.size * 4, transcendentals=0
        ),
        compiler_params=LIMIT,
        name="statistics",
    )(on_chip(coded), codes_one, codes_two, *[on_chip(x) for x in lows])


def join_kernel(shift, a_ref, b_ref, out_ref):
    out_ref[:STATS, :] = a_ref[:STATS, :] + b_ref[:STATS, :]
    keep = PAY - STATS - shift
    out_ref[STATS:PAY, :] = a_ref[STATS:PAY, :]
    out_ref[STATS : STATS + keep, :] = jnp.minimum(
        a_ref[STATS : STATS + keep, :], b_ref[STATS + shift : PAY, :]
    )


def join(a, b, shift):
    return pl.pallas_call(
        functools.partial(join_kernel, shift),
        out_shape=pltpu.VMEM(a.shape, f32),
        in_specs=[VM, VM],
        out_specs=VM,
        cost_estimate=pl.CostEstimate(flops=a.size, bytes_accessed=a.size * 12, transcendentals=0),
        compiler_params=LIMIT,
        name="join",
    )(on_chip(a), on_chip(b))


def update_kernel(width, a_ref, b_ref, c_ref, d_ref, init_ref, squares_ref, books_ref, gap_ref):
    core = lax.rem(lax.axis_index("cent"), 2)
    total = (a_ref[:STATS, :] + b_ref[:STATS, :]) + (c_ref[:STATS, :] + d_ref[:STATS, :])
    init = jnp.where(core == 1, init_ref[:, 128:], init_ref[:, :128])
    count_one = total[2 * width : 2 * width + 1]
    count_two = total[2 * width + 4 : 2 * width + 5]
    one = (total[:width] + prior_weight * init) / (count_one + prior_weight)
    two = (total[width : 2 * width] + prior_weight * one) / (count_two + prior_weight)
    books_ref[:width, :] = one
    books_ref[width:, :] = two
    low = jnp.minimum(
        jnp.minimum(a_ref[STATS : STATS + 1, :], b_ref[STATS + 1 : STATS + 2, :]),
        jnp.minimum(c_ref[STATS + 2 : STATS + 3, :], d_ref[STATS + 3 : STATS + 4, :]),
    )
    gap_ref[...] = (low + squares_ref[...]) * (1.0 / 1024.0)


def update(parts, init, squares):
    width = init.shape[0]
    return pl.pallas_call(
        functools.partial(update_kernel, width),
        out_shape=(
            pltpu.VMEM((2 * width, 128), f32),
            jax.ShapeDtypeStruct((1, 128), f32),
        ),
        in_specs=[VM] * 6,
        out_specs=(VM, VM),
        cost_estimate=pl.CostEstimate(flops=8 * STATS * 128, bytes_accessed=5 * PAY * 512, transcendentals=0),
        compiler_params=LIMIT,
        name="update",
    )(*[on_chip(x) for x in parts], init, on_chip(squares))


def distortion_kernel(sub_ref, two_ref, mine_ref, theirs_ref, one_out_ref, two_out_ref, out_ref):
    groups, width, rows = sub_ref.shape
    odd = lax.rem(lax.axis_index("cent"), 2) == 1
    mine, theirs = mine_ref[...], theirs_ref[...]
    books = jnp.concatenate([jnp.where(odd, theirs, mine), jnp.where(odd, mine, theirs)], axis=1)
    one_out_ref[...] = books[:width]
    book = books[width:]
    two_out_ref[...] = book
    high, low = halves_of(book)
    left = jnp.concatenate([high, low], axis=0)
    words = book.shape[1]
    for g in range(0, groups, 2):
        lanes = slice(rows * g, rows * g + 2 * rows)
        word = lax.broadcasted_iota(jnp.int32, (words, 2 * rows), 0)
        hit = (word == two_ref[:, lanes]).astype(f32).astype(bf16)
        rebuilt = jnp.dot(left, hit, preferred_element_type=f32)
        rebuilt = rebuilt[:width] + rebuilt[width:]
        sub = jnp.concatenate([sub_ref[g], sub_ref[g + 1]], axis=1)
        miss = sub - rebuilt
        out_ref[:, lanes] = jnp.sum(miss * miss, axis=0, keepdims=True) * (1.0 / width)


def distortions(sub, codes_two, mine, theirs):
    groups, width, rows = sub.shape
    return pl.pallas_call(
        distortion_kernel,
        out_shape=(
            jax.ShapeDtypeStruct((width, 256), f32),
            jax.ShapeDtypeStruct((width, 256), f32),
            jax.ShapeDtypeStruct((1, groups * rows), f32),
        ),
        in_specs=[VM] * 4,
        out_specs=(VM, VM, VM),
        cost_estimate=pl.CostEstimate(
            flops=4 * sub.size * 256, bytes_accessed=sub.size * 4, transcendentals=0
        ),
        compiler_params=LIMIT,
        name="distortion",
    )(on_chip(sub), codes_two, on_chip(mine), on_chip(theirs))


def swap(x, offset):
    return lax.ppermute(x, "cent", [(i, i ^ offset) for i in range(16)])


def step(emb_values, emb_scales, coarse_ids, centroids, codes_one, codes_two, codebook_init):
    _, width = emb_values.shape
    count = centroids.shape[0]
    sub_width = codebook_init.shape[2]
    peers = coarse_ids.shape[0]
    slots = 16

    q, row_squares, sent = prepare(emb_values, emb_scales, coarse_ids, centroids, slots)

    core = 1

    blocks = {0: q, 2: swap(q, 2), 6: swap(q, 6), 8: swap(q, 8)}
    blocks[core] = swap(q, core)

    fetched = lax.all_to_all(sent.reshape(peers, slots, width), "cent", 0, 0)
    fetched = fetched.reshape(peers * slots, width)

    blocks[14] = swap(blocks[8], 6)
    blocks[10] = swap(blocks[8], 2)
    blocks[4] = swap(blocks[6], 2)
    blocks[12] = swap(blocks[10], 6)
    for d in (2, 6, 8, 4, 10, 14, 12):
        blocks[d ^ core] = swap(blocks[d], core)

    orders = ((0, 1, 8, 9), (2, 3, 6, 7, 10, 11, 14, 15), (4, 5, 12, 13))
    lows, kept = [], ()
    for order, mode in zip(orders, ("once", "keep", "again")):
        low, kept = nearest([blocks[d] for d in order], centroids, mode, kept)
        lows.append(low)
    where = {d: (k, j) for k, order in enumerate(orders) for j, d in enumerate(order)}

    coded = residuals(coarse_ids, fetched, q, count, slots, sub_width)
    coded = lax.all_to_all(coded, "rows", 0, 0)

    mine, theirs, sub = statistics(coded, codes_one, codes_two, lows, where)
    mine = join(mine, swap(theirs, 1), 0)
    mine = join(mine, swap(mine, 8), 4)
    parts = [mine] + [swap(mine, d) for d in (2, 4, 6)]
    init = codebook_init[0].T
    books, coarse_gap = update(parts, init, row_squares)
    book_one, book_two, distortion = distortions(sub, codes_two, books, swap(books, 1))
    return coarse_gap[0], book_one.T[None], book_two.T[None], distortion


def solution(mesh):
    placed = (
        P(("cent", "rows"), None),
        P(("cent", "rows"), None),
        P(None, "rows"),
        P("cent", None),
        P("rows", "cent"),
        P("rows", "cent"),
        P("rows", None, None),
    )
    return jax.shard_map(
        step,
        mesh=mesh,
        in_specs=placed,
        out_specs=(
            P(("cent", "rows")),
            P("rows", None, None),
            P("rows", None, None),
            P("rows", "cent"),
        ),
        check_vma=False,
    )
```

```python
import functools

import jax
import jax.numpy as jnp
from jax import lax
from jax.experimental import pallas as pl
from jax.experimental.pallas import tpu as pltpu
from jax.sharding import PartitionSpec as P


bf16 = jnp.bfloat16
f32 = jnp.float32
prior_weight = 8.0
VM = pl.BlockSpec(memory_space=pltpu.VMEM)
HBM = pl.BlockSpec(memory_space=pltpu.HBM)
LIMIT = pltpu.CompilerParams(vmem_limit_bytes=16 << 20)


def off_chip(x):
    return pltpu.with_memory_space_constraint(x, pltpu.HBM)


def on_chip(x):
    return pltpu.with_memory_space_constraint(x, pltpu.VMEM)


STATS = 136
PAY = 144


def prepare_kernel(
    slots, step, values_hbm, scales_hbm, ids_hbm, cents_hbm, q_ref, squares_ref, out_ref,
    values, scales_t, ids_ref, cents_ref, onehot_ref, sems,
):
    count, width = cents_hbm.shape
    groups, rows = ids_ref.shape
    small = (
        pltpu.make_async_copy(ids_hbm, ids_ref, sems.at[0]),
        pltpu.make_async_copy(scales_hbm, scales_t, sems.at[1]),
        pltpu.make_async_copy(values_hbm, values, sems.at[2]),
    )
    large = [
        pltpu.make_async_copy(cents_hbm.at[:, pl.ds(step * j, step)], cents_ref.at[j], sems.at[3 + j])
        for j in range(width // step)
    ]
    for copy in small:
        copy.start()
    for copy in large:
        copy.start()

    small[0].wait()
    local = ids_ref[...] - lax.axis_index("cent") * count
    mine = (local >= 0) & (local < count)
    before = lax.broadcasted_iota(jnp.int32, (rows, rows), 0) <= lax.broadcasted_iota(
        jnp.int32, (rows, rows), 1
    )
    rank = jnp.dot(
        mine.astype(f32).astype(bf16), before.astype(f32).astype(bf16), preferred_element_type=f32
    )
    slot = jnp.where(mine, rank - 1.0, -1.0)
    local = local.astype(f32)
    spread_slot = jnp.concatenate(
        [jnp.broadcast_to(slot[g : g + 1], (slots, rows)) for g in range(groups)], axis=0
    )
    spread_local = jnp.concatenate(
        [jnp.broadcast_to(local[g : g + 1], (slots, rows)) for g in range(groups)], axis=0
    )
    number = lax.rem(lax.broadcasted_iota(jnp.int32, (groups * slots, rows), 0), slots).astype(f32)
    chosen = jnp.sum(jnp.where(spread_slot == number, spread_local + 1.0, 0.0), axis=1, keepdims=True)
    chosen = chosen.astype(jnp.int32) - 1

    small[1].wait()
    small[2].wait()
    scales = scales_t[...].astype(f32).T
    squares = None
    for b in range(scales.shape[1]):
        lanes = slice(128 * b, 128 * b + 128)
        q = (values[:, lanes].astype(f32) * scales[:, b : b + 1]).astype(bf16)
        q_ref[:, lanes] = q
        wide = q.astype(f32)
        squares = wide * wide if squares is None else squares + wide * wide
    squares_ref[...] = jnp.sum(squares.T, axis=0, keepdims=True)

    for j in range(count // 256):
        at = lax.broadcasted_iota(jnp.int32, (groups * slots, 256), 1) + 256 * j
        onehot_ref[:, 256 * j : 256 * j + 256] = (at == chosen).astype(f32).astype(bf16)
    for j, copy in enumerate(large):
        copy.wait()
        lanes = slice(step * j, step * j + step)
        out_ref[:, lanes] = jnp.dot(
            onehot_ref[...], cents_ref[j], preferred_element_type=f32
        ).astype(bf16)


def prepare(values, scales, ids, cents, slots):
    rows, width = values.shape
    groups = ids.shape[0]
    count = cents.shape[0]
    scales = scales.T
    step = 256
    return pl.pallas_call(
        functools.partial(prepare_kernel, slots, step),
        out_shape=(
            pltpu.VMEM((rows, width), bf16),
            pltpu.VMEM((1, rows), f32),
            pltpu.VMEM((groups * slots, width), bf16),
        ),
        in_specs=[HBM] * 4,
        out_specs=(VM, VM, VM),
        scratch_shapes=[
            pltpu.VMEM(values.shape, bf16),
            pltpu.VMEM(scales.shape, bf16),
            pltpu.VMEM(ids.shape, jnp.int32),
            pltpu.VMEM((width // step, count, step), bf16),
            pltpu.VMEM((groups * slots, count), bf16),
            pltpu.SemaphoreType.DMA((width // step + 3,)),
        ],
        cost_estimate=pl.CostEstimate(
            flops=2 * groups * slots * count * width, bytes_accessed=count * width * 2, transcendentals=0
        ),
        compiler_params=LIMIT,
        name="prepare",
    )(off_chip(values), off_chip(scales), off_chip(ids), off_chip(cents))


def pack(out_ref, first, residual, sub_width):
    half = sub_width // 2
    for k in range(residual.shape[0] // sub_width):
        part = residual[sub_width * k : sub_width * (k + 1)]
        most = jnp.maximum(jnp.max(jnp.abs(part), axis=0, keepdims=True), 1e-30)
        power = jnp.floor(jnp.log2(most)) + 1.0
        coded = jnp.clip(jnp.round(part * jnp.exp2(15.0 - power)), -32767.0, 32767.0).astype(jnp.int32)
        word = lax.shift_left(coded[:half], 16) | (coded[half:] & 0xFFFF)
        out_ref[first + k, :half, :] = word
        out_ref[first + k, half:, :] = jnp.broadcast_to(power.astype(jnp.int32), (8, part.shape[1]))


def unpack(words):
    half = words.shape[0] - 8
    unit = jnp.exp2(words[half : half + 1].astype(f32) - 15.0)
    words = words[:half]
    high = lax.shift_right_arithmetic(words, 16)
    low = lax.shift_right_arithmetic(lax.shift_left(words, 16), 16)
    return jnp.concatenate([high, low], axis=0).astype(f32) * unit


def residual_kernel(count, slots, sub_width, ids_ref, fetched_ref, q_ref, out_ref):
    rows, width = q_ref.shape
    ids = ids_ref[pl.ds(lax.axis_index("cent"), 1), :]
    owner = lax.div(ids, count)
    across = jnp.broadcast_to(owner, (rows, rows))
    down = across.astype(f32).T.astype(jnp.int32)
    earlier = lax.broadcasted_iota(jnp.int32, (rows, rows), 0) < lax.broadcasted_iota(
        jnp.int32, (rows, rows), 1
    )
    rank = jnp.sum(jnp.where((across == down) & earlier, 1.0, 0.0), axis=0, keepdims=True)
    slot = owner * slots + rank.astype(jnp.int32)
    number = lax.broadcasted_iota(jnp.int32, (fetched_ref.shape[0], rows), 0)
    place = (number == slot).astype(f32).astype(bf16)
    for j in range(width // 128):
        lanes = slice(128 * j, 128 * j + 128)
        fetched = lax.dot_general(
            place, fetched_ref[:, lanes], (((0,), (0,)), ((), ())), preferred_element_type=f32
        )
        pack(out_ref, 2 * j, (q_ref[:, lanes].astype(f32) - fetched).T, sub_width)


def residuals(ids, fetched, q, count, slots, sub_width):
    rows, width = q.shape
    return pl.pallas_call(
        functools.partial(residual_kernel, count, slots, sub_width),
        out_shape=pltpu.VMEM((width // sub_width, sub_width // 2 + 8, rows), jnp.int32),
        in_specs=[VM] * 3,
        out_specs=VM,
        cost_estimate=pl.CostEstimate(
            flops=2 * fetched.size * rows, bytes_accessed=fetched.size * 2 + rows * width * 6, transcendentals=0
        ),
        compiler_params=LIMIT,
        name="residuals",
    )(ids, on_chip(fetched), on_chip(q))


def nearest_kernel(step, ahead, blocks, mode, *refs):
    x_refs, refs = refs[:blocks], refs[blocks:]
    if mode == "again":
        cents_ref, squares_ref, out_ref = refs
        copies = []
    else:
        cents_hbm, out_ref, cents_ref, squares_ref, sems = refs
        half = step // 2
        copies = [
            pltpu.make_async_copy(cents_hbm.at[pl.ds(half * i, half), :], cents_ref.at[i], sems.at[i])
            for i in range(cents_ref.shape[0])
        ]
    for copy in copies[:ahead]:
        copy.start()
    best = [None] * (blocks // 2)
    for i in range(0, cents_ref.shape[0], 2):
        for k in (i, i + 1) if copies else ():
            copies[k].wait()
            if k + ahead < len(copies):
                copies[k + ahead].start()
        block = jnp.concatenate([cents_ref[i], cents_ref[i + 1]], axis=0)
        at = slice(step // 2 * i, step // 2 * i + step)
        if mode == "again":
            squares = squares_ref[at, :]
        else:
            total = None
            for b in range(block.shape[1] // 128):
                wide = block[:, 128 * b : 128 * b + 128].astype(f32)
                total = wide * wide if total is None else total + wide * wide
            squares = jnp.broadcast_to(jnp.sum(total, axis=1, keepdims=True), (step, 128))
            squares_ref[at, :] = squares
        squares = jnp.concatenate([squares, squares], axis=1)
        for j in range(len(best)):
            x = jnp.concatenate([x_refs[2 * j][...], x_refs[2 * j + 1][...]], axis=0)
            cross = lax.dot_general(block, x, (((1,), (1,)), ((), ())), preferred_element_type=f32)
            low = jnp.min(squares - 2.0 * cross, axis=0, keepdims=True)
            best[j] = low if best[j] is None else jnp.minimum(best[j], low)
    for j, low in enumerate(best):
        for k in range(2):
            out_ref[2 * j + k : 2 * j + k + 1, :] = low[:, 128 * k : 128 * k + 128]


def nearest(xs, cents, mode, kept=()):
    count, width = cents.shape
    rows = sum(x.shape[0] for x in xs)
    step = 512
    out = [pltpu.VMEM((rows // 128, 128), f32)]
    held = [pltpu.VMEM((2 * count // step, step // 2, width), bf16), pltpu.VMEM((count, 128), f32)]
    sems = [pltpu.SemaphoreType.DMA((2 * count // step,))]
    more = {
        "once": ([HBM], out, held + sems),
        "keep": ([HBM], out + held, sems),
        "again": ([VM, VM], out, []),
    }
    ins, outs, scratch = more[mode]
    result = pl.pallas_call(
        functools.partial(nearest_kernel, step, 3, len(xs), mode),
        out_shape=tuple(outs),
        in_specs=[VM] * len(xs) + ins,
        out_specs=tuple([VM] * len(outs)),
        scratch_shapes=scratch,
        cost_estimate=pl.CostEstimate(
            flops=2 * rows * count * width, bytes_accessed=count * width * 2 + rows * width * 2, transcendentals=0
        ),
        compiler_params=LIMIT,
        name="nearest",
    )(*[on_chip(x) for x in xs], *([on_chip(x) for x in kept] or [off_chip(cents)]))
    return result[0], result[1:]


def halves_of(x):
    high = x.astype(bf16)
    return high, (x - high.astype(f32)).astype(bf16)


def statistics_kernel(where, coded_ref, one_ref, two_ref, *refs):
    gap_refs, (mine_ref, theirs_ref, sub_out_ref) = refs[:-3], refs[-3:]
    groups, width, rows = sub_out_ref.shape
    words = 256
    high, low = [], []
    for g in range(groups):
        sub = unpack(coded_ref[g])
        sub_out_ref[g] = sub
        h, l = halves_of(sub)
        high.append(h)
        low.append(l)
    ones = jnp.ones((16, groups * rows), bf16)
    left = jnp.concatenate([jnp.concatenate(high, axis=1), jnp.concatenate(low, axis=1), ones], axis=0)
    word = lax.broadcasted_iota(jnp.int32, (words, groups * rows), 0)
    core = lax.rem(lax.axis_index("cent"), 2)
    odd = core == 1

    def totals(codes_ref):
        hit = (word == codes_ref[...]).astype(f32).astype(bf16)
        out = lax.dot_general(left, hit, (((1,), (1,)), ((), ())), preferred_element_type=f32)
        return out[:width] + out[width : 2 * width], out[2 * width : 2 * width + 8]

    for at, codes_ref in enumerate((one_ref, two_ref)):
        total, count = totals(codes_ref)
        rows_at = slice(width * at, width * at + width)
        a, b = total[:, :128], total[:, 128:]
        mine_ref[rows_at, :] = jnp.where(odd, b, a)
        theirs_ref[rows_at, :] = jnp.where(odd, a, b)
        a, b = count[:4, :128], count[:4, 128:]
        count_at = slice(2 * width + 4 * at, 2 * width + 4 * at + 4)
        mine_ref[count_at, :] = jnp.where(odd, b, a)
        theirs_ref[count_at, :] = jnp.where(odd, a, b)
    for j in range(8):
        for out_ref, d in ((mine_ref, 2 * j), (theirs_ref, 2 * j + 1)):
            k, row = where[d]
            out_ref[STATS + j : STATS + j + 1, :] = gap_refs[k][row : row + 1, :]


def statistics(coded, codes_one, codes_two, lows, where):
    groups, words, rows = coded.shape
    sub = jax.ShapeDtypeStruct((groups, 2 * (words - 8), rows), f32)
    shape = pltpu.VMEM((PAY, 128), f32)
    return pl.pallas_call(
        functools.partial(statistics_kernel, where),
        out_shape=(shape, shape, pltpu.VMEM(sub.shape, f32)),
        in_specs=[VM] * (3 + len(lows)),
        out_specs=(VM, VM, VM),
        cost_estimate=pl.CostEstimate(
            flops=2 * 2 * sub.size * 512, bytes_accessed=sub.size * 4, transcendentals=0
        ),
        compiler_params=LIMIT,
        name="statistics",
    )(on_chip(coded), codes_one, codes_two, *[on_chip(x) for x in lows])


def join_kernel(lows, a_ref, b_ref, out_ref):
    out_ref[:STATS, :] = a_ref[:STATS, :] + b_ref[:STATS, :]
    out_ref[STATS:PAY, :] = a_ref[STATS:PAY, :]
    for mine, theirs in lows:
        at, of = STATS + mine, STATS + theirs
        out_ref[at : at + 1, :] = jnp.minimum(a_ref[at : at + 1, :], b_ref[of : of + 1, :])


def join(a, b, lows):
    return pl.pallas_call(
        functools.partial(join_kernel, lows),
        out_shape=pltpu.VMEM(a.shape, f32),
        in_specs=[VM, VM],
        out_specs=VM,
        cost_estimate=pl.CostEstimate(flops=a.size, bytes_accessed=a.size * 12, transcendentals=0),
        compiler_params=LIMIT,
        name="join",
    )(on_chip(a), on_chip(b))


def update_kernel(width, a_ref, b_ref, init_ref, squares_ref, books_ref, gap_ref):
    core = lax.rem(lax.axis_index("cent"), 2)
    total = a_ref[:STATS, :] + b_ref[:STATS, :]
    init = jnp.where(core == 1, init_ref[:, 128:], init_ref[:, :128])
    count_one = total[2 * width : 2 * width + 1]
    count_two = total[2 * width + 4 : 2 * width + 5]
    one = (total[:width] + prior_weight * init) / (count_one + prior_weight)
    two = (total[width : 2 * width] + prior_weight * one) / (count_two + prior_weight)
    books_ref[:width, :] = one
    books_ref[width:, :] = two
    low = jnp.minimum(a_ref[STATS : STATS + 1, :], b_ref[STATS + 3 : STATS + 4, :])
    gap_ref[...] = (low + squares_ref[...]) * (1.0 / 1024.0)


def update(parts, init, squares):
    width = init.shape[0]
    return pl.pallas_call(
        functools.partial(update_kernel, width),
        out_shape=(
            pltpu.VMEM((2 * width, 128), f32),
            jax.ShapeDtypeStruct((1, 128), f32),
        ),
        in_specs=[VM] * 4,
        out_specs=(VM, VM),
        cost_estimate=pl.CostEstimate(flops=8 * STATS * 128, bytes_accessed=5 * PAY * 512, transcendentals=0),
        compiler_params=LIMIT,
        name="update",
    )(*[on_chip(x) for x in parts], init, on_chip(squares))


def distortion_kernel(sub_ref, two_ref, mine_ref, theirs_ref, one_out_ref, two_out_ref, out_ref):
    groups, width, rows = sub_ref.shape
    odd = lax.rem(lax.axis_index("cent"), 2) == 1
    mine, theirs = mine_ref[...], theirs_ref[...]
    books = jnp.concatenate([jnp.where(odd, theirs, mine), jnp.where(odd, mine, theirs)], axis=1)
    one_out_ref[...] = books[:width]
    book = books[width:]
    two_out_ref[...] = book
    high, low = halves_of(book)
    left = jnp.concatenate([high, low], axis=0)
    words = book.shape[1]
    for g in range(0, groups, 2):
        lanes = slice(rows * g, rows * g + 2 * rows)
        word = lax.broadcasted_iota(jnp.int32, (words, 2 * rows), 0)
        hit = (word == two_ref[:, lanes]).astype(f32).astype(bf16)
        rebuilt = jnp.dot(left, hit, preferred_element_type=f32)
        rebuilt = rebuilt[:width] + rebuilt[width:]
        sub = jnp.concatenate([sub_ref[g], sub_ref[g + 1]], axis=1)
        miss = sub - rebuilt
        out_ref[:, lanes] = jnp.sum(miss * miss, axis=0, keepdims=True) * (1.0 / width)


def distortions(sub, codes_two, mine, theirs):
    groups, width, rows = sub.shape
    return pl.pallas_call(
        distortion_kernel,
        out_shape=(
            jax.ShapeDtypeStruct((width, 256), f32),
            jax.ShapeDtypeStruct((width, 256), f32),
            jax.ShapeDtypeStruct((1, groups * rows), f32),
        ),
        in_specs=[VM] * 4,
        out_specs=(VM, VM, VM),
        cost_estimate=pl.CostEstimate(
            flops=4 * sub.size * 256, bytes_accessed=sub.size * 4, transcendentals=0
        ),
        compiler_params=LIMIT,
        name="distortion",
    )(on_chip(sub), codes_two, on_chip(mine), on_chip(theirs))


def swap(x, offset):
    return lax.ppermute(x, "cent", [(i, i ^ offset) for i in range(16)])


def step(emb_values, emb_scales, coarse_ids, centroids, codes_one, codes_two, codebook_init):
    _, width = emb_values.shape
    count = centroids.shape[0]
    sub_width = codebook_init.shape[2]
    peers = coarse_ids.shape[0]
    slots = 16

    q, row_squares, sent = prepare(emb_values, emb_scales, coarse_ids, centroids, slots)

    core = 1

    blocks = {0: q, 2: swap(q, 2), 6: swap(q, 6), 8: swap(q, 8)}
    blocks[core] = swap(q, core)

    fetched = lax.all_to_all(sent.reshape(peers, slots, width), "cent", 0, 0)
    fetched = fetched.reshape(peers * slots, width)

    blocks[14] = swap(blocks[8], 6)
    blocks[10] = swap(blocks[8], 2)
    blocks[4] = swap(blocks[6], 2)
    blocks[12] = swap(blocks[10], 6)
    for d in (2, 6, 8, 4, 10, 14, 12):
        blocks[d ^ core] = swap(blocks[d], core)

    orders = ((0, 1, 8, 9), (2, 3, 6, 7, 10, 11, 14, 15), (4, 5, 12, 13))
    lows, kept = [], ()
    for order, mode in zip(orders, ("once", "keep", "again")):
        low, kept = nearest([blocks[d] for d in order], centroids, mode, kept)
        lows.append(low)
    where = {d: (k, j) for k, order in enumerate(orders) for j, d in enumerate(order)}

    coded = residuals(coarse_ids, fetched, q, count, slots, sub_width)
    coded = lax.all_to_all(coded, "rows", 0, 0)

    mine, theirs, sub = statistics(coded, codes_one, codes_two, lows, where)
    mine = join(mine, swap(theirs, 1), [(i, i) for i in range(8)])
    mine = join(mine, swap(mine, 8), [(i, i + 4) for i in range(4)])
    mine = join(mine, swap(mine, 2), [(0, 1), (3, 2)])
    parts = [mine, swap(mine, 6)]
    init = codebook_init[0].T
    books, coarse_gap = update(parts, init, row_squares)
    book_one, book_two, distortion = distortions(sub, codes_two, books, swap(books, 1))
    return coarse_gap[0], book_one.T[None], book_two.T[None], distortion


def solution(mesh):
    placed = (
        P(("cent", "rows"), None),
        P(("cent", "rows"), None),
        P(None, "rows"),
        P("cent", None),
        P("rows", "cent"),
        P("rows", "cent"),
        P("rows", None, None),
    )
    return jax.shard_map(
        step,
        mesh=mesh,
        in_specs=placed,
        out_specs=(
            P(("cent", "rows")),
            P("rows", None, None),
            P("rows", None, None),
            P("rows", "cent"),
        ),
        check_vma=False,
    )
```

```python
import functools

import jax
import jax.numpy as jnp
from jax import lax
from jax.experimental import pallas as pl
from jax.experimental.pallas import tpu as pltpu
from jax.sharding import PartitionSpec as P


bf16 = jnp.bfloat16
f32 = jnp.float32
prior_weight = 8.0
VM = pl.BlockSpec(memory_space=pltpu.VMEM)
HBM = pl.BlockSpec(memory_space=pltpu.HBM)
LIMIT = pltpu.CompilerParams(vmem_limit_bytes=16 << 20)


def off_chip(x):
    return pltpu.with_memory_space_constraint(x, pltpu.HBM)


def on_chip(x):
    return pltpu.with_memory_space_constraint(x, pltpu.VMEM)


STATS = 136
PAY = 144


def prepare_kernel(
    slots, step, values_hbm, scales_hbm, ids_hbm, cents_hbm, q_ref, squares_ref, out_ref,
    values, scales_t, ids_ref, cents_ref, onehot_ref, sems,
):
    count, width = cents_hbm.shape
    groups, rows = ids_ref.shape
    small = (
        pltpu.make_async_copy(ids_hbm, ids_ref, sems.at[0]),
        pltpu.make_async_copy(scales_hbm, scales_t, sems.at[1]),
        pltpu.make_async_copy(values_hbm, values, sems.at[2]),
    )
    large = [
        pltpu.make_async_copy(cents_hbm.at[:, pl.ds(step * j, step)], cents_ref.at[j], sems.at[3 + j])
        for j in range(width // step)
    ]
    for copy in small:
        copy.start()
    for copy in large:
        copy.start()

    small[0].wait()
    local = ids_ref[...] - lax.axis_index("cent") * count
    mine = (local >= 0) & (local < count)
    before = lax.broadcasted_iota(jnp.int32, (rows, rows), 0) <= lax.broadcasted_iota(
        jnp.int32, (rows, rows), 1
    )
    rank = jnp.dot(
        mine.astype(f32).astype(bf16), before.astype(f32).astype(bf16), preferred_element_type=f32
    )
    slot = jnp.where(mine, rank - 1.0, -1.0)
    local = local.astype(f32)
    spread_slot = jnp.concatenate(
        [jnp.broadcast_to(slot[g : g + 1], (slots, rows)) for g in range(groups)], axis=0
    )
    spread_local = jnp.concatenate(
        [jnp.broadcast_to(local[g : g + 1], (slots, rows)) for g in range(groups)], axis=0
    )
    number = lax.rem(lax.broadcasted_iota(jnp.int32, (groups * slots, rows), 0), slots).astype(f32)
    chosen = jnp.sum(jnp.where(spread_slot == number, spread_local + 1.0, 0.0), axis=1, keepdims=True)
    chosen = chosen.astype(jnp.int32) - 1

    small[1].wait()
    small[2].wait()
    scales = scales_t[...].astype(f32).T
    squares = None
    for b in range(scales.shape[1]):
        lanes = slice(128 * b, 128 * b + 128)
        q = (values[:, lanes].astype(f32) * scales[:, b : b + 1]).astype(bf16)
        q_ref[:, lanes] = q
        wide = q.astype(f32)
        squares = wide * wide if squares is None else squares + wide * wide
    squares_ref[...] = jnp.sum(squares.T, axis=0, keepdims=True)

    for j in range(count // 256):
        at = lax.broadcasted_iota(jnp.int32, (groups * slots, 256), 1) + 256 * j
        onehot_ref[:, 256 * j : 256 * j + 256] = (at == chosen).astype(f32).astype(bf16)
    for j, copy in enumerate(large):
        copy.wait()
        lanes = slice(step * j, step * j + step)
        out_ref[:, lanes] = jnp.dot(
            onehot_ref[...], cents_ref[j], preferred_element_type=f32
        ).astype(bf16)


def prepare(values, scales, ids, cents, slots):
    rows, width = values.shape
    groups = ids.shape[0]
    count = cents.shape[0]
    scales = scales.T
    step = 256
    return pl.pallas_call(
        functools.partial(prepare_kernel, slots, step),
        out_shape=(
            pltpu.VMEM((rows, width), bf16),
            pltpu.VMEM((1, rows), f32),
            pltpu.VMEM((groups * slots, width), bf16),
        ),
        in_specs=[HBM] * 4,
        out_specs=(VM, VM, VM),
        scratch_shapes=[
            pltpu.VMEM(values.shape, bf16),
            pltpu.VMEM(scales.shape, bf16),
            pltpu.VMEM(ids.shape, jnp.int32),
            pltpu.VMEM((width // step, count, step), bf16),
            pltpu.VMEM((groups * slots, count), bf16),
            pltpu.SemaphoreType.DMA((width // step + 3,)),
        ],
        cost_estimate=pl.CostEstimate(
            flops=2 * groups * slots * count * width, bytes_accessed=count * width * 2, transcendentals=0
        ),
        compiler_params=LIMIT,
        name="prepare",
    )(off_chip(values), off_chip(scales), off_chip(ids), off_chip(cents))


def pack(out_ref, first, residual, sub_width):
    half = sub_width // 2
    for k in range(residual.shape[0] // sub_width):
        part = residual[sub_width * k : sub_width * (k + 1)]
        most = jnp.maximum(jnp.max(jnp.abs(part), axis=0, keepdims=True), 1e-30)
        power = jnp.floor(jnp.log2(most)) + 1.0
        coded = jnp.clip(jnp.round(part * jnp.exp2(15.0 - power)), -32767.0, 32767.0).astype(jnp.int32)
        word = lax.shift_left(coded[:half], 16) | (coded[half:] & 0xFFFF)
        out_ref[first + k, :half, :] = word
        out_ref[first + k, half:, :] = jnp.broadcast_to(power.astype(jnp.int32), (8, part.shape[1]))


def unpack(words):
    half = words.shape[0] - 8
    unit = jnp.exp2(words[half : half + 1].astype(f32) - 15.0)
    words = words[:half]
    high = lax.shift_right_arithmetic(words, 16)
    low = lax.shift_right_arithmetic(lax.shift_left(words, 16), 16)
    return jnp.concatenate([high, low], axis=0).astype(f32) * unit


def residual_kernel(count, slots, sub_width, ids_ref, fetched_ref, q_ref, out_ref):
    rows, width = q_ref.shape
    ids = ids_ref[pl.ds(lax.axis_index("cent"), 1), :]
    owner = lax.div(ids, count)
    across = jnp.broadcast_to(owner, (rows, rows))
    down = across.astype(f32).T.astype(jnp.int32)
    earlier = lax.broadcasted_iota(jnp.int32, (rows, rows), 0) < lax.broadcasted_iota(
        jnp.int32, (rows, rows), 1
    )
    rank = jnp.sum(jnp.where((across == down) & earlier, 1.0, 0.0), axis=0, keepdims=True)
    slot = owner * slots + rank.astype(jnp.int32)
    number = lax.broadcasted_iota(jnp.int32, (fetched_ref.shape[0], rows), 0)
    place = (number == slot).astype(f32).astype(bf16)
    for j in range(width // 128):
        lanes = slice(128 * j, 128 * j + 128)
        fetched = lax.dot_general(
            place, fetched_ref[:, lanes], (((0,), (0,)), ((), ())), preferred_element_type=f32
        )
        pack(out_ref, 2 * j, (q_ref[:, lanes].astype(f32) - fetched).T, sub_width)


def residuals(ids, fetched, q, count, slots, sub_width):
    rows, width = q.shape
    return pl.pallas_call(
        functools.partial(residual_kernel, count, slots, sub_width),
        out_shape=pltpu.VMEM((width // sub_width, sub_width // 2 + 8, rows), jnp.int32),
        in_specs=[VM] * 3,
        out_specs=VM,
        cost_estimate=pl.CostEstimate(
            flops=2 * fetched.size * rows, bytes_accessed=fetched.size * 2 + rows * width * 6, transcendentals=0
        ),
        compiler_params=LIMIT,
        name="residuals",
    )(ids, on_chip(fetched), on_chip(q))


def nearest_kernel(step, ahead, blocks, mode, *refs):
    x_refs, refs = refs[:blocks], refs[blocks:]
    copies = []
    if mode == "again":
        cents_ref, squares_ref, out_ref = refs
    else:
        if mode == "first":
            cents_hbm, out_ref, squares_ref, cents_ref, sems = refs
        else:
            cents_hbm, squares_ref, out_ref, cents_ref, sems = refs
        half = step // 2
        copies = [
            pltpu.make_async_copy(cents_hbm.at[pl.ds(half * i, half), :], cents_ref.at[i], sems.at[i])
            for i in range(cents_ref.shape[0])
        ]
    for copy in copies[:ahead]:
        copy.start()
    best = [None] * (blocks // 2)
    for i in range(0, cents_ref.shape[0], 2):
        for k in (i, i + 1) if copies else ():
            copies[k].wait()
            if k + ahead < len(copies):
                copies[k + ahead].start()
        block = jnp.concatenate([cents_ref[i], cents_ref[i + 1]], axis=0)
        at = slice(step // 2 * i, step // 2 * i + step)
        if mode != "first":
            squares = squares_ref[at, :]
        else:
            total = None
            for b in range(block.shape[1] // 128):
                wide = block[:, 128 * b : 128 * b + 128].astype(f32)
                total = wide * wide if total is None else total + wide * wide
            squares = jnp.broadcast_to(jnp.sum(total, axis=1, keepdims=True), (step, 128))
            squares_ref[at, :] = squares
        squares = jnp.concatenate([squares, squares], axis=1)
        for j in range(len(best)):
            x = jnp.concatenate([x_refs[2 * j][...], x_refs[2 * j + 1][...]], axis=0)
            cross = lax.dot_general(block, x, (((1,), (1,)), ((), ())), preferred_element_type=f32)
            low = jnp.min(squares - 2.0 * cross, axis=0, keepdims=True)
            best[j] = low if best[j] is None else jnp.minimum(best[j], low)
    for j, low in enumerate(best):
        for k in range(2):
            out_ref[2 * j + k : 2 * j + k + 1, :] = low[:, 128 * k : 128 * k + 128]


def nearest(xs, cents, squares=None, kept=None):
    count, width = cents.shape
    rows = sum(x.shape[0] for x in xs)
    step = 512
    mode = "first" if squares is None else "keep" if kept is None else "again"
    out = [pltpu.VMEM((rows // 128, 128), f32)]
    held = [pltpu.VMEM((2 * count // step, step // 2, width), bf16)]
    sems = [pltpu.SemaphoreType.DMA((2 * count // step,))]
    ins, operands, outs, scratch = {
        "first": ([HBM], [off_chip(cents)], out + [pltpu.VMEM((count, 128), f32)], held + sems),
        "keep": ([HBM, VM], [off_chip(cents), squares], out + held, sems),
        "again": ([VM, VM], [kept, squares], out, []),
    }[mode]
    operands = operands[:1] + [on_chip(x) for x in operands[1:]]
    if mode == "again":
        operands[0] = on_chip(operands[0])
    return pl.pallas_call(
        functools.partial(nearest_kernel, step, 3, len(xs), mode),
        out_shape=tuple(outs),
        in_specs=[VM] * len(xs) + ins,
        out_specs=tuple([VM] * len(outs)),
        scratch_shapes=scratch,
        cost_estimate=pl.CostEstimate(
            flops=2 * rows * count * width, bytes_accessed=count * width * 2 + rows * width * 2, transcendentals=0
        ),
        compiler_params=LIMIT,
        name="nearest",
    )(*[on_chip(x) for x in xs], *operands)


def halves_of(x):
    high = x.astype(bf16)
    return high, (x - high.astype(f32)).astype(bf16)


def statistics_kernel(where, coded_ref, one_ref, two_ref, *refs):
    gap_refs, (mine_ref, theirs_ref, sub_out_ref) = refs[:-3], refs[-3:]
    groups, width, rows = sub_out_ref.shape
    words = 256
    high, low = [], []
    for g in range(groups):
        sub = unpack(coded_ref[g])
        sub_out_ref[g] = sub
        h, l = halves_of(sub)
        high.append(h)
        low.append(l)
    ones = jnp.ones((16, groups * rows), bf16)
    left = jnp.concatenate([jnp.concatenate(high, axis=1), jnp.concatenate(low, axis=1), ones], axis=0)
    word = lax.broadcasted_iota(jnp.int32, (words, groups * rows), 0)
    core = lax.rem(lax.axis_index("cent"), 2)
    odd = core == 1

    def totals(codes_ref):
        hit = (word == codes_ref[...]).astype(f32).astype(bf16)
        out = lax.dot_general(left, hit, (((1,), (1,)), ((), ())), preferred_element_type=f32)
        return out[:width] + out[width : 2 * width], out[2 * width : 2 * width + 8]

    for at, codes_ref in enumerate((one_ref, two_ref)):
        total, count = totals(codes_ref)
        rows_at = slice(width * at, width * at + width)
        a, b = total[:, :128], total[:, 128:]
        mine_ref[rows_at, :] = jnp.where(odd, b, a)
        theirs_ref[rows_at, :] = jnp.where(odd, a, b)
        a, b = count[:4, :128], count[:4, 128:]
        count_at = slice(2 * width + 4 * at, 2 * width + 4 * at + 4)
        mine_ref[count_at, :] = jnp.where(odd, b, a)
        theirs_ref[count_at, :] = jnp.where(odd, a, b)
    for j in range(8):
        for out_ref, d in ((mine_ref, 2 * j), (theirs_ref, 2 * j + 1)):
            k, row = where[d]
            out_ref[STATS + j : STATS + j + 1, :] = gap_refs[k][row : row + 1, :]


def statistics(coded, codes_one, codes_two, lows, where):
    groups, words, rows = coded.shape
    sub = jax.ShapeDtypeStruct((groups, 2 * (words - 8), rows), f32)
    shape = pltpu.VMEM((PAY, 128), f32)
    return pl.pallas_call(
        functools.partial(statistics_kernel, where),
        out_shape=(shape, shape, pltpu.VMEM(sub.shape, f32)),
        in_specs=[VM] * (3 + len(lows)),
        out_specs=(VM, VM, VM),
        cost_estimate=pl.CostEstimate(
            flops=2 * 2 * sub.size * 512, bytes_accessed=sub.size * 4, transcendentals=0
        ),
        compiler_params=LIMIT,
        name="statistics",
    )(on_chip(coded), codes_one, codes_two, *[on_chip(x) for x in lows])


def join_kernel(shift, a_ref, b_ref, out_ref):
    out_ref[:STATS, :] = a_ref[:STATS, :] + b_ref[:STATS, :]
    keep = PAY - STATS - shift
    out_ref[STATS:PAY, :] = a_ref[STATS:PAY, :]
    out_ref[STATS : STATS + keep, :] = jnp.minimum(
        a_ref[STATS : STATS + keep, :], b_ref[STATS + shift : PAY, :]
    )


def join(a, b, shift):
    return pl.pallas_call(
        functools.partial(join_kernel, shift),
        out_shape=pltpu.VMEM(a.shape, f32),
        in_specs=[VM, VM],
        out_specs=VM,
        cost_estimate=pl.CostEstimate(flops=a.size, bytes_accessed=a.size * 12, transcendentals=0),
        compiler_params=LIMIT,
        name="join",
    )(on_chip(a), on_chip(b))


def update_kernel(width, a_ref, b_ref, c_ref, d_ref, init_ref, squares_ref, books_ref, gap_ref):
    core = lax.rem(lax.axis_index("cent"), 2)
    total = (a_ref[:STATS, :] + b_ref[:STATS, :]) + (c_ref[:STATS, :] + d_ref[:STATS, :])
    init = jnp.where(core == 1, init_ref[:, 128:], init_ref[:, :128])
    count_one = total[2 * width : 2 * width + 1]
    count_two = total[2 * width + 4 : 2 * width + 5]
    one = (total[:width] + prior_weight * init) / (count_one + prior_weight)
    two = (total[width : 2 * width] + prior_weight * one) / (count_two + prior_weight)
    books_ref[:width, :] = one
    books_ref[width:, :] = two
    low = jnp.minimum(
        jnp.minimum(a_ref[STATS : STATS + 1, :], b_ref[STATS + 1 : STATS + 2, :]),
        jnp.minimum(c_ref[STATS + 2 : STATS + 3, :], d_ref[STATS + 3 : STATS + 4, :]),
    )
    gap_ref[...] = (low + squares_ref[...]) * (1.0 / 1024.0)


def update(parts, init, squares):
    width = init.shape[0]
    return pl.pallas_call(
        functools.partial(update_kernel, width),
        out_shape=(
            pltpu.VMEM((2 * width, 128), f32),
            jax.ShapeDtypeStruct((1, 128), f32),
        ),
        in_specs=[VM] * 6,
        out_specs=(VM, VM),
        cost_estimate=pl.CostEstimate(flops=8 * STATS * 128, bytes_accessed=5 * PAY * 512, transcendentals=0),
        compiler_params=LIMIT,
        name="update",
    )(*[on_chip(x) for x in parts], init, on_chip(squares))


def distortion_kernel(sub_ref, two_ref, mine_ref, theirs_ref, one_out_ref, two_out_ref, out_ref):
    groups, width, rows = sub_ref.shape
    odd = lax.rem(lax.axis_index("cent"), 2) == 1
    mine, theirs = mine_ref[...], theirs_ref[...]
    books = jnp.concatenate([jnp.where(odd, theirs, mine), jnp.where(odd, mine, theirs)], axis=1)
    one_out_ref[...] = books[:width]
    book = books[width:]
    two_out_ref[...] = book
    high, low = halves_of(book)
    left = jnp.concatenate([high, low], axis=0)
    words = book.shape[1]
    for g in range(0, groups, 2):
        lanes = slice(rows * g, rows * g + 2 * rows)
        word = lax.broadcasted_iota(jnp.int32, (words, 2 * rows), 0)
        hit = (word == two_ref[:, lanes]).astype(f32).astype(bf16)
        rebuilt = jnp.dot(left, hit, preferred_element_type=f32)
        rebuilt = rebuilt[:width] + rebuilt[width:]
        sub = jnp.concatenate([sub_ref[g], sub_ref[g + 1]], axis=1)
        miss = sub - rebuilt
        out_ref[:, lanes] = jnp.sum(miss * miss, axis=0, keepdims=True) * (1.0 / width)


def distortions(sub, codes_two, mine, theirs):
    groups, width, rows = sub.shape
    return pl.pallas_call(
        distortion_kernel,
        out_shape=(
            jax.ShapeDtypeStruct((width, 256), f32),
            jax.ShapeDtypeStruct((width, 256), f32),
            jax.ShapeDtypeStruct((1, groups * rows), f32),
        ),
        in_specs=[VM] * 4,
        out_specs=(VM, VM, VM),
        cost_estimate=pl.CostEstimate(
            flops=4 * sub.size * 256, bytes_accessed=sub.size * 4, transcendentals=0
        ),
        compiler_params=LIMIT,
        name="distortion",
    )(on_chip(sub), codes_two, on_chip(mine), on_chip(theirs))


def swap(x, offset):
    return lax.ppermute(x, "cent", [(i, i ^ offset) for i in range(16)])


def step(emb_values, emb_scales, coarse_ids, centroids, codes_one, codes_two, codebook_init):
    _, width = emb_values.shape
    count = centroids.shape[0]
    sub_width = codebook_init.shape[2]
    peers = coarse_ids.shape[0]
    slots = 16

    q, row_squares, sent = prepare(emb_values, emb_scales, coarse_ids, centroids, slots)

    core = 1

    blocks = {0: q, 2: swap(q, 2), 6: swap(q, 6), 8: swap(q, 8)}
    blocks[core] = swap(q, core)

    fetched = lax.all_to_all(sent.reshape(peers, slots, width), "cent", 0, 0)
    fetched = fetched.reshape(peers * slots, width)

    blocks[14] = swap(blocks[8], 6)
    blocks[10] = swap(blocks[8], 2)
    blocks[4] = swap(blocks[6], 2)
    blocks[12] = swap(blocks[10], 6)
    for d in (2, 6, 8, 4, 10, 14, 12):
        blocks[d ^ core] = swap(blocks[d], core)

    orders = ((0, 1, 8, 9), (2, 3, 6, 7, 10, 11, 14, 15), (4, 12), (5, 13))
    lows, squares, kept = [], None, None
    for k, order in enumerate(orders):
        low, *more = nearest([blocks[d] for d in order], centroids, squares, kept)
        lows.append(low)
        if k == 0:
            (squares,) = more
        elif k == 1:
            (kept,) = more
    where = {d: (k, j) for k, order in enumerate(orders) for j, d in enumerate(order)}

    coded = residuals(coarse_ids, fetched, q, count, slots, sub_width)
    coded = lax.all_to_all(coded, "rows", 0, 0)

    mine, theirs, sub = statistics(coded, codes_one, codes_two, lows, where)
    mine = join(mine, swap(theirs, 1), 0)
    mine = join(mine, swap(mine, 8), 4)
    parts = [mine] + [swap(mine, d) for d in (2, 4, 6)]
    init = codebook_init[0].T
    books, coarse_gap = update(parts, init, row_squares)
    book_one, book_two, distortion = distortions(sub, codes_two, books, swap(books, 1))
    return coarse_gap[0], book_one.T[None], book_two.T[None], distortion


def solution(mesh):
    placed = (
        P(("cent", "rows"), None),
        P(("cent", "rows"), None),
        P(None, "rows"),
        P("cent", None),
        P("rows", "cent"),
        P("rows", "cent"),
        P("rows", None, None),
    )
    return jax.shard_map(
        step,
        mesh=mesh,
        in_specs=placed,
        out_specs=(
            P(("cent", "rows")),
            P("rows", None, None),
            P("rows", None, None),
            P("rows", "cent"),
        ),
        check_vma=False,
    )
```

```python
import functools

import jax
import jax.numpy as jnp
from jax import lax
from jax.experimental import pallas as pl
from jax.experimental.pallas import tpu as pltpu
from jax.sharding import PartitionSpec as P


bf16 = jnp.bfloat16
f32 = jnp.float32
prior_weight = 8.0
VM = pl.BlockSpec(memory_space=pltpu.VMEM)
HBM = pl.BlockSpec(memory_space=pltpu.HBM)
LIMIT = pltpu.CompilerParams(vmem_limit_bytes=16 << 20)


def off_chip(x):
    return pltpu.with_memory_space_constraint(x, pltpu.HBM)


def on_chip(x):
    return pltpu.with_memory_space_constraint(x, pltpu.VMEM)


STATS = 136
PAY = 144


def prepare_kernel(
    slots, step, values_hbm, scales_hbm, ids_hbm, cents_hbm, q_ref, squares_ref, out_ref,
    values, scales_t, ids_ref, cents_ref, onehot_ref, total_ref, sems,
):
    count, _ = cents_hbm.shape
    groups, rows = ids_ref.shape
    small = (
        pltpu.make_async_copy(ids_hbm, ids_ref, sems.at[0]),
        pltpu.make_async_copy(scales_hbm, scales_t, sems.at[1]),
        pltpu.make_async_copy(values_hbm, values, sems.at[2]),
    )
    large = [
        pltpu.make_async_copy(cents_hbm.at[pl.ds(step * j, step), :], cents_ref.at[j], sems.at[3 + j])
        for j in range(count // step)
    ]
    for copy in small:
        copy.start()
    for copy in large:
        copy.start()

    small[0].wait()
    local = ids_ref[...] - lax.axis_index("cent") * count
    mine = (local >= 0) & (local < count)
    before = lax.broadcasted_iota(jnp.int32, (rows, rows), 0) <= lax.broadcasted_iota(
        jnp.int32, (rows, rows), 1
    )
    rank = jnp.dot(
        mine.astype(f32).astype(bf16), before.astype(f32).astype(bf16), preferred_element_type=f32
    )
    slot = jnp.where(mine, rank - 1.0, -1.0)
    local = local.astype(f32)
    spread_slot = jnp.concatenate(
        [jnp.broadcast_to(slot[g : g + 1], (slots, rows)) for g in range(groups)], axis=0
    )
    spread_local = jnp.concatenate(
        [jnp.broadcast_to(local[g : g + 1], (slots, rows)) for g in range(groups)], axis=0
    )
    number = lax.rem(lax.broadcasted_iota(jnp.int32, (groups * slots, rows), 0), slots).astype(f32)
    chosen = jnp.sum(jnp.where(spread_slot == number, spread_local + 1.0, 0.0), axis=1, keepdims=True)
    chosen = chosen.astype(jnp.int32) - 1

    small[1].wait()
    small[2].wait()
    scales = scales_t[...].astype(f32).T
    squares = None
    for b in range(scales.shape[1]):
        lanes = slice(128 * b, 128 * b + 128)
        q = (values[:, lanes].astype(f32) * scales[:, b : b + 1]).astype(bf16)
        q_ref[:, lanes] = q
        wide = q.astype(f32)
        squares = wide * wide if squares is None else squares + wide * wide
    squares_ref[...] = jnp.sum(squares.T, axis=0, keepdims=True)

    for j in range(count // 256):
        at = lax.broadcasted_iota(jnp.int32, (groups * slots, 256), 1) + 256 * j
        onehot_ref[:, 256 * j : 256 * j + 256] = (at == chosen).astype(f32).astype(bf16)
    for j, copy in enumerate(large):
        copy.wait()
        part = jnp.dot(
            onehot_ref[:, step * j : step * j + step], cents_ref[j], preferred_element_type=f32
        )
        if j > 0:
            part = total_ref[...] + part
        if j + 1 < len(large):
            total_ref[...] = part
        else:
            out_ref[...] = part.astype(bf16)


def prepare(values, scales, ids, cents, slots):
    rows, width = values.shape
    groups = ids.shape[0]
    count = cents.shape[0]
    scales = scales.T
    step = 512
    return pl.pallas_call(
        functools.partial(prepare_kernel, slots, step),
        out_shape=(
            pltpu.VMEM((rows, width), bf16),
            pltpu.VMEM((1, rows), f32),
            pltpu.VMEM((groups * slots, width), bf16),
        ),
        in_specs=[HBM] * 4,
        out_specs=(VM, VM, VM),
        scratch_shapes=[
            pltpu.VMEM(values.shape, bf16),
            pltpu.VMEM(scales.shape, bf16),
            pltpu.VMEM(ids.shape, jnp.int32),
            pltpu.VMEM((count // step, step, width), bf16),
            pltpu.VMEM((groups * slots, count), bf16),
            pltpu.VMEM((groups * slots, width), f32),
            pltpu.SemaphoreType.DMA((count // step + 3,)),
        ],
        cost_estimate=pl.CostEstimate(
            flops=2 * groups * slots * count * width, bytes_accessed=count * width * 2, transcendentals=0
        ),
        compiler_params=LIMIT,
        name="prepare",
    )(off_chip(values), off_chip(scales), off_chip(ids), off_chip(cents))


def pack(out_ref, first, residual, sub_width):
    half = sub_width // 2
    for k in range(residual.shape[0] // sub_width):
        part = residual[sub_width * k : sub_width * (k + 1)]
        most = jnp.maximum(jnp.max(jnp.abs(part), axis=0, keepdims=True), 1e-30)
        power = jnp.floor(jnp.log2(most)) + 1.0
        coded = jnp.clip(jnp.round(part * jnp.exp2(15.0 - power)), -32767.0, 32767.0).astype(jnp.int32)
        word = lax.shift_left(coded[:half], 16) | (coded[half:] & 0xFFFF)
        out_ref[first + k, :half, :] = word
        out_ref[first + k, half:, :] = jnp.broadcast_to(power.astype(jnp.int32), (8, part.shape[1]))


def unpack(words):
    half = words.shape[0] - 8
    unit = jnp.exp2(words[half : half + 1].astype(f32) - 15.0)
    words = words[:half]
    high = lax.shift_right_arithmetic(words, 16)
    low = lax.shift_right_arithmetic(lax.shift_left(words, 16), 16)
    return jnp.concatenate([high, low], axis=0).astype(f32) * unit


def residual_kernel(count, slots, sub_width, ids_ref, fetched_ref, q_ref, out_ref):
    rows, width = q_ref.shape
    ids = ids_ref[pl.ds(lax.axis_index("cent"), 1), :]
    owner = lax.div(ids, count)
    across = jnp.broadcast_to(owner, (rows, rows))
    down = across.astype(f32).T.astype(jnp.int32)
    earlier = lax.broadcasted_iota(jnp.int32, (rows, rows), 0) < lax.broadcasted_iota(
        jnp.int32, (rows, rows), 1
    )
    rank = jnp.sum(jnp.where((across == down) & earlier, 1.0, 0.0), axis=0, keepdims=True)
    slot = owner * slots + rank.astype(jnp.int32)
    number = lax.broadcasted_iota(jnp.int32, (fetched_ref.shape[0], rows), 0)
    place = (number == slot).astype(f32).astype(bf16)
    for j in range(width // 128):
        lanes = slice(128 * j, 128 * j + 128)
        fetched = lax.dot_general(
            place, fetched_ref[:, lanes], (((0,), (0,)), ((), ())), preferred_element_type=f32
        )
        pack(out_ref, 2 * j, (q_ref[:, lanes].astype(f32) - fetched).T, sub_width)


def residuals(ids, fetched, q, count, slots, sub_width):
    rows, width = q.shape
    return pl.pallas_call(
        functools.partial(residual_kernel, count, slots, sub_width),
        out_shape=pltpu.VMEM((width // sub_width, sub_width // 2 + 8, rows), jnp.int32),
        in_specs=[VM] * 3,
        out_specs=VM,
        cost_estimate=pl.CostEstimate(
            flops=2 * fetched.size * rows, bytes_accessed=fetched.size * 2 + rows * width * 6, transcendentals=0
        ),
        compiler_params=LIMIT,
        name="residuals",
    )(ids, on_chip(fetched), on_chip(q))


def nearest_kernel(step, ahead, blocks, mode, *refs):
    x_refs, refs = refs[:blocks], refs[blocks:]
    if mode == "first":
        cents_hbm, out_ref, squares_ref, head_ref, tail_ref, sems = refs
    elif mode == "keep":
        cents_hbm, squares_ref, head_ref, out_ref, tail_ref, sems = refs
    else:
        squares_ref, head_ref, tail_ref, out_ref = refs
    half = step // 2
    kept = head_ref.shape[0]
    parts = kept + tail_ref.shape[0]

    def place(i):
        return head_ref.at[i] if i < kept else tail_ref.at[i - kept]

    copies = {}
    if mode != "again":
        for i in range(0 if mode == "first" else kept, parts):
            copies[i] = pltpu.make_async_copy(
                cents_hbm.at[pl.ds(half * i, half), :], place(i), sems.at[i]
            )
    waiting = list(copies)
    for i in waiting[:ahead]:
        copies[i].start()
    waiting = waiting[ahead:]
    best = [None] * (blocks // 2)
    for i in range(0, parts, 2):
        for k in (i, i + 1):
            if k in copies:
                copies[k].wait()
                if waiting:
                    copies[waiting.pop(0)].start()
        block = jnp.concatenate([place(i)[...], place(i + 1)[...]], axis=0)
        at = slice(step // 2 * i, step // 2 * i + step)
        if mode != "first":
            squares = squares_ref[at, :]
        else:
            total = None
            for b in range(block.shape[1] // 128):
                wide = block[:, 128 * b : 128 * b + 128].astype(f32)
                total = wide * wide if total is None else total + wide * wide
            squares = jnp.broadcast_to(jnp.sum(total, axis=1, keepdims=True), (step, 128))
            squares_ref[at, :] = squares
        squares = jnp.concatenate([squares, squares], axis=1)
        for j in range(len(best)):
            x = jnp.concatenate([x_refs[2 * j][...], x_refs[2 * j + 1][...]], axis=0)
            cross = lax.dot_general(block, x, (((1,), (1,)), ((), ())), preferred_element_type=f32)
            low = jnp.min(squares - 2.0 * cross, axis=0, keepdims=True)
            best[j] = low if best[j] is None else jnp.minimum(best[j], low)
    for j, low in enumerate(best):
        for k in range(2):
            out_ref[2 * j + k : 2 * j + k + 1, :] = low[:, 128 * k : 128 * k + 128]


def nearest(xs, cents, squares=None, head=None, tail=None):
    count, width = cents.shape
    rows = sum(x.shape[0] for x in xs)
    step = 512
    parts = 2 * count // step
    mode = "first" if squares is None else "keep" if tail is None else "again"
    out = pltpu.VMEM((rows // 128, 128), f32)
    first, rest = (pltpu.VMEM((n, step // 2, width), bf16) for n in (2, parts - 2))
    sems = pltpu.SemaphoreType.DMA((parts,))
    far, near, outs, scratch = {
        "first": ([cents], [], [out, pltpu.VMEM((count, 128), f32), first], [rest, sems]),
        "keep": ([cents], [squares, head], [out, rest], [sems]),
        "again": ([], [squares, head, tail], [out], []),
    }[mode]
    return pl.pallas_call(
        functools.partial(nearest_kernel, step, 3, len(xs), mode),
        out_shape=tuple(outs),
        in_specs=[VM] * len(xs) + [HBM] * len(far) + [VM] * len(near),
        out_specs=tuple([VM] * len(outs)),
        scratch_shapes=scratch,
        cost_estimate=pl.CostEstimate(
            flops=2 * rows * count * width, bytes_accessed=count * width * 2 + rows * width * 2, transcendentals=0
        ),
        compiler_params=LIMIT,
        name="nearest",
    )(*[on_chip(x) for x in xs], *[off_chip(x) for x in far], *[on_chip(x) for x in near])


def halves_of(x):
    high = x.astype(bf16)
    return high, (x - high.astype(f32)).astype(bf16)


def statistics_kernel(where, coded_ref, one_ref, two_ref, *refs):
    gap_refs, (mine_ref, theirs_ref, sub_out_ref) = refs[:-3], refs[-3:]
    groups, width, rows = sub_out_ref.shape
    words = 256
    high, low = [], []
    for g in range(groups):
        sub = unpack(coded_ref[g])
        sub_out_ref[g] = sub
        h, l = halves_of(sub)
        high.append(h)
        low.append(l)
    ones = jnp.ones((16, groups * rows), bf16)
    left = jnp.concatenate([jnp.concatenate(high, axis=1), jnp.concatenate(low, axis=1), ones], axis=0)
    word = lax.broadcasted_iota(jnp.int32, (words, groups * rows), 0)
    core = lax.rem(lax.axis_index("cent"), 2)
    odd = core == 1

    def totals(codes_ref):
        hit = (word == codes_ref[...]).astype(f32).astype(bf16)
        out = lax.dot_general(left, hit, (((1,), (1,)), ((), ())), preferred_element_type=f32)
        return out[:width] + out[width : 2 * width], out[2 * width : 2 * width + 8]

    for at, codes_ref in enumerate((one_ref, two_ref)):
        total, count = totals(codes_ref)
        rows_at = slice(width * at, width * at + width)
        a, b = total[:, :128], total[:, 128:]
        mine_ref[rows_at, :] = jnp.where(odd, b, a)
        theirs_ref[rows_at, :] = jnp.where(odd, a, b)
        a, b = count[:4, :128], count[:4, 128:]
        count_at = slice(2 * width + 4 * at, 2 * width + 4 * at + 4)
        mine_ref[count_at, :] = jnp.where(odd, b, a)
        theirs_ref[count_at, :] = jnp.where(odd, a, b)
    for j in range(8):
        for out_ref, d in ((mine_ref, 2 * j), (theirs_ref, 2 * j + 1)):
            k, row = where[d]
            out_ref[STATS + j : STATS + j + 1, :] = gap_refs[k][row : row + 1, :]


def statistics(coded, codes_one, codes_two, lows, where):
    groups, words, rows = coded.shape
    sub = jax.ShapeDtypeStruct((groups, 2 * (words - 8), rows), f32)
    shape = pltpu.VMEM((PAY, 128), f32)
    return pl.pallas_call(
        functools.partial(statistics_kernel, where),
        out_shape=(shape, shape, pltpu.VMEM(sub.shape, f32)),
        in_specs=[VM] * (3 + len(lows)),
        out_specs=(VM, VM, VM),
        cost_estimate=pl.CostEstimate(
            flops=2 * 2 * sub.size * 512, bytes_accessed=sub.size * 4, transcendentals=0
        ),
        compiler_params=LIMIT,
        name="statistics",
    )(on_chip(coded), codes_one, codes_two, *[on_chip(x) for x in lows])


def join_kernel(shift, a_ref, b_ref, out_ref):
    out_ref[:STATS, :] = a_ref[:STATS, :] + b_ref[:STATS, :]
    keep = PAY - STATS - shift
    out_ref[STATS:PAY, :] = a_ref[STATS:PAY, :]
    out_ref[STATS : STATS + keep, :] = jnp.minimum(
        a_ref[STATS : STATS + keep, :], b_ref[STATS + shift : PAY, :]
    )


def join(a, b, shift):
    return pl.pallas_call(
        functools.partial(join_kernel, shift),
        out_shape=pltpu.VMEM(a.shape, f32),
        in_specs=[VM, VM],
        out_specs=VM,
        cost_estimate=pl.CostEstimate(flops=a.size, bytes_accessed=a.size * 12, transcendentals=0),
        compiler_params=LIMIT,
        name="join",
    )(on_chip(a), on_chip(b))


def update_kernel(width, a_ref, b_ref, c_ref, d_ref, init_ref, squares_ref, books_ref, gap_ref):
    core = lax.rem(lax.axis_index("cent"), 2)
    total = (a_ref[:STATS, :] + b_ref[:STATS, :]) + (c_ref[:STATS, :] + d_ref[:STATS, :])
    init = jnp.where(core == 1, init_ref[:, 128:], init_ref[:, :128])
    count_one = total[2 * width : 2 * width + 1]
    count_two = total[2 * width + 4 : 2 * width + 5]
    one = (total[:width] + prior_weight * init) / (count_one + prior_weight)
    two = (total[width : 2 * width] + prior_weight * one) / (count_two + prior_weight)
    books_ref[:width, :] = one
    books_ref[width:, :] = two
    low = jnp.minimum(
        jnp.minimum(a_ref[STATS : STATS + 1, :], b_ref[STATS + 1 : STATS + 2, :]),
        jnp.minimum(c_ref[STATS + 2 : STATS + 3, :], d_ref[STATS + 3 : STATS + 4, :]),
    )
    gap_ref[...] = (low + squares_ref[...]) * (1.0 / 1024.0)


def update(parts, init, squares):
    width = init.shape[0]
    return pl.pallas_call(
        functools.partial(update_kernel, width),
        out_shape=(
            pltpu.VMEM((2 * width, 128), f32),
            jax.ShapeDtypeStruct((1, 128), f32),
        ),
        in_specs=[VM] * 6,
        out_specs=(VM, VM),
        cost_estimate=pl.CostEstimate(flops=8 * STATS * 128, bytes_accessed=5 * PAY * 512, transcendentals=0),
        compiler_params=LIMIT,
        name="update",
    )(*[on_chip(x) for x in parts], init, on_chip(squares))


def distortion_kernel(sub_ref, two_ref, mine_ref, theirs_ref, one_out_ref, two_out_ref, out_ref):
    groups, width, rows = sub_ref.shape
    odd = lax.rem(lax.axis_index("cent"), 2) == 1
    mine, theirs = mine_ref[...], theirs_ref[...]
    books = jnp.concatenate([jnp.where(odd, theirs, mine), jnp.where(odd, mine, theirs)], axis=1)
    one_out_ref[...] = books[:width]
    book = books[width:]
    two_out_ref[...] = book
    high, low = halves_of(book)
    left = jnp.concatenate([high, low], axis=0)
    words = book.shape[1]
    for g in range(0, groups, 2):
        lanes = slice(rows * g, rows * g + 2 * rows)
        word = lax.broadcasted_iota(jnp.int32, (words, 2 * rows), 0)
        hit = (word == two_ref[:, lanes]).astype(f32).astype(bf16)
        rebuilt = jnp.dot(left, hit, preferred_element_type=f32)
        rebuilt = rebuilt[:width] + rebuilt[width:]
        sub = jnp.concatenate([sub_ref[g], sub_ref[g + 1]], axis=1)
        miss = sub - rebuilt
        out_ref[:, lanes] = jnp.sum(miss * miss, axis=0, keepdims=True) * (1.0 / width)


def distortions(sub, codes_two, mine, theirs):
    groups, width, rows = sub.shape
    return pl.pallas_call(
        distortion_kernel,
        out_shape=(
            jax.ShapeDtypeStruct((width, 256), f32),
            jax.ShapeDtypeStruct((width, 256), f32),
            jax.ShapeDtypeStruct((1, groups * rows), f32),
        ),
        in_specs=[VM] * 4,
        out_specs=(VM, VM, VM),
        cost_estimate=pl.CostEstimate(
            flops=4 * sub.size * 256, bytes_accessed=sub.size * 4, transcendentals=0
        ),
        compiler_params=LIMIT,
        name="distortion",
    )(on_chip(sub), codes_two, on_chip(mine), on_chip(theirs))


def swap(x, offset):
    return lax.ppermute(x, "cent", [(i, i ^ offset) for i in range(16)])


def step(emb_values, emb_scales, coarse_ids, centroids, codes_one, codes_two, codebook_init):
    _, width = emb_values.shape
    count = centroids.shape[0]
    sub_width = codebook_init.shape[2]
    peers = coarse_ids.shape[0]
    slots = 16

    q, row_squares, sent = prepare(emb_values, emb_scales, coarse_ids, centroids, slots)

    core = 1

    blocks = {0: q, 2: swap(q, 2), 6: swap(q, 6), 8: swap(q, 8)}
    blocks[core] = swap(q, core)

    fetched = lax.all_to_all(sent.reshape(peers, slots, width), "cent", 0, 0)
    fetched = fetched.reshape(peers * slots, width)

    blocks[14] = swap(blocks[8], 6)
    blocks[10] = swap(blocks[8], 2)
    blocks[4] = swap(blocks[6], 2)
    blocks[12] = swap(blocks[10], 6)
    for d in (2, 6, 8, 4, 10, 14, 12):
        blocks[d ^ core] = swap(blocks[d], core)

    orders = ((0, 1, 8, 9), (2, 3, 6, 7, 10, 11, 14, 15), (4, 12), (5, 13))
    lows, kept = [], []
    for order in orders:
        low, *more = nearest([blocks[d] for d in order], centroids, *kept)
        lows.append(low)
        kept += more
    where = {d: (k, j) for k, order in enumerate(orders) for j, d in enumerate(order)}

    coded = residuals(coarse_ids, fetched, q, count, slots, sub_width)
    coded = lax.all_to_all(coded, "rows", 0, 0)

    mine, theirs, sub = statistics(coded, codes_one, codes_two, lows, where)
    mine = join(mine, swap(theirs, 1), 0)
    mine = join(mine, swap(mine, 8), 4)
    parts = [mine] + [swap(mine, d) for d in (2, 4, 6)]
    init = codebook_init[0].T
    books, coarse_gap = update(parts, init, row_squares)
    book_one, book_two, distortion = distortions(sub, codes_two, books, swap(books, 1))
    return coarse_gap[0], book_one.T[None], book_two.T[None], distortion


def solution(mesh):
    placed = (
        P(("cent", "rows"), None),
        P(("cent", "rows"), None),
        P(None, "rows"),
        P("cent", None),
        P("rows", "cent"),
        P("rows", "cent"),
        P("rows", None, None),
    )
    return jax.shard_map(
        step,
        mesh=mesh,
        in_specs=placed,
        out_specs=(
            P(("cent", "rows")),
            P("rows", None, None),
            P("rows", None, None),
            P("rows", "cent"),
        ),
        check_vma=False,
    )
```

```python
import functools

import jax
import jax.numpy as jnp
from jax import lax
from jax.experimental import pallas as pl
from jax.experimental.pallas import tpu as pltpu
from jax.sharding import PartitionSpec as P


bf16 = jnp.bfloat16
f32 = jnp.float32
prior_weight = 8.0
VM = pl.BlockSpec(memory_space=pltpu.VMEM)
HBM = pl.BlockSpec(memory_space=pltpu.HBM)
LIMIT = pltpu.CompilerParams(vmem_limit_bytes=16 << 20)


def off_chip(x):
    return pltpu.with_memory_space_constraint(x, pltpu.HBM)


def on_chip(x):
    return pltpu.with_memory_space_constraint(x, pltpu.VMEM)


STATS = 136
PAY = 144


def prepare_kernel(
    slots, step, values_hbm, scales_hbm, ids_hbm, cents_hbm, q_ref, squares_ref, out_ref, cent_squares_ref,
    values, scales_t, ids_ref, cents_ref, onehot_ref, total_ref, sems,
):
    count, width = cents_hbm.shape
    groups, rows = ids_ref.shape
    small = (
        pltpu.make_async_copy(ids_hbm, ids_ref, sems.at[0]),
        pltpu.make_async_copy(scales_hbm, scales_t, sems.at[1]),
        pltpu.make_async_copy(values_hbm, values, sems.at[2]),
    )
    large = [
        pltpu.make_async_copy(cents_hbm.at[pl.ds(step * j, step), :], cents_ref.at[j], sems.at[3 + j])
        for j in range(count // step)
    ]
    for copy in small:
        copy.start()
    for copy in large:
        copy.start()

    small[0].wait()
    local = ids_ref[...] - lax.axis_index("cent") * count
    mine = (local >= 0) & (local < count)
    before = lax.broadcasted_iota(jnp.int32, (rows, rows), 0) <= lax.broadcasted_iota(
        jnp.int32, (rows, rows), 1
    )
    rank = jnp.dot(
        mine.astype(f32).astype(bf16), before.astype(f32).astype(bf16), preferred_element_type=f32
    )
    slot = jnp.where(mine, rank - 1.0, -1.0)
    local = local.astype(f32)
    spread_slot = jnp.concatenate(
        [jnp.broadcast_to(slot[g : g + 1], (slots, rows)) for g in range(groups)], axis=0
    )
    spread_local = jnp.concatenate(
        [jnp.broadcast_to(local[g : g + 1], (slots, rows)) for g in range(groups)], axis=0
    )
    number = lax.rem(lax.broadcasted_iota(jnp.int32, (groups * slots, rows), 0), slots).astype(f32)
    chosen = jnp.sum(jnp.where(spread_slot == number, spread_local + 1.0, 0.0), axis=1, keepdims=True)
    chosen = chosen.astype(jnp.int32) - 1

    small[1].wait()
    small[2].wait()
    scales = scales_t[...].astype(f32).T
    squares = None
    for b in range(scales.shape[1]):
        lanes = slice(128 * b, 128 * b + 128)
        q = (values[:, lanes].astype(f32) * scales[:, b : b + 1]).astype(bf16)
        q_ref[:, lanes] = q
        wide = q.astype(f32)
        squares = wide * wide if squares is None else squares + wide * wide
    squares_ref[...] = jnp.sum(squares.T, axis=0, keepdims=True)

    for j in range(count // 256):
        at = lax.broadcasted_iota(jnp.int32, (groups * slots, 256), 1) + 256 * j
        onehot_ref[:, 256 * j : 256 * j + 256] = (at == chosen).astype(f32).astype(bf16)
    for j, copy in enumerate(large):
        copy.wait()
        part = jnp.dot(
            onehot_ref[:, step * j : step * j + step], cents_ref[j], preferred_element_type=f32
        )
        if j > 0:
            part = total_ref[...] + part
        if j + 1 < len(large):
            total_ref[...] = part
        else:
            out_ref[...] = part.astype(bf16)
        block = cents_ref[j]
        total = None
        for b in range(width // 128):
            wide = block[:, 128 * b : 128 * b + 128].astype(f32)
            total = wide * wide if total is None else total + wide * wide
        cent_squares_ref[step * j : step * j + step, :] = jnp.broadcast_to(
            jnp.sum(total, axis=1, keepdims=True), (step, 128)
        )


def prepare(values, scales, ids, cents, slots):
    rows, width = values.shape
    groups = ids.shape[0]
    count = cents.shape[0]
    scales = scales.T
    step = 512
    return pl.pallas_call(
        functools.partial(prepare_kernel, slots, step),
        out_shape=(
            pltpu.VMEM((rows, width), bf16),
            pltpu.VMEM((1, rows), f32),
            pltpu.VMEM((groups * slots, width), bf16),
            pltpu.VMEM((count, 128), f32),
        ),
        in_specs=[HBM] * 4,
        out_specs=(VM, VM, VM, VM),
        scratch_shapes=[
            pltpu.VMEM(values.shape, bf16),
            pltpu.VMEM(scales.shape, bf16),
            pltpu.VMEM(ids.shape, jnp.int32),
            pltpu.VMEM((count // step, step, width), bf16),
            pltpu.VMEM((groups * slots, count), bf16),
            pltpu.VMEM((groups * slots, width), f32),
            pltpu.SemaphoreType.DMA((count // step + 3,)),
        ],
        cost_estimate=pl.CostEstimate(
            flops=2 * groups * slots * count * width, bytes_accessed=count * width * 2, transcendentals=0
        ),
        compiler_params=LIMIT,
        name="prepare",
    )(off_chip(values), off_chip(scales), off_chip(ids), off_chip(cents))


def pack(out_ref, first, residual, sub_width):
    half = sub_width // 2
    for k in range(residual.shape[0] // sub_width):
        part = residual[sub_width * k : sub_width * (k + 1)]
        most = jnp.maximum(jnp.max(jnp.abs(part), axis=0, keepdims=True), 1e-30)
        power = jnp.floor(jnp.log2(most)) + 1.0
        coded = jnp.clip(jnp.round(part * jnp.exp2(15.0 - power)), -32767.0, 32767.0).astype(jnp.int32)
        word = lax.shift_left(coded[:half], 16) | (coded[half:] & 0xFFFF)
        out_ref[first + k, :half, :] = word
        out_ref[first + k, half:, :] = jnp.broadcast_to(power.astype(jnp.int32), (8, part.shape[1]))


def unpack(words):
    half = words.shape[0] - 8
    unit = jnp.exp2(words[half : half + 1].astype(f32) - 15.0)
    words = words[:half]
    high = lax.shift_right_arithmetic(words, 16)
    low = lax.shift_right_arithmetic(lax.shift_left(words, 16), 16)
    return jnp.concatenate([high, low], axis=0).astype(f32) * unit


def residual_kernel(count, slots, sub_width, ids_ref, fetched_ref, q_ref, out_ref):
    rows, width = q_ref.shape
    ids = ids_ref[pl.ds(lax.axis_index("cent"), 1), :]
    owner = lax.div(ids, count)
    across = jnp.broadcast_to(owner, (rows, rows))
    down = across.astype(f32).T.astype(jnp.int32)
    earlier = lax.broadcasted_iota(jnp.int32, (rows, rows), 0) < lax.broadcasted_iota(
        jnp.int32, (rows, rows), 1
    )
    rank = jnp.sum(jnp.where((across == down) & earlier, 1.0, 0.0), axis=0, keepdims=True)
    slot = owner * slots + rank.astype(jnp.int32)
    number = lax.broadcasted_iota(jnp.int32, (fetched_ref.shape[0], rows), 0)
    place = (number == slot).astype(f32).astype(bf16)
    for j in range(width // 128):
        lanes = slice(128 * j, 128 * j + 128)
        fetched = lax.dot_general(
            place, fetched_ref[:, lanes], (((0,), (0,)), ((), ())), preferred_element_type=f32
        )
        pack(out_ref, 2 * j, (q_ref[:, lanes].astype(f32) - fetched).T, sub_width)


def residuals(ids, fetched, q, count, slots, sub_width):
    rows, width = q.shape
    return pl.pallas_call(
        functools.partial(residual_kernel, count, slots, sub_width),
        out_shape=pltpu.VMEM((width // sub_width, sub_width // 2 + 8, rows), jnp.int32),
        in_specs=[VM] * 3,
        out_specs=VM,
        cost_estimate=pl.CostEstimate(
            flops=2 * fetched.size * rows, bytes_accessed=fetched.size * 2 + rows * width * 6, transcendentals=0
        ),
        compiler_params=LIMIT,
        name="residuals",
    )(ids, on_chip(fetched), on_chip(q))


def nearest_kernel(step, ahead, blocks, load, *refs):
    x_refs, refs = refs[:blocks], refs[blocks:]
    if load:
        squares_ref, cents_hbm, out_ref, cents_ref, sems = refs
    else:
        squares_ref, cents_ref, out_ref = refs
    half = step // 2
    parts = cents_ref.shape[0]
    copies = [
        pltpu.make_async_copy(cents_hbm.at[pl.ds(half * i, half), :], cents_ref.at[i], sems.at[i])
        for i in range(parts if load else 0)
    ]
    for copy in copies[:ahead]:
        copy.start()
    for first in range(0, blocks, 4):
        pairs = [(x_refs[j], x_refs[j + 1]) for j in range(first, min(first + 4, blocks), 2)]
        best = [None] * len(pairs)
        for i in range(0, parts, 2):
            for k in (i, i + 1) if load and first == 0 else ():
                copies[k].wait()
                if k + ahead < parts:
                    copies[k + ahead].start()
            block = jnp.concatenate([cents_ref[i], cents_ref[i + 1]], axis=0)
            squares = squares_ref[half * i : half * i + step, :]
            squares = jnp.concatenate([squares, squares], axis=1)
            for j, pair in enumerate(pairs):
                x = jnp.concatenate([ref[...] for ref in pair], axis=0)
                cross = lax.dot_general(block, x, (((1,), (1,)), ((), ())), preferred_element_type=f32)
                low = jnp.min(squares - 2.0 * cross, axis=0, keepdims=True)
                best[j] = low if best[j] is None else jnp.minimum(best[j], low)
        for j, low in enumerate(best):
            for k in range(2):
                row = first + 2 * j + k
                out_ref[row : row + 1, :] = low[:, 128 * k : 128 * k + 128]


def nearest(xs, squares, cents, kept, keep):
    count, width = cents.shape
    rows = sum(x.shape[0] for x in xs)
    step = 512
    load = kept is None
    held = pltpu.VMEM((2 * count // step, step // 2, width), bf16)
    sems = pltpu.SemaphoreType.DMA((2 * count // step,))
    outs = [pltpu.VMEM((rows // 128, 128), f32)] + [held] * keep
    result = pl.pallas_call(
        functools.partial(nearest_kernel, step, 3, len(xs), load),
        out_shape=tuple(outs),
        in_specs=[VM] * (len(xs) + 1) + [HBM if load else VM],
        out_specs=tuple([VM] * len(outs)),
        scratch_shapes=([] if keep else [held]) * load + [sems] * load,
        cost_estimate=pl.CostEstimate(
            flops=2 * rows * count * width, bytes_accessed=count * width * 2 + rows * width * 2, transcendentals=0
        ),
        compiler_params=LIMIT,
        name="nearest",
    )(*[on_chip(x) for x in xs], on_chip(squares), off_chip(cents) if load else on_chip(kept))
    return result[0], result[1] if keep else kept


def halves_of(x):
    high = x.astype(bf16)
    return high, (x - high.astype(f32)).astype(bf16)


def statistics_kernel(where, coded_ref, one_ref, two_ref, *refs):
    gap_refs, (mine_ref, theirs_ref, sub_out_ref) = refs[:-3], refs[-3:]
    groups, width, rows = sub_out_ref.shape
    words = 256
    high, low = [], []
    for g in range(groups):
        sub = unpack(coded_ref[g])
        sub_out_ref[g] = sub
        h, l = halves_of(sub)
        high.append(h)
        low.append(l)
    ones = jnp.ones((16, groups * rows), bf16)
    left = jnp.concatenate([jnp.concatenate(high, axis=1), jnp.concatenate(low, axis=1), ones], axis=0)
    word = lax.broadcasted_iota(jnp.int32, (words, groups * rows), 0)
    core = lax.rem(lax.axis_index("cent"), 2)
    odd = core == 1

    def totals(codes_ref):
        hit = (word == codes_ref[...]).astype(f32).astype(bf16)
        out = lax.dot_general(left, hit, (((1,), (1,)), ((), ())), preferred_element_type=f32)
        return out[:width] + out[width : 2 * width], out[2 * width : 2 * width + 8]

    for at, codes_ref in enumerate((one_ref, two_ref)):
        total, count = totals(codes_ref)
        rows_at = slice(width * at, width * at + width)
        a, b = total[:, :128], total[:, 128:]
        mine_ref[rows_at, :] = jnp.where(odd, b, a)
        theirs_ref[rows_at, :] = jnp.where(odd, a, b)
        a, b = count[:4, :128], count[:4, 128:]
        count_at = slice(2 * width + 4 * at, 2 * width + 4 * at + 4)
        mine_ref[count_at, :] = jnp.where(odd, b, a)
        theirs_ref[count_at, :] = jnp.where(odd, a, b)
    for j in range(8):
        for out_ref, d in ((mine_ref, 2 * j), (theirs_ref, 2 * j + 1)):
            k, row = where[d]
            out_ref[STATS + j : STATS + j + 1, :] = gap_refs[k][row : row + 1, :]


def statistics(coded, codes_one, codes_two, lows, where):
    groups, words, rows = coded.shape
    sub = jax.ShapeDtypeStruct((groups, 2 * (words - 8), rows), f32)
    shape = pltpu.VMEM((PAY, 128), f32)
    return pl.pallas_call(
        functools.partial(statistics_kernel, where),
        out_shape=(shape, shape, pltpu.VMEM(sub.shape, f32)),
        in_specs=[VM] * (3 + len(lows)),
        out_specs=(VM, VM, VM),
        cost_estimate=pl.CostEstimate(
            flops=2 * 2 * sub.size * 512, bytes_accessed=sub.size * 4, transcendentals=0
        ),
        compiler_params=LIMIT,
        name="statistics",
    )(on_chip(coded), codes_one, codes_two, *[on_chip(x) for x in lows])


def join_kernel(shift, a_ref, b_ref, out_ref):
    out_ref[:STATS, :] = a_ref[:STATS, :] + b_ref[:STATS, :]
    keep = PAY - STATS - shift
    out_ref[STATS:PAY, :] = a_ref[STATS:PAY, :]
    out_ref[STATS : STATS + keep, :] = jnp.minimum(
        a_ref[STATS : STATS + keep, :], b_ref[STATS + shift : PAY, :]
    )


def join(a, b, shift):
    return pl.pallas_call(
        functools.partial(join_kernel, shift),
        out_shape=pltpu.VMEM(a.shape, f32),
        in_specs=[VM, VM],
        out_specs=VM,
        cost_estimate=pl.CostEstimate(flops=a.size, bytes_accessed=a.size * 12, transcendentals=0),
        compiler_params=LIMIT,
        name="join",
    )(on_chip(a), on_chip(b))


def update_kernel(width, a_ref, b_ref, c_ref, d_ref, init_ref, squares_ref, books_ref, gap_ref):
    core = lax.rem(lax.axis_index("cent"), 2)
    total = (a_ref[:STATS, :] + b_ref[:STATS, :]) + (c_ref[:STATS, :] + d_ref[:STATS, :])
    init = jnp.where(core == 1, init_ref[:, 128:], init_ref[:, :128])
    count_one = total[2 * width : 2 * width + 1]
    count_two = total[2 * width + 4 : 2 * width + 5]
    one = (total[:width] + prior_weight * init) / (count_one + prior_weight)
    two = (total[width : 2 * width] + prior_weight * one) / (count_two + prior_weight)
    books_ref[:width, :] = one
    books_ref[width:, :] = two
    low = jnp.minimum(
        jnp.minimum(a_ref[STATS : STATS + 1, :], b_ref[STATS + 1 : STATS + 2, :]),
        jnp.minimum(c_ref[STATS + 2 : STATS + 3, :], d_ref[STATS + 3 : STATS + 4, :]),
    )
    gap_ref[...] = (low + squares_ref[...]) * (1.0 / 1024.0)


def update(parts, init, squares):
    width = init.shape[0]
    return pl.pallas_call(
        functools.partial(update_kernel, width),
        out_shape=(
            pltpu.VMEM((2 * width, 128), f32),
            jax.ShapeDtypeStruct((1, 128), f32),
        ),
        in_specs=[VM] * 6,
        out_specs=(VM, VM),
        cost_estimate=pl.CostEstimate(flops=8 * STATS * 128, bytes_accessed=5 * PAY * 512, transcendentals=0),
        compiler_params=LIMIT,
        name="update",
    )(*[on_chip(x) for x in parts], init, on_chip(squares))


def distortion_kernel(sub_ref, two_ref, mine_ref, theirs_ref, one_out_ref, two_out_ref, out_ref):
    groups, width, rows = sub_ref.shape
    odd = lax.rem(lax.axis_index("cent"), 2) == 1
    mine, theirs = mine_ref[...], theirs_ref[...]
    books = jnp.concatenate([jnp.where(odd, theirs, mine), jnp.where(odd, mine, theirs)], axis=1)
    one_out_ref[...] = books[:width]
    book = books[width:]
    two_out_ref[...] = book
    high, low = halves_of(book)
    left = jnp.concatenate([high, low], axis=0)
    words = book.shape[1]
    for g in range(0, groups, 2):
        lanes = slice(rows * g, rows * g + 2 * rows)
        word = lax.broadcasted_iota(jnp.int32, (words, 2 * rows), 0)
        hit = (word == two_ref[:, lanes]).astype(f32).astype(bf16)
        rebuilt = jnp.dot(left, hit, preferred_element_type=f32)
        rebuilt = rebuilt[:width] + rebuilt[width:]
        sub = jnp.concatenate([sub_ref[g], sub_ref[g + 1]], axis=1)
        miss = sub - rebuilt
        out_ref[:, lanes] = jnp.sum(miss * miss, axis=0, keepdims=True) * (1.0 / width)


def distortions(sub, codes_two, mine, theirs):
    groups, width, rows = sub.shape
    return pl.pallas_call(
        distortion_kernel,
        out_shape=(
            jax.ShapeDtypeStruct((width, 256), f32),
            jax.ShapeDtypeStruct((width, 256), f32),
            jax.ShapeDtypeStruct((1, groups * rows), f32),
        ),
        in_specs=[VM] * 4,
        out_specs=(VM, VM, VM),
        cost_estimate=pl.CostEstimate(
            flops=4 * sub.size * 256, bytes_accessed=sub.size * 4, transcendentals=0
        ),
        compiler_params=LIMIT,
        name="distortion",
    )(on_chip(sub), codes_two, on_chip(mine), on_chip(theirs))


def swap(x, offset):
    return lax.ppermute(x, "cent", [(i, i ^ offset) for i in range(16)])


def step(emb_values, emb_scales, coarse_ids, centroids, codes_one, codes_two, codebook_init):
    _, width = emb_values.shape
    count = centroids.shape[0]
    sub_width = codebook_init.shape[2]
    peers = coarse_ids.shape[0]
    slots = 16

    q, row_squares, sent, cent_squares = prepare(emb_values, emb_scales, coarse_ids, centroids, slots)

    core = 1

    blocks = {0: q, 2: swap(q, 2), 6: swap(q, 6), 8: swap(q, 8)}
    blocks[core] = swap(q, core)

    fetched = lax.all_to_all(sent.reshape(peers, slots, width), "cent", 0, 0)
    fetched = fetched.reshape(peers * slots, width)

    blocks[14] = swap(blocks[8], 6)
    blocks[10] = swap(blocks[8], 2)
    blocks[4] = swap(blocks[6], 2)
    blocks[12] = swap(blocks[10], 6)
    for d in (2, 6, 8, 4, 10, 14, 12):
        blocks[d ^ core] = swap(blocks[d], core)

    orders = ((0, 1, 8, 9), (2, 3, 6, 7, 10, 11, 14, 15), (4, 12), (5, 13))
    lows, kept = [], None
    for k, order in enumerate(orders):
        low, kept = nearest([blocks[d] for d in order], cent_squares, centroids, kept, k == 1)
        lows.append(low)
    where = {d: (k, j) for k, order in enumerate(orders) for j, d in enumerate(order)}

    coded = residuals(coarse_ids, fetched, q, count, slots, sub_width)
    coded = lax.all_to_all(coded, "rows", 0, 0)

    mine, theirs, sub = statistics(coded, codes_one, codes_two, lows, where)
    mine = join(mine, swap(theirs, 1), 0)
    mine = join(mine, swap(mine, 8), 4)
    parts = [mine] + [swap(mine, d) for d in (2, 4, 6)]
    init = codebook_init[0].T
    books, coarse_gap = update(parts, init, row_squares)
    book_one, book_two, distortion = distortions(sub, codes_two, books, swap(books, 1))
    return coarse_gap[0], book_one.T[None], book_two.T[None], distortion


def solution(mesh):
    placed = (
        P(("cent", "rows"), None),
        P(("cent", "rows"), None),
        P(None, "rows"),
        P("cent", None),
        P("rows", "cent"),
        P("rows", "cent"),
        P("rows", None, None),
    )
    return jax.shard_map(
        step,
        mesh=mesh,
        in_specs=placed,
        out_specs=(
            P(("cent", "rows")),
            P("rows", None, None),
            P("rows", None, None),
            P("rows", "cent"),
        ),
        check_vma=False,
    )
```

```python
import functools

import jax
import jax.numpy as jnp
from jax import lax
from jax.experimental import pallas as pl
from jax.experimental.pallas import tpu as pltpu
from jax.sharding import PartitionSpec as P


bf16 = jnp.bfloat16
f32 = jnp.float32
prior_weight = 8.0
VM = pl.BlockSpec(memory_space=pltpu.VMEM)
HBM = pl.BlockSpec(memory_space=pltpu.HBM)
LIMIT = pltpu.CompilerParams(vmem_limit_bytes=16 << 20)


def off_chip(x):
    return pltpu.with_memory_space_constraint(x, pltpu.HBM)


def on_chip(x):
    return pltpu.with_memory_space_constraint(x, pltpu.VMEM)


STATS = 136
PAY = 144


def prepare_kernel(
    slots, step, values_hbm, scales_hbm, ids_hbm, cents_hbm, q_ref, squares_ref, out_ref, cent_squares_ref,
    values, scales_t, ids_ref, cents_ref, onehot_ref, total_ref, sems,
):
    count, width = cents_hbm.shape
    groups, rows = ids_ref.shape
    small = (
        pltpu.make_async_copy(ids_hbm, ids_ref, sems.at[0]),
        pltpu.make_async_copy(scales_hbm, scales_t, sems.at[1]),
        pltpu.make_async_copy(values_hbm, values, sems.at[2]),
    )
    large = [
        pltpu.make_async_copy(cents_hbm.at[pl.ds(step * j, step), :], cents_ref.at[j], sems.at[3 + j])
        for j in range(count // step)
    ]
    for copy in small:
        copy.start()
    for copy in large:
        copy.start()

    small[0].wait()
    local = ids_ref[...] - lax.axis_index("cent") * count
    mine = (local >= 0) & (local < count)
    before = lax.broadcasted_iota(jnp.int32, (rows, rows), 0) <= lax.broadcasted_iota(
        jnp.int32, (rows, rows), 1
    )
    rank = jnp.dot(
        mine.astype(f32).astype(bf16), before.astype(f32).astype(bf16), preferred_element_type=f32
    )
    slot = jnp.where(mine, rank - 1.0, -1.0)
    local = local.astype(f32)
    spread_slot = jnp.concatenate(
        [jnp.broadcast_to(slot[g : g + 1], (slots, rows)) for g in range(groups)], axis=0
    )
    spread_local = jnp.concatenate(
        [jnp.broadcast_to(local[g : g + 1], (slots, rows)) for g in range(groups)], axis=0
    )
    number = lax.rem(lax.broadcasted_iota(jnp.int32, (groups * slots, rows), 0), slots).astype(f32)
    chosen = jnp.sum(jnp.where(spread_slot == number, spread_local + 1.0, 0.0), axis=1, keepdims=True)
    chosen = chosen.astype(jnp.int32) - 1

    small[1].wait()
    small[2].wait()
    scales = scales_t[...].astype(f32).T
    squares = None
    for b in range(scales.shape[1]):
        lanes = slice(128 * b, 128 * b + 128)
        q = (values[:, lanes].astype(f32) * scales[:, b : b + 1]).astype(bf16)
        q_ref[:, lanes] = q
        wide = q.astype(f32)
        squares = wide * wide if squares is None else squares + wide * wide
    squares_ref[...] = jnp.sum(squares.T, axis=0, keepdims=True)

    for j in range(count // 256):
        at = lax.broadcasted_iota(jnp.int32, (groups * slots, 256), 1) + 256 * j
        onehot_ref[:, 256 * j : 256 * j + 256] = (at == chosen).astype(f32).astype(bf16)
    for j, copy in enumerate(large):
        copy.wait()
        part = jnp.dot(
            onehot_ref[:, step * j : step * j + step], cents_ref[j], preferred_element_type=f32
        )
        if j > 0:
            part = total_ref[...] + part
        if j + 1 < len(large):
            total_ref[...] = part
        else:
            out_ref[...] = part.astype(bf16)
        block = cents_ref[j]
        total = None
        for b in range(width // 128):
            wide = block[:, 128 * b : 128 * b + 128].astype(f32)
            total = wide * wide if total is None else total + wide * wide
        cent_squares_ref[step * j : step * j + step, :] = jnp.broadcast_to(
            jnp.sum(total, axis=1, keepdims=True), (step, 128)
        )


def prepare(values, scales, ids, cents, slots):
    rows, width = values.shape
    groups = ids.shape[0]
    count = cents.shape[0]
    scales = scales.T
    step = 512
    return pl.pallas_call(
        functools.partial(prepare_kernel, slots, step),
        out_shape=(
            pltpu.VMEM((rows, width), bf16),
            pltpu.VMEM((1, rows), f32),
            pltpu.VMEM((groups * slots, width), bf16),
            pltpu.VMEM((count, 128), f32),
        ),
        in_specs=[HBM] * 4,
        out_specs=(VM, VM, VM, VM),
        scratch_shapes=[
            pltpu.VMEM(values.shape, bf16),
            pltpu.VMEM(scales.shape, bf16),
            pltpu.VMEM(ids.shape, jnp.int32),
            pltpu.VMEM((count // step, step, width), bf16),
            pltpu.VMEM((groups * slots, count), bf16),
            pltpu.VMEM((groups * slots, width), f32),
            pltpu.SemaphoreType.DMA((count // step + 3,)),
        ],
        cost_estimate=pl.CostEstimate(
            flops=2 * groups * slots * count * width, bytes_accessed=count * width * 2, transcendentals=0
        ),
        compiler_params=LIMIT,
        name="prepare",
    )(off_chip(values), off_chip(scales), off_chip(ids), off_chip(cents))


def pack(out_ref, first, residual, sub_width):
    half = sub_width // 2
    for k in range(residual.shape[0] // sub_width):
        part = residual[sub_width * k : sub_width * (k + 1)]
        most = jnp.maximum(jnp.max(jnp.abs(part), axis=0, keepdims=True), 1e-30)
        power = jnp.floor(jnp.log2(most)) + 1.0
        coded = jnp.clip(jnp.round(part * jnp.exp2(15.0 - power)), -32767.0, 32767.0).astype(jnp.int32)
        word = lax.shift_left(coded[:half], 16) | (coded[half:] & 0xFFFF)
        out_ref[first + k, :half, :] = word
        out_ref[first + k, half:, :] = jnp.broadcast_to(power.astype(jnp.int32), (8, part.shape[1]))


def unpack(words):
    half = words.shape[0] - 8
    unit = jnp.exp2(words[half : half + 1].astype(f32) - 15.0)
    words = words[:half]
    high = lax.shift_right_arithmetic(words, 16)
    low = lax.shift_right_arithmetic(lax.shift_left(words, 16), 16)
    return jnp.concatenate([high, low], axis=0).astype(f32) * unit


def residual_kernel(count, slots, sub_width, ids_ref, fetched_ref, q_ref, out_ref):
    rows, width = q_ref.shape
    ids = ids_ref[pl.ds(lax.axis_index("cent"), 1), :]
    owner = lax.div(ids, count)
    across = jnp.broadcast_to(owner, (rows, rows))
    down = across.astype(f32).T.astype(jnp.int32)
    earlier = lax.broadcasted_iota(jnp.int32, (rows, rows), 0) < lax.broadcasted_iota(
        jnp.int32, (rows, rows), 1
    )
    rank = jnp.sum(jnp.where((across == down) & earlier, 1.0, 0.0), axis=0, keepdims=True)
    slot = owner * slots + rank.astype(jnp.int32)
    number = lax.broadcasted_iota(jnp.int32, (fetched_ref.shape[0], rows), 0)
    place = (number == slot).astype(f32).astype(bf16)
    for j in range(width // 128):
        lanes = slice(128 * j, 128 * j + 128)
        fetched = lax.dot_general(
            place, fetched_ref[:, lanes], (((0,), (0,)), ((), ())), preferred_element_type=f32
        )
        pack(out_ref, 2 * j, (q_ref[:, lanes].astype(f32) - fetched).T, sub_width)


def residuals(ids, fetched, q, count, slots, sub_width):
    rows, width = q.shape
    return pl.pallas_call(
        functools.partial(residual_kernel, count, slots, sub_width),
        out_shape=pltpu.VMEM((width // sub_width, sub_width // 2 + 8, rows), jnp.int32),
        in_specs=[VM] * 3,
        out_specs=VM,
        cost_estimate=pl.CostEstimate(
            flops=2 * fetched.size * rows, bytes_accessed=fetched.size * 2 + rows * width * 6, transcendentals=0
        ),
        compiler_params=LIMIT,
        name="residuals",
    )(ids, on_chip(fetched), on_chip(q))


def nearest_kernel(step, blocks, load, *refs):
    x_refs, refs = refs[:blocks], refs[blocks:]
    if load:
        squares_ref, cents_hbm, out_ref, cents_ref, sems = refs
    else:
        squares_ref, cents_ref, out_ref = refs
    half = step // 2
    parts = cents_ref.shape[0]
    copies = [
        pltpu.make_async_copy(cents_hbm.at[pl.ds(half * i, half), :], cents_ref.at[i], sems.at[i])
        for i in range(parts if load else 0)
    ]
    for copy in copies:
        copy.start()
    for first in range(0, blocks, 4):
        pairs = [(x_refs[j], x_refs[j + 1]) for j in range(first, min(first + 4, blocks), 2)]
        best = [None] * len(pairs)
        for i in range(0, parts, 2):
            for k in (i, i + 1) if load and first == 0 else ():
                copies[k].wait()
            block = jnp.concatenate([cents_ref[i], cents_ref[i + 1]], axis=0)
            squares = squares_ref[half * i : half * i + step, :]
            squares = jnp.concatenate([squares, squares], axis=1)
            for j, pair in enumerate(pairs):
                x = jnp.concatenate([ref[...] for ref in pair], axis=0)
                cross = lax.dot_general(block, x, (((1,), (1,)), ((), ())), preferred_element_type=f32)
                low = jnp.min(squares - 2.0 * cross, axis=0, keepdims=True)
                best[j] = low if best[j] is None else jnp.minimum(best[j], low)
        for j, low in enumerate(best):
            for k in range(2):
                row = first + 2 * j + k
                out_ref[row : row + 1, :] = low[:, 128 * k : 128 * k + 128]


def nearest(xs, squares, cents, kept, keep):
    count, width = cents.shape
    rows = sum(x.shape[0] for x in xs)
    step = 512
    load = kept is None
    held = pltpu.VMEM((2 * count // step, step // 2, width), bf16)
    sems = pltpu.SemaphoreType.DMA((2 * count // step,))
    outs = [pltpu.VMEM((rows // 128, 128), f32)] + [held] * keep
    result = pl.pallas_call(
        functools.partial(nearest_kernel, step, len(xs), load),
        out_shape=tuple(outs),
        in_specs=[VM] * (len(xs) + 1) + [HBM if load else VM],
        out_specs=tuple([VM] * len(outs)),
        scratch_shapes=([] if keep else [held]) * load + [sems] * load,
        cost_estimate=pl.CostEstimate(
            flops=2 * rows * count * width, bytes_accessed=count * width * 2 + rows * width * 2, transcendentals=0
        ),
        compiler_params=LIMIT,
        name="nearest",
    )(*[on_chip(x) for x in xs], on_chip(squares), off_chip(cents) if load else on_chip(kept))
    return result[0], result[1] if keep else kept


def halves_of(x):
    high = x.astype(bf16)
    return high, (x - high.astype(f32)).astype(bf16)


def statistics_kernel(where, coded_ref, one_ref, two_ref, *refs):
    gap_refs, (mine_ref, theirs_ref, sub_out_ref) = refs[:-3], refs[-3:]
    groups, width, rows = sub_out_ref.shape
    words = 256
    high, low = [], []
    for g in range(groups):
        sub = unpack(coded_ref[g])
        sub_out_ref[g] = sub
        h, l = halves_of(sub)
        high.append(h)
        low.append(l)
    ones = jnp.ones((16, groups * rows), bf16)
    left = jnp.concatenate([jnp.concatenate(high, axis=1), jnp.concatenate(low, axis=1), ones], axis=0)
    word = lax.broadcasted_iota(jnp.int32, (words, groups * rows), 0)
    core = lax.rem(lax.axis_index("cent"), 2)
    odd = core == 1

    def totals(codes_ref):
        hit = (word == codes_ref[...]).astype(f32).astype(bf16)
        out = lax.dot_general(left, hit, (((1,), (1,)), ((), ())), preferred_element_type=f32)
        return out[:width] + out[width : 2 * width], out[2 * width : 2 * width + 8]

    for at, codes_ref in enumerate((one_ref, two_ref)):
        total, count = totals(codes_ref)
        rows_at = slice(width * at, width * at + width)
        a, b = total[:, :128], total[:, 128:]
        mine_ref[rows_at, :] = jnp.where(odd, b, a)
        theirs_ref[rows_at, :] = jnp.where(odd, a, b)
        a, b = count[:4, :128], count[:4, 128:]
        count_at = slice(2 * width + 4 * at, 2 * width + 4 * at + 4)
        mine_ref[count_at, :] = jnp.where(odd, b, a)
        theirs_ref[count_at, :] = jnp.where(odd, a, b)
    for j in range(8):
        for out_ref, d in ((mine_ref, 2 * j), (theirs_ref, 2 * j + 1)):
            k, row = where[d]
            out_ref[STATS + j : STATS + j + 1, :] = gap_refs[k][row : row + 1, :]


def statistics(coded, codes_one, codes_two, lows, where):
    groups, words, rows = coded.shape
    sub = jax.ShapeDtypeStruct((groups, 2 * (words - 8), rows), f32)
    shape = pltpu.VMEM((PAY, 128), f32)
    return pl.pallas_call(
        functools.partial(statistics_kernel, where),
        out_shape=(shape, shape, pltpu.VMEM(sub.shape, f32)),
        in_specs=[VM] * (3 + len(lows)),
        out_specs=(VM, VM, VM),
        cost_estimate=pl.CostEstimate(
            flops=2 * 2 * sub.size * 512, bytes_accessed=sub.size * 4, transcendentals=0
        ),
        compiler_params=LIMIT,
        name="statistics",
    )(on_chip(coded), codes_one, codes_two, *[on_chip(x) for x in lows])


def join_kernel(shift, a_ref, b_ref, out_ref):
    out_ref[:STATS, :] = a_ref[:STATS, :] + b_ref[:STATS, :]
    keep = PAY - STATS - shift
    out_ref[STATS:PAY, :] = a_ref[STATS:PAY, :]
    out_ref[STATS : STATS + keep, :] = jnp.minimum(
        a_ref[STATS : STATS + keep, :], b_ref[STATS + shift : PAY, :]
    )


def join(a, b, shift):
    return pl.pallas_call(
        functools.partial(join_kernel, shift),
        out_shape=pltpu.VMEM(a.shape, f32),
        in_specs=[VM, VM],
        out_specs=VM,
        cost_estimate=pl.CostEstimate(flops=a.size, bytes_accessed=a.size * 12, transcendentals=0),
        compiler_params=LIMIT,
        name="join",
    )(on_chip(a), on_chip(b))


def update_kernel(width, a_ref, b_ref, c_ref, d_ref, init_ref, squares_ref, books_ref, gap_ref):
    core = lax.rem(lax.axis_index("cent"), 2)
    total = (a_ref[:STATS, :] + b_ref[:STATS, :]) + (c_ref[:STATS, :] + d_ref[:STATS, :])
    init = jnp.where(core == 1, init_ref[:, 128:], init_ref[:, :128])
    count_one = total[2 * width : 2 * width + 1]
    count_two = total[2 * width + 4 : 2 * width + 5]
    one = (total[:width] + prior_weight * init) / (count_one + prior_weight)
    two = (total[width : 2 * width] + prior_weight * one) / (count_two + prior_weight)
    books_ref[:width, :] = one
    books_ref[width:, :] = two
    low = jnp.minimum(
        jnp.minimum(a_ref[STATS : STATS + 1, :], b_ref[STATS + 1 : STATS + 2, :]),
        jnp.minimum(c_ref[STATS + 2 : STATS + 3, :], d_ref[STATS + 3 : STATS + 4, :]),
    )
    gap_ref[...] = (low + squares_ref[...]) * (1.0 / 1024.0)


def update(parts, init, squares):
    width = init.shape[0]
    return pl.pallas_call(
        functools.partial(update_kernel, width),
        out_shape=(
            pltpu.VMEM((2 * width, 128), f32),
            jax.ShapeDtypeStruct((1, 128), f32),
        ),
        in_specs=[VM] * 6,
        out_specs=(VM, VM),
        cost_estimate=pl.CostEstimate(flops=8 * STATS * 128, bytes_accessed=5 * PAY * 512, transcendentals=0),
        compiler_params=LIMIT,
        name="update",
    )(*[on_chip(x) for x in parts], init, on_chip(squares))


def distortion_kernel(sub_ref, two_ref, mine_ref, theirs_ref, one_out_ref, two_out_ref, out_ref):
    groups, width, rows = sub_ref.shape
    odd = lax.rem(lax.axis_index("cent"), 2) == 1
    mine, theirs = mine_ref[...], theirs_ref[...]
    books = jnp.concatenate([jnp.where(odd, theirs, mine), jnp.where(odd, mine, theirs)], axis=1)
    one_out_ref[...] = books[:width]
    book = books[width:]
    two_out_ref[...] = book
    high, low = halves_of(book)
    left = jnp.concatenate([high, low], axis=0)
    words = book.shape[1]
    for g in range(0, groups, 2):
        lanes = slice(rows * g, rows * g + 2 * rows)
        word = lax.broadcasted_iota(jnp.int32, (words, 2 * rows), 0)
        hit = (word == two_ref[:, lanes]).astype(f32).astype(bf16)
        rebuilt = jnp.dot(left, hit, preferred_element_type=f32)
        rebuilt = rebuilt[:width] + rebuilt[width:]
        sub = jnp.concatenate([sub_ref[g], sub_ref[g + 1]], axis=1)
        miss = sub - rebuilt
        out_ref[:, lanes] = jnp.sum(miss * miss, axis=0, keepdims=True) * (1.0 / width)


def distortions(sub, codes_two, mine, theirs):
    groups, width, rows = sub.shape
    return pl.pallas_call(
        distortion_kernel,
        out_shape=(
            jax.ShapeDtypeStruct((width, 256), f32),
            jax.ShapeDtypeStruct((width, 256), f32),
            jax.ShapeDtypeStruct((1, groups * rows), f32),
        ),
        in_specs=[VM] * 4,
        out_specs=(VM, VM, VM),
        cost_estimate=pl.CostEstimate(
            flops=4 * sub.size * 256, bytes_accessed=sub.size * 4, transcendentals=0
        ),
        compiler_params=LIMIT,
        name="distortion",
    )(on_chip(sub), codes_two, on_chip(mine), on_chip(theirs))


def swap(x, offset):
    return lax.ppermute(x, "cent", [(i, i ^ offset) for i in range(16)])


def step(emb_values, emb_scales, coarse_ids, centroids, codes_one, codes_two, codebook_init):
    _, width = emb_values.shape
    count = centroids.shape[0]
    sub_width = codebook_init.shape[2]
    peers = coarse_ids.shape[0]
    slots = 16

    q, row_squares, sent, cent_squares = prepare(emb_values, emb_scales, coarse_ids, centroids, slots)

    core = 1

    blocks = {0: q, 2: swap(q, 2), 6: swap(q, 6), 8: swap(q, 8)}
    blocks[core] = swap(q, core)

    fetched = lax.all_to_all(sent.reshape(peers, slots, width), "cent", 0, 0)
    fetched = fetched.reshape(peers * slots, width)

    blocks[14] = swap(blocks[8], 6)
    blocks[10] = swap(blocks[8], 2)
    blocks[4] = swap(blocks[6], 2)
    blocks[12] = swap(blocks[10], 6)
    for d in (2, 6, 8, 4, 10, 14, 12):
        blocks[d ^ core] = swap(blocks[d], core)

    orders = ((0, 1, 8, 9), (2, 3, 6, 7, 10, 11, 14, 15), (4, 12), (5, 13))
    lows, kept = [], None
    for k, order in enumerate(orders):
        low, kept = nearest([blocks[d] for d in order], cent_squares, centroids, kept, k == 1)
        lows.append(low)
    where = {d: (k, j) for k, order in enumerate(orders) for j, d in enumerate(order)}

    coded = residuals(coarse_ids, fetched, q, count, slots, sub_width)
    coded = lax.all_to_all(coded, "rows", 0, 0)

    mine, theirs, sub = statistics(coded, codes_one, codes_two, lows, where)
    mine = join(mine, swap(theirs, 1), 0)
    mine = join(mine, swap(mine, 8), 4)
    parts = [mine] + [swap(mine, d) for d in (2, 4, 6)]
    init = codebook_init[0].T
    books, coarse_gap = update(parts, init, row_squares)
    book_one, book_two, distortion = distortions(sub, codes_two, books, swap(books, 1))
    return coarse_gap[0], book_one.T[None], book_two.T[None], distortion


def solution(mesh):
    placed = (
        P(("cent", "rows"), None),
        P(("cent", "rows"), None),
        P(None, "rows"),
        P("cent", None),
        P("rows", "cent"),
        P("rows", "cent"),
        P("rows", None, None),
    )
    return jax.shard_map(
        step,
        mesh=mesh,
        in_specs=placed,
        out_specs=(
            P(("cent", "rows")),
            P("rows", None, None),
            P("rows", None, None),
            P("rows", "cent"),
        ),
        check_vma=False,
    )
```
